32 devices in a mesh: rows: 8 (over y, x, core), cols: 4 (over z).
Axes of the slice: x: 2, y: 2, z: 4, core: 2. Of those that a mesh axis runs over, the one named last changes fastest.
Arguments:
- images: float32 [4, 56, 28, 512], P(None, 'rows', 'cols')
- cotangent: float32 [4, 56, 28, 512], P(None, 'rows', 'cols'), may hold values from -6 to 6
- rel_index: int32 [49, 49], replicated, may hold values from 0 to 168, as said below
- rel_table: float32 [169, 16], replicated
- qkv_weight: bfloat16 [512, 1536], P(('rows', 'cols')), may hold values from -0.25 to 0.25
- proj_weight: bfloat16 [512, 512], P(('rows', 'cols')), may hold values from -1 to 1
- up_weight: bfloat16 [512, 2048], P(('rows', 'cols')), may hold values from -0.25 to 0.25
- down_weight: bfloat16 [2048, 512], P(('rows', 'cols')), may hold values from -0.125 to 0.125
- norm1_gain: bfloat16 [512], P(('rows', 'cols')), may hold values from 0.5 to 1.5
- norm1_bias: bfloat16 [512], P(('rows', 'cols')), may hold values from -3 to 3
- query_bias: bfloat16 [512], P(('rows', 'cols')), may hold values from -3 to 3
- value_bias: bfloat16 [512], P(('rows', 'cols')), may hold values from -3 to 3
- proj_bias: bfloat16 [512], P(('rows', 'cols')), may hold values from -3 to 3
- norm2_gain: bfloat16 [512], P(('rows', 'cols')), may hold values from 0.5 to 1.5
- norm2_bias: bfloat16 [512], P(('rows', 'cols')), may hold values from -3 to 3
- up_bias: bfloat16 [2048], P(('rows', 'cols')), may hold values from -3 to 3
- down_bias: bfloat16 [512], P(('rows', 'cols')), may hold values from -3 to 3
Outputs:
- block_out: float32 [4, 56, 28, 512], P(None, 'rows', 'cols')
- grad_images: float32 [4, 56, 28, 512], P(None, 'rows', 'cols')
- grad_qkv_weight: float32 [512, 1536], P(('rows', 'cols'))
- grad_proj_weight: float32 [512, 512], P(('rows', 'cols'))
- grad_up_weight: float32 [512, 2048], P(('rows', 'cols'))
- grad_down_weight: float32 [2048, 512], P(('rows', 'cols'))
- grad_norm1_gain: float32 [512], P(('rows', 'cols'))
- grad_norm1_bias: float32 [512], P(('rows', 'cols'))
- grad_query_bias: float32 [512], P(('rows', 'cols'))
- grad_value_bias: float32 [512], P(('rows', 'cols'))
- grad_proj_bias: float32 [512], P(('rows', 'cols'))
- grad_norm2_gain: float32 [512], P(('rows', 'cols'))
- grad_norm2_bias: float32 [512], P(('rows', 'cols'))
- grad_up_bias: float32 [2048], P(('rows', 'cols'))
- grad_down_bias: float32 [512], P(('rows', 'cols'))
- grad_rel_table: float32 [169, 16], replicated
The draws below stay inside these ranges and needn't reach their ends.
Inputs may be any that keep to these rules, and one draw needn't show every extreme that they name: `rel_index`: every value from 0 to 168 appears.
All inputs are finite; a program needn't handle non-finite values.
Results may differ from the reference program's by a relative error of at most 0.012.
Values may be sent and summed in bfloat16 or wider, within the bound.
A program may use at most 128 MiB of HBM per device.

```python
import math
import jax
import jax.numpy as jnp
from jax import lax

D = 512
FF = 2048
HEADS = 16
WIN = 7
IMAGES = 4
SHIFT = 3
REL = 169
NH = 56
NW = 28
N_ROWS = 8
N_COLS = 4


def draw_images(key, part):
    key_vals, key_cols, key_rows = jax.random.split(key, 3)
    shape = (IMAGES, NH, NW, D)
    col_scale = jnp.exp(jax.random.uniform(key_cols, (D,), minval=math.log(0.3), maxval=math.log(3.0)))
    row_scale = jnp.exp(jax.random.uniform(key_rows, (IMAGES, NH, NW, 1), minval=math.log(0.3), maxval=math.log(3.0)))
    values = jax.random.normal(key_vals, shape) * col_scale * row_scale
    return values.astype(jnp.float32)


def draw_rel_index(key, part):
    key_fill, key_head, key_order = jax.random.split(jax.random.fold_in(key, 11), 3)
    window = WIN * WIN
    filler = jax.random.randint(key_fill, (window * window - REL,), 0, REL).astype(jnp.int32)
    leading = jax.random.permutation(key_head, REL).astype(jnp.int32)
    joined = jnp.concatenate([leading, filler])
    order = jax.random.permutation(key_order, window * window)
    return joined[order].reshape(window, window).astype(jnp.int32)


def draw_rel_table(key, part):
    key_base = jax.random.fold_in(jax.random.fold_in(key, 23), 0)
    values = jax.random.normal(key_base, (REL, HEADS))
    return values.astype(jnp.float32)


def steps_of(key, shape, pieces, smallest, top_value):
    loudness = 1.0
    for dim, blocks in pieces:
        steps = jax.random.uniform(jax.random.fold_in(jax.random.fold_in(key, 6), dim), (blocks,), jnp.float32, smallest / len(pieces), top_value / len(pieces))
        loudness = loudness * jnp.repeat(jnp.exp(steps), shape[dim] // blocks).reshape((-1,) + (1,) * (len(shape) - 1 - dim))
    return loudness


def bell_draw(own_key, extent, deviation, bound, pieces=(), held_as=jnp.bfloat16):
    values = jax.random.normal(own_key, extent, jnp.float32) * deviation
    if len(pieces) > 0:
        values = steps_of(own_key, extent, pieces, -0.22, 0.18) * values
    return jnp.clip(values, min=-bound, max=bound).astype(held_as)


def setup_inputs(seed: int = 0) -> dict:
    key_of = jax.random.split(jax.random.key(seed), 18)
    return {
        "images": draw_images(jax.random.fold_in(key_of[17], 71), 0),
        "cotangent": bell_draw(key_of[1], (IMAGES, NH, NW, D), 1.0, 6.0, ((1, 8), (2, 4)), jnp.float32),
        "rel_index": draw_rel_index(jax.random.fold_in(key_of[17], 71), 0),
        "rel_table": draw_rel_table(jax.random.fold_in(key_of[17], 71), 0),
        "qkv_weight": bell_draw(key_of[4], (D, 3 * D), D ** -0.5, 0.25, ((0, 32),)),
        "proj_weight": bell_draw(key_of[5], (D, D), (D // 16) ** -0.5, 1.0, ((0, 32),)),
        "up_weight": bell_draw(key_of[6], (D, FF), D ** -0.5, 0.25, ((0, 32),)),
        "down_weight": bell_draw(key_of[7], (FF, D), FF ** -0.5, 0.125, ((0, 32),)),
        "norm1_gain": jnp.clip(1.0 + 0.1 * jax.random.normal(key_of[8], (D,), jnp.float32), 0.5, 1.5).astype(jnp.bfloat16),
        "norm1_bias": bell_draw(key_of[9], (D,), 0.5, 3.0, ((0, 32),)),
        "query_bias": bell_draw(key_of[10], (D,), 0.5, 3.0, ((0, 32),)),
        "value_bias": bell_draw(key_of[11], (D,), 0.5, 3.0, ((0, 32),)),
        "proj_bias": bell_draw(key_of[12], (D,), 0.5, 3.0, ((0, 32),)),
        "norm2_gain": jnp.clip(1.0 + 0.1 * jax.random.normal(key_of[13], (D,), jnp.float32), 0.5, 1.5).astype(jnp.bfloat16),
        "norm2_bias": bell_draw(key_of[14], (D,), 0.5, 3.0, ((0, 32),)),
        "up_bias": bell_draw(key_of[15], (FF,), 0.5, 3.0, ((0, 32),)),
        "down_bias": bell_draw(key_of[16], (D,), 0.5, 3.0, ((0, 32),)),
    }


norm_eps = 1e-05
root_half = 0.7071067811865476
tau_factor = 0.3989422804014327
big_negative = -1e+30

def layer_norm(values, gain_vec, offset):
    mean_val = lax.optimization_barrier(jnp.mean(values, axis=-1, keepdims=True))
    centred = values - mean_val
    inv_std = lax.rsqrt(lax.optimization_barrier(jnp.mean(centred * centred, axis=-1, keepdims=True)) + norm_eps)
    normed = centred * inv_std
    return (normed * gain_vec + offset, normed, inv_std)

def norm_back(grad_out, normed, inv_std, gain_vec):
    scaled = grad_out * gain_vec
    row_inner = scaled - lax.optimization_barrier(jnp.mean(scaled, axis=-1, keepdims=True)) - normed * lax.optimization_barrier(jnp.mean(scaled * normed, axis=-1, keepdims=True))
    return (inv_std * row_inner, lax.optimization_barrier(jnp.sum(grad_out * normed, axis=0)), lax.optimization_barrier(jnp.sum(grad_out, axis=0)))

def dot_plain(former, latter):
    return jnp.dot(former, latter, preferred_element_type=jnp.float32)

def dot_lead(former, latter):
    return lax.dot_general(former, latter, (((0,), (0,)), ((), ())), preferred_element_type=jnp.float32)

def dot_tail(former, latter):
    return lax.dot_general(former, latter, (((1,), (1,)), ((), ())), preferred_element_type=jnp.float32)

def band_of(positions, length):
    return (positions >= length - WIN).astype(jnp.int32) + (positions >= length - SHIFT).astype(jnp.int32)

def window_pass(tokens, grad_rows, allowed, bias_heads, params):
    qkv_weight, proj_weight, up_weight, down_weight, norm1_gain, norm1_bias, query_bias, value_bias, proj_bias, norm2_gain, norm2_bias, up_bias, down_bias = params
    row_total, features = tokens.shape
    window = allowed.shape[-1]
    image_windows = row_total // window
    head_count = bias_heads.shape[0]
    head_width = features // head_count
    score_scale = head_width ** (-0.5)
    highest = lax.Precision.HIGHEST

    def split_heads(values):
        return values.astype(jnp.float32).reshape(image_windows, window, head_count, head_width)

    def scores_of(query_b, key_b):
        raw_scores = jnp.einsum('wqhd,wkhd->whqk', split_heads(query_b), split_heads(key_b), precision=highest)
        return jnp.where(allowed, raw_scores + bias_heads[None], big_negative)
    gain_one = norm1_gain.astype(jnp.float32)
    gain_two = norm2_gain.astype(jnp.float32)
    out_one, normed_one, inv_one = layer_norm(tokens, gain_one, norm1_bias.astype(jnp.float32))
    h_one = out_one.astype(jnp.bfloat16)
    projected = dot_plain(h_one, qkv_weight)
    query_b = ((projected[:, :features] + query_bias.astype(jnp.float32)) * score_scale).astype(jnp.bfloat16)
    key_b = projected[:, features:2 * features].astype(jnp.bfloat16)
    value_b = (projected[:, 2 * features:] + value_bias.astype(jnp.float32)).astype(jnp.bfloat16)
    scores = scores_of(query_b, key_b)
    row_top = lax.optimization_barrier(jnp.max(scores, axis=-1, keepdims=True))
    log_total = row_top + jnp.log(lax.optimization_barrier(jnp.sum(jnp.exp(scores - row_top), axis=-1, keepdims=True)))
    attend_b = jnp.exp(scores - log_total).astype(jnp.bfloat16)
    attn_b = jnp.einsum('whqk,wkhd->wqhd', attend_b.astype(jnp.float32), split_heads(value_b), precision=highest).reshape(row_total, features).astype(jnp.bfloat16)
    residual = tokens + dot_plain(attn_b, proj_weight) + proj_bias.astype(jnp.float32)
    out_two, normed_two, inv_two = layer_norm(residual, gain_two, norm2_bias.astype(jnp.float32))
    h_two = out_two.astype(jnp.bfloat16)
    hidden_pre = dot_plain(h_two, up_weight) + up_bias.astype(jnp.float32)
    gauss_cdf = 0.5 * (1.0 + lax.erf(hidden_pre * root_half))
    act_b = (hidden_pre * gauss_cdf).astype(jnp.bfloat16)
    result = residual + dot_plain(act_b, down_weight) + down_bias.astype(jnp.float32)
    grad_b = grad_rows.astype(jnp.bfloat16)
    grad_down = dot_lead(act_b, grad_b)
    grad_down_add = lax.optimization_barrier(jnp.sum(grad_rows, axis=0))
    grad_act = dot_tail(grad_b, down_weight)
    density = jnp.exp(-0.5 * hidden_pre * hidden_pre) * tau_factor
    grad_pre = grad_act * (gauss_cdf + hidden_pre * density)
    grad_pre_b = grad_pre.astype(jnp.bfloat16)
    grad_up = dot_lead(h_two, grad_pre_b)
    grad_up_add = lax.optimization_barrier(jnp.sum(grad_pre, axis=0))
    grad_h_two = dot_tail(grad_pre_b, up_weight)
    grad_resid, grad_gain_two, grad_bias_two = norm_back(grad_h_two, normed_two, inv_two, gain_two)
    grad_resid = grad_resid + grad_rows
    grad_resid_b = grad_resid.astype(jnp.bfloat16)
    grad_proj = dot_lead(attn_b, grad_resid_b)
    grad_proj_add = lax.optimization_barrier(jnp.sum(grad_resid, axis=0))
    grad_attn_b = dot_tail(grad_resid_b, proj_weight).astype(jnp.bfloat16)
    grad_heads = split_heads(grad_attn_b)
    grad_attend = jnp.einsum('wqhd,wkhd->whqk', grad_heads, split_heads(value_b), precision=highest)
    attend = jnp.exp(scores_of(query_b, key_b) - log_total)
    grad_value = jnp.einsum('whqk,wqhd->wkhd', attend.astype(jnp.bfloat16).astype(jnp.float32), grad_heads, precision=highest).reshape(row_total, features)
    row_inner = lax.optimization_barrier(jnp.sum(attend * grad_attend, axis=-1, keepdims=True))
    grad_scores = attend * (grad_attend - row_inner)
    grad_bias_heads = lax.optimization_barrier(jnp.sum(grad_scores, axis=0)).reshape(head_count, window * window)
    grad_scores_b = grad_scores.astype(jnp.bfloat16)
    grad_query = (jnp.einsum('whqk,wkhd->wqhd', grad_scores_b.astype(jnp.float32), split_heads(key_b), precision=highest) * score_scale).reshape(row_total, features)
    grad_key = jnp.einsum('whqk,wqhd->wkhd', grad_scores_b.astype(jnp.float32), split_heads(query_b), precision=highest).reshape(row_total, features)
    grad_query_add = lax.optimization_barrier(jnp.sum(grad_query, axis=0))
    grad_value_add = lax.optimization_barrier(jnp.sum(grad_value, axis=0))
    grad_mixed_b = jnp.concatenate([grad_query, grad_key, grad_value], axis=1).astype(jnp.bfloat16)
    grad_qkv = dot_lead(h_one, grad_mixed_b)
    grad_h_one = dot_tail(grad_mixed_b, qkv_weight)
    grad_in, grad_gain_one, grad_bias_one = norm_back(grad_h_one, normed_one, inv_one, gain_one)
    grad_tokens = grad_resid + grad_in
    grads = (grad_qkv, grad_proj, grad_up, grad_down, grad_gain_one, grad_bias_one, grad_query_add, grad_value_add, grad_proj_add, grad_gain_two, grad_bias_two, grad_up_add, grad_down_add)
    return (result, grad_tokens, grads, grad_bias_heads)

def to_windows(grid_vals):
    channels = grid_vals.shape[-1]
    return grid_vals.reshape(N_ROWS, WIN, N_COLS, WIN, channels).transpose(0, 2, 1, 3, 4).reshape(N_ROWS * N_COLS, WIN * WIN, channels)

def from_windows(windows):
    channels = windows.shape[-1]
    return windows.reshape(N_ROWS, N_COLS, WIN, WIN, channels).transpose(0, 2, 1, 3, 4).reshape(NH, NW, channels)

def reference(images, cotangent, rel_index, rel_table, qkv_weight, proj_weight, up_weight, down_weight, norm1_gain, norm1_bias, query_bias, value_bias, proj_bias, norm2_gain, norm2_bias, up_bias, down_bias):
    params = (qkv_weight, proj_weight, up_weight, down_weight, norm1_gain, norm1_bias, query_bias, value_bias, proj_bias, norm2_gain, norm2_bias, up_bias, down_bias)
    window = WIN * WIN
    onehot = (rel_index.reshape(window * window).astype(jnp.int32)[:, None] == jnp.arange(REL, dtype=jnp.int32)[None, :]).astype(jnp.float32)
    bias_flat = jnp.dot(onehot, rel_table, precision=lax.Precision.HIGHEST, preferred_element_type=jnp.float32)
    bias_heads = bias_flat.T.reshape(HEADS, window, window)
    band_rows = band_of(jnp.arange(NH, dtype=jnp.int32), NH)
    band_cols = band_of(jnp.arange(NW, dtype=jnp.int32), NW)
    region_grid = 3 * band_rows[:, None] + band_cols[None, :]
    region_win = to_windows(region_grid[:, :, None])[:, :, 0]
    allowed = (region_win[:, :, None] == region_win[:, None, :])[:, None]

    def per_image(totals, image_pair):
        image, grad_image = image_pair
        rolled = jnp.roll(image, (-SHIFT, -SHIFT), axis=(0, 1))
        rolled_grad = jnp.roll(grad_image, (-SHIFT, -SHIFT), axis=(0, 1))
        tokens = to_windows(rolled).reshape(-1, D)
        grad_rows = to_windows(rolled_grad).reshape(-1, D)
        result, grad_tokens, grads, grad_bias = window_pass(tokens, grad_rows, allowed, bias_heads, params)
        totals = jax.tree.map(jnp.add, totals, grads + (grad_bias,))
        out_image = jnp.roll(from_windows(result.reshape(-1, window, D)), (SHIFT, SHIFT), axis=(0, 1))
        grad_out_image = jnp.roll(from_windows(grad_tokens.reshape(-1, window, D)), (SHIFT, SHIFT), axis=(0, 1))
        return (totals, (out_image, grad_out_image))
    zeros_init = tuple((jnp.zeros(p.shape, jnp.float32) for p in params)) + (jnp.zeros((HEADS, window * window), jnp.float32),)
    totals_end, (block_out, grad_images) = lax.scan(per_image, zeros_init, (images, cotangent))
    grad_rel_table = lax.dot_general(onehot, totals_end[13], (((0,), (1,)), ((), ())), precision=lax.Precision.HIGHEST, preferred_element_type=jnp.float32)
    return (block_out, grad_images, totals_end[0], totals_end[1], totals_end[2], totals_end[3], totals_end[4], totals_end[5], totals_end[6], totals_end[7], totals_end[8], totals_end[9], totals_end[10], totals_end[11], totals_end[12], grad_rel_table)
```

```python
import functools

import jax
import jax.numpy as jnp
from jax import lax
from jax.experimental import pallas as pl
from jax.experimental.pallas import tpu as pltpu
from jax.sharding import PartitionSpec as P

WIN = 7
SHIFT = 3


norm_eps = 1e-05
root_half = 0.7071067811865476
tau_factor = 0.3989422804014327
big_negative = -1e30


def shifted(array, axis, by):
    length = lax.axis_size(axis)
    return lax.ppermute(array, axis, [(i, (i + by) % length) for i in range(length)])


def as_sent(array):

    def short(part):
        return part.astype(jnp.bfloat16) if part.dtype == jnp.float32 else part

    return jax.tree.map(short, array)


def layer_norm(values, gain_vec, offset):
    mean_val = jnp.mean(values, axis=-1, keepdims=True)
    centred = values - mean_val
    inv_std = lax.rsqrt(jnp.mean(centred * centred, axis=-1, keepdims=True) + norm_eps)
    normed = centred * inv_std
    return (normed * gain_vec + offset, normed, inv_std)


def norm_back(grad_out, normed, inv_std, gain_vec):
    scaled = grad_out * gain_vec
    row_inner = (
        scaled
        - jnp.mean(scaled, axis=-1, keepdims=True)
        - normed * jnp.mean(scaled * normed, axis=-1, keepdims=True)
    )
    return (inv_std * row_inner, jnp.sum(grad_out * normed, axis=0), jnp.sum(grad_out, axis=0))


def dot_plain(former, latter):
    return jnp.dot(former, latter, preferred_element_type=jnp.float32)


def dot_lead(former, latter):
    return lax.dot_general(
        former, latter, (((0,), (0,)), ((), ())), preferred_element_type=jnp.float32
    )


def dot_tail(former, latter):
    return lax.dot_general(
        former, latter, (((1,), (1,)), ((), ())), preferred_element_type=jnp.float32
    )


def band_of(positions, length):
    return (positions >= length - WIN).astype(jnp.int32) + (positions >= length - SHIFT).astype(
        jnp.int32
    )


def roll_in(images, cotangent):
    from_below = shifted((images[:, :SHIFT], cotangent[:, :SHIFT]), "rows", -1)
    tall_tokens = jnp.concatenate([images[:, SHIFT:], from_below[0]], axis=1)
    tall_grads = jnp.concatenate([cotangent[:, SHIFT:], from_below[1]], axis=1)
    beside = shifted((tall_tokens[:, :, :SHIFT], tall_grads[:, :, :SHIFT]), "cols", -1)
    return (
        jnp.concatenate([tall_tokens[:, :, SHIFT:], beside[0]], axis=2),
        jnp.concatenate([tall_grads[:, :, SHIFT:], beside[1]], axis=2),
    )


def roll_out(result, grad_tokens):
    from_above = (
        shifted(result[:, -SHIFT:].astype(jnp.bfloat16), "rows", 1).astype(jnp.float32),
        shifted(grad_tokens[:, -SHIFT:].astype(jnp.bfloat16), "rows", 1).astype(jnp.float32),
    )
    tall_result = jnp.concatenate([from_above[0], result[:, :-SHIFT]], axis=1)
    tall_grads = jnp.concatenate([from_above[1], grad_tokens[:, :-SHIFT]], axis=1)
    beside = (
        shifted(tall_result[:, :, -SHIFT:].astype(jnp.bfloat16), "cols", 1).astype(jnp.float32),
        shifted(as_sent(tall_grads[:, :, -SHIFT:]), "cols", 1),
    )
    return (
        jnp.concatenate([beside[0], tall_result[:, :, :-SHIFT]], axis=2),
        jnp.concatenate([beside[1], tall_grads[:, :, :-SHIFT]], axis=2),
    )


MESH = pl.DeviceIdType.MESH
CORES = 2


def grid_of(rows):
    chips = rows // CORES
    across = 1
    for size in range(1, chips + 1):
        if chips % size == 0 and size * size <= chips:
            across = size
    return chips // across, across


def whereabouts(dims):
    height, width = dims[0], dims[1]
    row, depth_at = lax.axis_index("rows"), lax.axis_index("cols")
    core = lax.rem(row, CORES)
    chip = row // CORES
    return chip // width, lax.rem(chip, width), core, depth_at


def device_at(dims, y, x, core, z):
    return ((y * dims[1] + x) * CORES + core, z)


def greet(dims, here):
    barrier = pltpu.get_barrier_semaphore()
    total = 0
    for axis in range(4):
        for step in range(1, dims[axis]):
            there = list(here)
            there[axis] = lax.rem(here[axis] + step, dims[axis])
            pl.semaphore_signal(
                barrier, inc=1, device_id=device_at(dims, *there), device_id_type=MESH
            )
            total += 1
    pl.semaphore_wait(barrier, total)


def moved(here, axis, step, dims):
    there = list(here)
    there[axis] = lax.rem(here[axis] + step, dims[axis])
    return there


def gather_kernel(dims, count, *refs):
    ins, outs = refs[:count], refs[count : 2 * count]
    local_sem, send_sem, recv_sem = refs[2 * count :]
    height, width, _, depth = dims
    here = whereabouts(dims)
    y, x, core, z = here
    greet(dims, here)
    used = [0] * count

    def send(stream, src, dst, there):
        slot = used[stream]
        used[stream] += 1
        copy = pltpu.make_async_remote_copy(
            src_ref=src,
            dst_ref=dst,
            send_sem=send_sem.at[stream, slot],
            recv_sem=recv_sem.at[stream, slot],
            device_id=device_at(dims, *there),
            device_id_type=MESH,
        )
        copy.start()
        return copy

    started = []
    along_z, locals_ = [], []
    for k in range(count):
        mine = pltpu.make_async_copy(ins[k], outs[k].at[y, x, core, z], local_sem.at[k])
        mine.start()
        locals_.append(mine)
        along_z.append(
            [
                send(k, ins[k], outs[k].at[y, x, core, z], moved(here, 3, step, dims))
                for step in range(1, depth)
            ]
        )
        started += along_z[k]
    first, second, partner = [], [], []
    other = moved(here, 2, 1, dims)
    for k in range(count):
        locals_[k].wait()
        for copy in along_z[k]:
            copy.wait_recv()
        axis = k % 2
        block = outs[k].at[y, x, core]
        first.append(
            [send(k, block, block, moved(here, axis, s, dims)) for s in range(1, dims[axis])]
        )
        partner.append([send(k, block, block, other)])
        started += first[k] + partner[k]
    for k in range(count):
        axis = k % 2
        cross = 1 - axis
        for copy in first[k]:
            copy.wait_recv()
        copies = []
        for lag in range(dims[axis]):
            at = moved(here, axis, lag, dims)
            block = outs[k].at[at[0], at[1], core]
            copies += [
                send(k, block, block, moved(here, cross, s, dims)) for s in range(1, dims[cross])
            ]
            if lag:
                partner[k].append(send(k, block, block, other))
                started.append(partner[k][-1])
        second.append(copies)
        started += copies
    for k in range(count):
        axis = k % 2
        cross = 1 - axis
        copies = iter(second[k])
        for lag in range(dims[axis]):
            for s in range(1, dims[cross]):
                next(copies).wait_recv()
                at = moved(here, axis, lag, dims)
                at[cross] = lax.rem(here[cross] + dims[cross] - s, dims[cross])
                block = outs[k].at[at[0], at[1], core]
                partner[k].append(send(k, block, block, other))
                started.append(partner[k][-1])
    for k in range(count):
        for copy in partner[k]:
            copy.wait_recv()
    for copy in started:
        copy.wait_send()


def reduce_kernel(dims, count, *refs):
    ins, table = refs[:count], refs[count]
    outs, table_out = refs[count + 1 : 2 * count + 1], refs[2 * count + 1]
    rest = refs[2 * count + 2 :]
    bufs = [rest[7 * k : 7 * k + 7] for k in range(count)]
    table_in = rest[7 * count : 7 * count + 4]
    table_sum = rest[7 * count + 4 : 7 * count + 7]
    send_sem, recv_sem = rest[7 * count + 7 :]
    height, width, _, depth = dims
    here = whereabouts(dims)
    y, x, core, z = here
    greet(dims, here)
    used = [0] * (count + 1)
    started = []

    def send(stream, src, dst, there):
        slot = used[stream]
        used[stream] += 1
        copy = pltpu.make_async_remote_copy(
            src_ref=src,
            dst_ref=dst,
            send_sem=send_sem.at[stream, slot],
            recv_sem=recv_sem.at[stream, slot],
            device_id=device_at(dims, *there),
            device_id_type=MESH,
        )
        copy.start()
        started.append(copy)
        return copy

    def add(dst, parts):
        def body(i, carry):
            total = parts[0][i].astype(jnp.float32)
            for part in parts[1:]:
                total = total + part[i].astype(jnp.float32)
            dst[i] = total.astype(dst.dtype)
            return carry

        lax.fori_loop(0, depth, body, 0)

    def table_step(stage, axis, src):
        table_in[stage][here[axis]] = src[...]
        return [
            send(count, src, table_in[stage].at[here[axis]], moved(here, axis, s, dims))
            for s in range(1, dims[axis])
        ]

    def table_add(stage, axis, copies, dst):
        for copy in copies:
            copy.wait_recv()
        total = table_in[stage][0]
        for j in range(1, dims[axis]):
            total = total + table_in[stage][j]
        dst[...] = total

    other = moved(here, 2, 1, dims)
    table_copies = table_step(0, 2, table)
    core_copies = []
    for k in range(count):
        axis = k % 2
        cross = 1 - axis
        group = {}
        for lag in list(range(1, dims[axis])) + [0]:
            for j in range(dims[cross]):
                at = moved(here, axis, lag, dims)
                at[cross] = j
                group[lag, j] = send(
                    k, ins[k].at[at[0], at[1], other[2]], bufs[k][0].at[at[0], at[1]], other
                )
        core_copies.append(group)
    table_add(0, 2, table_copies, table_sum[0])
    table_copies = table_step(1, 0, table_sum[0])
    first = []
    for k in range(count):
        axis = k % 2
        cross = 1 - axis
        from_core, sum_core, from_first = bufs[k][0], bufs[k][1], bufs[k][2]
        group = []
        for lag in list(range(1, dims[axis])) + [0]:
            for j in range(dims[cross]):
                at = moved(here, axis, lag, dims)
                at[cross] = j
                core_copies[k][lag, j].wait_recv()
                block = sum_core.at[at[0], at[1]]
                add(block, [ins[k].at[at[0], at[1], core], from_core.at[at[0], at[1]]])
                if lag:
                    group.append(
                        send(k, block, from_first.at[lag - 1, j], moved(here, axis, lag, dims))
                    )
        first.append(group)
    table_add(1, 0, table_copies, table_sum[1])
    table_copies = table_step(2, 1, table_sum[1])
    second = []
    for k in range(count):
        axis = k % 2
        cross = 1 - axis
        sum_core, from_first, sum_first, from_second = bufs[k][1:5]
        for copy in first[k]:
            copy.wait_recv()
        group = []
        for lag in list(range(1, dims[cross])) + [0]:
            at = moved(here, cross, lag, dims)
            j = at[cross]
            block = sum_first.at[j]
            add(
                block,
                [sum_core.at[at[0], at[1]]]
                + [from_first.at[s - 1, j] for s in range(1, dims[axis])],
            )
            if lag:
                group.append(send(k, block, from_second.at[lag - 1], at))
        second.append(group)
    table_add(2, 1, table_copies, table_sum[2])
    table_copies = table_step(3, 3, table_sum[2])
    third = []
    for k in range(count):
        axis = k % 2
        cross = 1 - axis
        sum_first, from_second, sum_second, from_third = bufs[k][3:7]
        for copy in second[k]:
            copy.wait_recv()
        add(
            sum_second,
            [sum_first.at[here[cross]]] + [from_second.at[s - 1] for s in range(1, dims[cross])],
        )
        group = []
        for step in range(1, depth):
            at = moved(here, 3, step, dims)
            group.append(send(k, sum_second.at[at[3]], from_third.at[step - 1], at))
        third.append(group)
    table_add(3, 3, table_copies, table_out)
    for k in range(count):
        sum_second, from_third = bufs[k][5:7]
        for copy in third[k]:
            copy.wait_recv()
        total = sum_second[z].astype(jnp.float32)
        for step in range(1, depth):
            total = total + from_third[step - 1].astype(jnp.float32)
        outs[k][...] = total
    for copy in started:
        copy.wait_send()


def sizes_here():
    rows, depth = lax.axis_size("rows"), lax.axis_size("cols")
    height, width = grid_of(rows)
    return height, width, CORES, depth


def blocked(rows, columns):
    if rows % 16 == 0:
        return rows, columns
    return rows * columns // 128, 128


def gather_all(shards):
    dims = sizes_here()
    height, width, cores, depth = dims
    count = len(shards)
    blocks = [blocked(*shard.shape) for shard in shards]
    slots = (depth - 1) + max(height, width) * 2 * height * width
    outs = pl.pallas_call(
        functools.partial(gather_kernel, dims, count),
        name="gather_all",
        out_shape=[
            jax.ShapeDtypeStruct(dims + block, shard.dtype)
            for block, shard in zip(blocks, shards)
        ],
        in_specs=[pl.BlockSpec(memory_space=pltpu.VMEM)] * count,
        out_specs=[pl.BlockSpec(memory_space=pl.ANY)] * count,
        scratch_shapes=[
            pltpu.SemaphoreType.DMA((count,)),
            pltpu.SemaphoreType.DMA((count, slots)),
            pltpu.SemaphoreType.DMA((count, slots)),
        ],
        compiler_params=pltpu.CompilerParams(collective_id=0, has_side_effects=True),
    )(*[shard.reshape(block) for block, shard in zip(blocks, shards)])
    total = height * width * cores * depth
    return [
        out.reshape(total * shard.shape[0], shard.shape[1]) for out, shard in zip(outs, shards)
    ]


def reduce_all(wholes, table):
    dims = sizes_here()
    height, width, cores, depth = dims
    total = height * width * cores * depth
    count = len(wholes)
    shares = [(whole.shape[0] // total, whole.shape[1]) for whole in wholes]
    blocks = [blocked(*share) for share in shares]
    scratch = []
    for k, (block, whole) in enumerate(zip(blocks, wholes)):
        along, cross = dims[k % 2], dims[1 - k % 2]
        for lead in (
            (height, width, depth),
            (height, width, depth),
            (max(along - 1, 1), cross, depth),
            (cross, depth),
            (max(cross - 1, 1), depth),
            (depth,),
            (max(depth - 1, 1),),
        ):
            scratch.append(pltpu.VMEM(lead + block, whole.dtype))
    for size in (cores, height, width, depth):
        scratch.append(pltpu.VMEM((size,) + table.shape, table.dtype))
    scratch += [pltpu.VMEM(table.shape, table.dtype)] * 3
    slots = 2 * height * width + height + width + depth
    scratch += [pltpu.SemaphoreType.DMA((count + 1, slots))] * 2
    outs = pl.pallas_call(
        functools.partial(reduce_kernel, dims, count),
        name="reduce_all",
        out_shape=[jax.ShapeDtypeStruct(block, jnp.float32) for block in blocks]
        + [jax.ShapeDtypeStruct(table.shape, table.dtype)],
        in_specs=[pl.BlockSpec(memory_space=pltpu.VMEM)] * (count + 1),
        out_specs=[pl.BlockSpec(memory_space=pltpu.VMEM)] * (count + 1),
        scratch_shapes=scratch,
        compiler_params=pltpu.CompilerParams(collective_id=1, has_side_effects=True),
    )(*[whole.reshape(dims + block) for block, whole in zip(blocks, wholes)], table)
    return [out.reshape(share) for out, share in zip(outs, shares)], outs[-1]


def padded(values, multiple):
    size = values.shape[-1]
    extra = -size % multiple
    return jnp.pad(values, [(0, 0)] * (values.ndim - 1) + [(0, extra)])


def plain_block(
    images,
    cotangent,
    rel_index,
    rel_table,
    qkv_weight,
    proj_weight,
    up_weight,
    down_weight,
    norm1_gain,
    norm1_bias,
    query_bias,
    value_bias,
    proj_bias,
    norm2_gain,
    norm2_bias,
    up_bias,
    down_bias,
):
    shards = (
        norm1_gain,
        norm1_bias,
        query_bias,
        value_bias,
        proj_bias,
        norm2_gain,
        norm2_bias,
        up_bias,
        down_bias,
    )
    vector_shard = padded(jnp.concatenate(shards)[None], 2048).reshape(-1, 128)
    qkv_full, down_full, up_full, proj_full, vector_full = gather_all(
        [qkv_weight, down_weight, up_weight, proj_weight, vector_shard]
    )
    device_count = lax.axis_size("rows") * lax.axis_size("cols")
    vector_full = vector_full.reshape(device_count, -1)
    vectors, offset = [], 0
    for shard in shards:
        size = shard.shape[0]
        vectors.append(vector_full[:, offset : offset + size].reshape(device_count * size))
        offset += size
    (
        gain_one_full,
        bias_one_full,
        query_add,
        value_add,
        proj_add,
        gain_two_full,
        bias_two_full,
        up_add,
        down_add,
    ) = vectors
    tokens_tile, grad_tile = roll_in(images, cotangent)
    image_count, tile_side, features = (
        tokens_tile.shape[0],
        tokens_tile.shape[1],
        tokens_tile.shape[3],
    )
    window = tile_side * tile_side
    row_total = image_count * window
    tokens = tokens_tile.reshape(row_total, features)
    grad_rows = grad_tile.reshape(row_total, features)
    local_pos = jnp.arange(tile_side, dtype=jnp.int32)
    band_rows = band_of(
        lax.axis_index("rows") * tile_side + local_pos, lax.axis_size("rows") * tile_side
    )
    band_cols = band_of(
        lax.axis_index("cols") * tile_side + local_pos, lax.axis_size("cols") * tile_side
    )
    region = (3 * band_rows[:, None] + band_cols[None, :]).reshape(window)
    allowed = (region[:, None] == region[None, :])[None, None]
    head_count = rel_table.shape[1]
    table_size = rel_table.shape[0]
    head_width = features // head_count
    score_scale = head_width ** (-0.5)
    onehot = (
        rel_index.reshape(window * window)[:, None]
        == jnp.arange(table_size, dtype=jnp.int32)[None, :]
    ).astype(jnp.float32)
    bias_flat = jnp.dot(
        onehot, rel_table, precision=lax.Precision.HIGHEST, preferred_element_type=jnp.float32
    )
    bias_heads = bias_flat.T.reshape(head_count, window, window)

    def split_heads(values):
        return values.reshape(image_count, window, head_count, head_width)

    def scores_of(query_b, key_b):
        raw_scores = jnp.einsum(
            "wqhd,wkhd->whqk",
            split_heads(query_b),
            split_heads(key_b),
            preferred_element_type=jnp.float32,
        )
        return jnp.where(allowed, raw_scores + bias_heads[None], big_negative)

    gain_one = gain_one_full.astype(jnp.float32)
    gain_two = gain_two_full.astype(jnp.float32)
    out_one, normed_one, inv_one = layer_norm(tokens, gain_one, bias_one_full.astype(jnp.float32))
    h_one = out_one.astype(jnp.bfloat16)
    projected = dot_plain(h_one, qkv_full)
    query_b = ((projected[:, :features] + query_add.astype(jnp.float32)) * score_scale).astype(
        jnp.bfloat16
    )
    key_b = projected[:, features : 2 * features].astype(jnp.bfloat16)
    value_b = (projected[:, 2 * features :] + value_add.astype(jnp.float32)).astype(jnp.bfloat16)
    scores = scores_of(query_b, key_b)
    row_top = jnp.max(scores, axis=-1, keepdims=True)
    log_total = row_top + jnp.log(jnp.sum(jnp.exp(scores - row_top), axis=-1, keepdims=True))
    attend_b = jnp.exp(scores - log_total).astype(jnp.bfloat16)
    attn_b = (
        jnp.einsum(
            "whqk,wkhd->wqhd", attend_b, split_heads(value_b), preferred_element_type=jnp.float32
        )
        .reshape(row_total, features)
        .astype(jnp.bfloat16)
    )
    residual = tokens + dot_plain(attn_b, proj_full) + proj_add.astype(jnp.float32)
    out_two, normed_two, inv_two = layer_norm(residual, gain_two, bias_two_full.astype(jnp.float32))
    h_two = out_two.astype(jnp.bfloat16)
    hidden_pre = dot_plain(h_two, up_full) + up_add.astype(jnp.float32)
    gauss_cdf = 0.5 * (1.0 + lax.erf(hidden_pre * root_half))
    act_b = (hidden_pre * gauss_cdf).astype(jnp.bfloat16)
    result = residual + dot_plain(act_b, down_full) + down_add.astype(jnp.float32)
    grad_b = grad_rows.astype(jnp.bfloat16)
    grad_down = dot_lead(act_b, grad_b)
    grad_down_add = jnp.sum(grad_rows, axis=0)
    grad_act = dot_tail(grad_b, down_full)
    density = jnp.exp(-0.5 * hidden_pre * hidden_pre) * tau_factor
    grad_pre = grad_act * (gauss_cdf + hidden_pre * density)
    grad_pre_b = grad_pre.astype(jnp.bfloat16)
    grad_up = dot_lead(h_two, grad_pre_b)
    grad_up_add = jnp.sum(grad_pre, axis=0)
    grad_h_two = dot_tail(grad_pre_b, up_full)
    grad_resid, grad_gain_two, grad_bias_two = norm_back(
        grad_h_two, normed_two, inv_two, gain_two
    )
    grad_resid = grad_resid + grad_rows
    grad_resid_b = grad_resid.astype(jnp.bfloat16)
    grad_proj = dot_lead(attn_b, grad_resid_b)
    grad_proj_add = jnp.sum(grad_resid, axis=0)
    grad_attn_b = dot_tail(grad_resid_b, proj_full).astype(jnp.bfloat16)
    grad_heads = split_heads(grad_attn_b)
    grad_attend = jnp.einsum(
        "wqhd,wkhd->whqk", grad_heads, split_heads(value_b), preferred_element_type=jnp.float32
    )
    attend = jnp.exp(scores_of(query_b, key_b) - log_total)
    grad_value = jnp.einsum(
        "whqk,wqhd->wkhd",
        attend.astype(jnp.bfloat16),
        grad_heads,
        preferred_element_type=jnp.float32,
    ).reshape(row_total, features)
    row_inner = jnp.sum(attend * grad_attend, axis=-1, keepdims=True)
    grad_scores = attend * (grad_attend - row_inner)
    grad_bias_heads = jnp.sum(grad_scores, axis=0).reshape(head_count, window * window)
    table_local = lax.dot_general(
        onehot,
        grad_bias_heads,
        (((0,), (1,)), ((), ())),
        precision=lax.Precision.HIGHEST,
        preferred_element_type=jnp.float32,
    )
    grad_scores_b = grad_scores.astype(jnp.bfloat16)
    grad_query = (
        jnp.einsum(
            "whqk,wkhd->wqhd", grad_scores_b, split_heads(key_b), preferred_element_type=jnp.float32
        )
        * score_scale
    ).reshape(row_total, features)
    grad_key = jnp.einsum(
        "whqk,wqhd->wkhd", grad_scores_b, split_heads(query_b), preferred_element_type=jnp.float32
    ).reshape(row_total, features)
    grad_query_add = jnp.sum(grad_query, axis=0)
    grad_value_add = jnp.sum(grad_value, axis=0)
    grad_mixed_b = jnp.concatenate([grad_query, grad_key, grad_value], axis=1).astype(jnp.bfloat16)
    grad_qkv = dot_lead(h_one, grad_mixed_b)
    grad_h_one = dot_tail(grad_mixed_b, qkv_full)
    grad_in, grad_gain_one, grad_bias_one = norm_back(
        grad_h_one, normed_one, inv_one, gain_one
    )
    grad_tokens = grad_resid + grad_in
    vector_grads = (
        grad_gain_one,
        grad_bias_one,
        grad_query_add,
        grad_value_add,
        grad_proj_add,
        grad_gain_two,
        grad_bias_two,
        grad_up_add,
        grad_down_add,
    )
    vector_rows = padded(
        jnp.concatenate([grad.reshape(device_count, -1) for grad in vector_grads], axis=1), 2048
    ).reshape(-1, 128)
    table_rows = padded(table_local.reshape(1, -1), 1024).reshape(-1, 128)
    (down_sum, up_sum, qkv_sum, proj_sum, vector_sum), table_sum = reduce_all(
        [
            grad_down.astype(jnp.bfloat16),
            grad_up.astype(jnp.bfloat16),
            grad_qkv.astype(jnp.bfloat16),
            grad_proj.astype(jnp.bfloat16),
            vector_rows,
        ],
        table_rows,
    )
    grad_table = table_sum.reshape(-1)[: table_local.size].reshape(table_local.shape)
    vector_sum = vector_sum.reshape(-1)
    vector_sums, offset = [], 0
    for shard in shards:
        size = shard.shape[0]
        vector_sums.append(vector_sum[offset : offset + size])
        offset += size
    shard_grads = (qkv_sum, proj_sum, up_sum, down_sum, *vector_sums)
    block_out, grad_images = roll_out(
        result.reshape(image_count, tile_side, tile_side, features),
        grad_tokens.reshape(image_count, tile_side, tile_side, features),
    )
    return (
        block_out,
        grad_images,
        shard_grads[0],
        shard_grads[1],
        shard_grads[2],
        shard_grads[3],
        shard_grads[4],
        shard_grads[5],
        shard_grads[6],
        shard_grads[7],
        shard_grads[8],
        shard_grads[9],
        shard_grads[10],
        shard_grads[11],
        shard_grads[12],
        grad_table,
    )


LANES = 128


def dot_nt(former, latter):
    return lax.dot_general(
        former, latter, (((1,), (1,)), ((), ())), preferred_element_type=jnp.float32
    )


def dot_tn(former, latter):
    return lax.dot_general(
        former, latter, (((0,), (0,)), ((), ())), preferred_element_type=jnp.float32
    )


def iota(shape, dim):
    return lax.broadcasted_iota(jnp.int32, shape, dim)


def aligned(value, multiple):
    return pl.multiple_of(value, multiple)


class Plan:
    def __init__(self, dims, images, rel_table, weights, vectors):
        self.dims = dims
        self.depth = dims[3]
        self.images, self.side, _, self.features = images.shape
        self.keep = self.side - SHIFT
        self.pitch = self.side + 1
        self.span = self.side * self.pitch
        self.rows = self.images * self.span
        self.table_size, self.heads = rel_table.shape
        self.head_width = self.features // self.heads
        self.group_heads = LANES // self.head_width
        self.groups = self.features // LANES
        self.lanes = self.group_heads * self.span
        self.table_rows = -(-self.table_size // 16) * 16
        self.shard_rows = [w.shape[0] for w in weights]
        self.widths = [w.shape[1] for w in weights]
        self.devices = dims[0] * dims[1] * dims[2] * dims[3]
        self.hidden = weights[2].shape[1]
        self.vector_sizes = [v.shape[0] for v in vectors]


def fits_fused(dims, images, weights, vectors):
    return (
        dims[0] == 2
        and dims[1] == 2
        and dims[2] == 2
        and dims[3] > 1
        and all(w.shape[0] % 16 == 0 for w in weights)
        and images.shape[1] == WIN
        and images.shape[2] == WIN
    )


def block_kernel(plan, *refs):
    p = plan
    take = iter(refs)

    def pull(count):
        return [next(take) for _ in range(count)]

    images, cotangent, rel_index, rel_table = pull(4)
    vector_ins = pull(9)
    shards = pull(4)
    out_y, out_g = pull(2)
    out_w = pull(4)
    (small_out,) = pull(1)
    (
        vec_shard,
        vec_full,
        vec,
        up_vec,
        xs,
        gs,
        normed,
        inv,
        h_b,
        qkv,
        probs,
        attn,
        attn_b,
        x1,
        normed2,
        inv2,
        h2_b,
        gy_b,
        act_b,
        dpre_b,
        ys,
        dh2,
        dx1,
        dx1_b,
        dattn,
        dqkv,
        dqkv_b,
        dh1,
        work,
        square,
        flipped,
        flipped_pad,
        index_t,
        tab,
        tab_b,
        onehot,
        bias_cube,
        bias,
        dbias,
        dcube,
        dtab,
        sums,
        sums_up,
        small,
        small_in,
        small_mid,
        small_z,
    ) = pull(47)
    full = pull(4)
    grads = pull(4)
    core_in = pull(4)
    x_in, y_in, a_in, b_in, z_in = pull(4), pull(4), pull(4), pull(4), pull(4)
    halo_in_src, halo_in_dst, halo_y_src, halo_y_dst, halo_g_src, halo_g_dst = pull(6)
    g_send, g_recv, r_send, r_recv, h_send, h_recv, s_send, s_recv = pull(8)

    dims, depth = p.dims, p.depth
    rows_total = lax.axis_size("rows")
    row, z = lax.axis_index("rows"), lax.axis_index("cols")
    here = whereabouts(dims)
    y, x, core = here[0], here[1], here[2]
    me = row * depth + z
    partner_at = (y * dims[1] + x) * CORES + (1 - core)
    x_at = (y * dims[1] + (1 - x)) * CORES + core
    y_at = ((1 - y) * dims[1] + x) * CORES + core
    chip_own = y * dims[1] + x
    chip_x = y * dims[1] + (1 - x)
    chip_y = (1 - y) * dims[1] + x
    chip_d = (1 - y) * dims[1] + (1 - x)
    row_up, row_down = lax.rem(row + rows_total - 1, rows_total), lax.rem(row + 1, rows_total)
    col_up, col_down = lax.rem(z + depth - 1, depth), lax.rem(z + 1, depth)
    started = []

    def remote(src, dst, send_sem, recv_sem, device):
        return pltpu.make_async_remote_copy(
            src_ref=src,
            dst_ref=dst,
            send_sem=send_sem,
            recv_sem=recv_sem,
            device_id=device,
            device_id_type=MESH,
        )

    def launch(*args):
        copy = remote(*args)
        copy.start()
        started.append(copy)
        return copy

    barrier = pltpu.get_barrier_semaphore()
    peers = [(lax.rem(row + s, rows_total), z) for s in range(1, rows_total)]
    peers += [(row, lax.rem(z + s, depth)) for s in range(1, depth)]
    peers += [(row_up, col_up), (row_down, col_down)]
    for peer in peers:
        pl.semaphore_signal(barrier, inc=1, device_id=peer, device_id_type=MESH)

    span, pitch, keep, side = p.span, p.pitch, p.keep, p.side
    halo_rows = 4 * keep

    def pack(read, dst, slot_of):
        for piece, (row_list, col_at, cols) in enumerate(slot_of):

            def body(b, carry):
                parts = [read(b, i, col_at) for i in row_list]
                parts += [jnp.zeros_like(parts[0])] * (4 - len(parts))
                value = jnp.concatenate(parts, axis=0)
                if cols < keep:
                    value = jnp.where(lax.rem(iota(value.shape, 0), keep) < cols, value, 0.0)
                dst(piece, b)[...] = value.astype(jnp.bfloat16)
                return carry

            lax.fori_loop(0, p.images, body, 0)

    head, rest = list(range(SHIFT)), list(range(SHIFT, side))
    pieces_in = [(head, SHIFT, keep), (rest, 0, SHIFT), (head, 0, SHIFT)]
    for n, source in enumerate((images, cotangent)):
        pack(
            lambda b, i, c, source=source: source[b, i, pl.ds(c, keep), :],
            lambda piece, b, n=n: halo_in_src.at[
                piece, n, pl.ds(aligned(b * halo_rows, 16), halo_rows)
            ],
            pieces_in,
        )

    vec_shard[...] = jnp.zeros_like(vec_shard)
    for k, ref in enumerate(vector_ins):
        vec_shard[k : k + 1, : p.vector_sizes[k]] = ref[...].astype(jnp.float32)
    vec_b = vec_full.at[pl.ds(aligned(me * 16, 16), 16)]
    vec_b[...] = vec_shard[...].astype(jnp.bfloat16)

    streams = [(vec_full, 16, LANES)] + [
        (full[k], p.shard_rows[k], p.widths[k]) for k in range(4)
    ]
    for k in range(4):
        size = p.shard_rows[k]
        full[k][pl.ds(aligned(me * size, 16), size), :] = shards[k][...]

    pl.semaphore_wait(barrier, len(peers))

    halo_in = []
    for piece, device in enumerate(((row_up, z), (row, col_up), (row_up, col_up))):
        halo_in.append(
            launch(
                halo_in_src.at[piece], halo_in_dst.at[piece], h_send.at[piece], h_recv.at[piece],
                device,
            )
        )

    along_z = {}
    hops = {}

    def g_copy(k, slot, src, device):
        copy = launch(src, src, g_send.at[k, slot], g_recv.at[k, slot], device)
        hops[k, slot] = copy

    def block_of(k, row_at):
        ref, size, _ = streams[k]
        return ref.at[pl.ds(aligned(row_at * depth * size, 16), depth * size)]

    def chip_row(chip):
        return chip * CORES + core

    def half(ref, k, which):
        width = streams[k][2]
        if width == LANES:
            return ref
        middle = width // 2
        return ref.at[:, pl.ds(which * middle, middle)]

    def gather_z(k):
        ref, size, _ = streams[k]
        mine = ref.at[pl.ds(aligned(me * size, 16), size)]
        for s in range(1, depth):
            g_copy(k, 12 + s, mine, (row, lax.rem(z + s, depth)))

    def gather_one(k):
        for s in range(1, depth):
            hops[k, 12 + s].wait_recv()
        block = block_of(k, row)
        g_copy(k, 0, block, (x_at, z))
        g_copy(k, 1, block, (y_at, z))
        g_copy(k, 4, block, (partner_at, z))

    def gather_two(k):
        single = streams[k][2] == LANES
        from_x, from_y = block_of(k, chip_row(chip_x)), block_of(k, chip_row(chip_y))
        hops[k, 0].wait_recv()
        g_copy(k, 2, half(from_x, k, 0), (y_at, z))
        g_copy(k, 5, from_x, (partner_at, z))
        hops[k, 1].wait_recv()
        if not single:
            g_copy(k, 3, half(from_y, k, 1), (x_at, z))
        g_copy(k, 6, from_y, (partner_at, z))

    def gather_three(k):
        single = streams[k][2] == LANES
        corner = block_of(k, chip_row(chip_d))
        hops[k, 2].wait_recv()
        g_copy(k, 7, half(corner, k, 0), (partner_at, z))
        if not single:
            hops[k, 3].wait_recv()
            g_copy(k, 8, half(corner, k, 1), (partner_at, z))

    def gather_end(k):
        for slot in (4, 5, 6, 7, 8):
            if (k, slot) in hops:
                hops[k, slot].wait_recv()

    VEC, QKV, PROJ, UP, DOWN = range(5)
    gather_z(VEC)
    gather_z(QKV)
    gather_z(PROJ)

    window = side * side
    square[...] = jnp.full(square.shape, -1.0, jnp.float32)
    raw_index = rel_index[...].astype(jnp.float32)
    for i in range(side):
        square[i * pitch : i * pitch + side, :window] = raw_index[i * side : (i + 1) * side]
    flipped[...] = square[...].T
    index_t[...] = jnp.full(index_t.shape, -1.0, jnp.float32)
    for i in range(side):
        index_t[i * pitch : i * pitch + side, :] = flipped[i * side : (i + 1) * side, :]
    tab[...] = jnp.zeros_like(tab)
    tab[: p.table_size, : p.heads] = rel_table[...]
    tab_high = tab[...].astype(jnp.bfloat16)
    tab_b[0] = tab_high
    tab_b[1] = (tab[...] - tab_high.astype(jnp.float32)).astype(jnp.bfloat16)

    def bias_step(c, carry):
        wanted = index_t[pl.ds(c, 1), :]
        hot = (iota((p.table_rows, LANES), 0).astype(jnp.float32) == wanted).astype(jnp.float32)
        hot = hot.astype(jnp.bfloat16)
        onehot[c] = hot
        entry = dot_tn(tab_b[0], hot) + dot_tn(tab_b[1], hot)
        bias_cube[:, c, :] = entry[: p.heads]
        return carry

    lax.fori_loop(0, span, bias_step, 0)

    def band(local, tile, axis):
        length = lax.axis_size(axis) * side
        at = tile * side + local
        return jnp.where(at >= length - WIN, 1, 0) + jnp.where(at >= length - SHIFT, 1, 0)

    def region_of(token):
        return 3 * band(token // pitch, row, "rows") + band(lax.rem(token, pitch), z, "cols")

    key_token = iota((span, p.lanes), 0)
    query_token = lax.rem(iota((span, p.lanes), 1), span)
    allowed = (region_of(key_token) == region_of(query_token)) & (
        lax.rem(key_token, pitch) < side
    )
    for g in range(p.groups):
        parts = [bias_cube[g * p.group_heads + h][:, :span] for h in range(p.group_heads)]
        bias[g] = jnp.where(allowed, jnp.concatenate(parts, axis=1), big_negative)

    gather_one(VEC)
    gather_one(QKV)
    gather_z(UP)

    def arrive(b, carry):
        for n, (source, dst) in enumerate(((images, xs), (cotangent, gs))):
            at = pl.ds(aligned(b * halo_rows, 16), halo_rows)
            by_row = halo_in_dst[0, n, at].astype(jnp.float32)
            by_col = halo_in_dst[1, n, at].astype(jnp.float32)
            by_both = halo_in_dst[2, n, at].astype(jnp.float32)
            for i in range(side):
                if i < keep:
                    left = source[b, i + SHIFT, SHIFT:side, :]
                    right = by_col[keep * i : keep * i + keep]
                else:
                    left = by_row[keep * (i - keep) : keep * (i - keep) + keep]
                    right = by_both[keep * (i - keep) : keep * (i - keep) + keep]
                if n == 1 and i < keep:
                    left = left
                dst[pl.ds(aligned(b * span + i * pitch, 8), pitch), :] = jnp.concatenate(
                    [left, right], axis=0
                )
        return carry

    def spans(body, count=None):
        lax.fori_loop(0, p.images if count is None else count, body, 0)

    def span_at(w):
        return pl.ds(aligned(w * span, 8), span)

    for copy in halo_in:
        copy.wait_recv()
    spans(arrive)
    gy_b[...] = gs[...].astype(jnp.bfloat16)

    def center(ref, dst, inv_ref):
        def body(w, carry):
            value = ref[span_at(w), :]
            mean_val = jnp.mean(value, axis=-1, keepdims=True)
            centred = value - mean_val
            inv_std = lax.rsqrt(
                jnp.mean(centred * centred, axis=-1, keepdims=True) + norm_eps
            )
            dst[span_at(w), :] = centred * inv_std
            inv_ref[span_at(w), :] = jnp.broadcast_to(inv_std, (span, LANES))
            return carry

        spans(body)

    center(xs, normed, inv)
    gather_two(VEC)
    gather_two(QKV)
    gather_one(PROJ)
    gather_three(VEC)
    gather_three(QKV)
    gather_two(PROJ)
    gather_end(VEC)

    size = p.vector_sizes[0]
    per = LANES // size
    for t in range(p.features // LANES):
        spread = (lax.rem(iota((LANES, LANES), 1), size) == iota((LANES, LANES), 0)).astype(
            jnp.float32
        ).astype(jnp.bfloat16)
        value = dot_plain(vec_full[t * per * 16 : (t + 1) * per * 16, :], spread)
        mine = iota(value.shape, 0) // 16 == iota(value.shape, 1) // size
        value = jnp.where(mine, value, 0.0)
        total = value[0:16]
        for d in range(1, per):
            total = total + value[d * 16 : (d + 1) * 16]
        vec[:, t * LANES : (t + 1) * LANES] = total
    size_up = p.vector_sizes[7]
    per_up = LANES // size_up
    for t in range(p.hidden // LANES):
        spread = (lax.rem(iota((LANES, LANES), 1), size_up) == iota((LANES, LANES), 0)).astype(
            jnp.float32
        ).astype(jnp.bfloat16)
        value = dot_plain(vec_full[t * per_up * 16 : (t + 1) * per_up * 16, :], spread)
        mine = iota(value.shape, 0) == 16 * (iota(value.shape, 1) // size_up) + 7
        value = jnp.where(mine, value, 0.0)
        up_vec[:, t * LANES : (t + 1) * LANES] = jnp.sum(value, axis=0, keepdims=True)

    def vector(k):
        return vec[k : k + 1, :]

    h_b[...] = (normed[...] * vector(0) + vector(1)).astype(jnp.bfloat16)
    gather_end(QKV)

    scale = p.head_width ** (-0.5)
    features = p.features
    for n in range(3):
        cols = slice(n * features, (n + 1) * features)
        value = dot_plain(h_b[...], full[0][:, cols])
        if n == 0:
            value = (value + vector(2)) * scale
        if n == 2:
            value = value + vector(3)
        qkv[:, cols] = value
    gather_three(PROJ)
    gather_one(UP)
    gather_z(DOWN)

    def expand(value):
        lane = iota(value.shape, 1) // p.head_width
        parts = [jnp.where(lane == h, value, 0.0) for h in range(p.group_heads)]
        return jnp.concatenate(parts, axis=0).astype(jnp.bfloat16)

    def fold(value):
        total = None
        for h in range(p.group_heads):
            part = value[h * span : (h + 1) * span]
            part = jnp.where(iota(part.shape, 1) // p.head_width == h, part, 0.0)
            total = part if total is None else total + part
        return total

    def lanes_at(g, third=0):
        return pl.ds(aligned(third * features + g * LANES, LANES), LANES)

    def attend(w):
        def body(g, carry):
            at = span_at(w)
            query = qkv[at, lanes_at(g, 0)]
            key = qkv[at, lanes_at(g, 1)].astype(jnp.bfloat16)
            value = qkv[at, lanes_at(g, 2)].astype(jnp.bfloat16)
            scores = dot_nt(key, expand(query)) + bias[g]
            top = jnp.max(scores, axis=0, keepdims=True)
            weight = jnp.exp(scores - top)
            prob = weight / jnp.sum(weight, axis=0, keepdims=True)
            probs[w * p.groups + g] = prob
            attn[at, lanes_at(g)] = fold(dot_tn(prob.astype(jnp.bfloat16), value))
            return carry

        lax.fori_loop(0, p.groups, body, 0)

    steps = {
        0: [lambda: gather_two(UP)],
        1: [lambda: gather_end(PROJ)],
        2: [lambda: gather_three(UP), lambda: gather_one(DOWN)],
        3: [],
    }
    for w in range(p.images):
        attend(w)
        for step in steps.get(w, []):
            step()
    gather_two(DOWN)
    attn_b[...] = attn[...].astype(jnp.bfloat16)
    x1[...] = xs[...] + dot_plain(attn_b[...], full[1][...]) + vector(4)
    center(x1, normed2, inv2)
    h2_b[...] = (normed2[...] * vector(5) + vector(6)).astype(jnp.bfloat16)
    gather_end(UP)
    gather_three(DOWN)
    gather_end(DOWN)

    ys[...] = x1[...] + vector(8)
    dh2[...] = jnp.zeros_like(dh2)
    tiles = dims[0] * dims[1]
    tile = p.hidden // tiles
    DN, UPW, PR, QK = 0, 1, 2, 3
    order = [3, 2, 1, 0]
    red = {
        DN: (grads[3], p.shard_rows[3], p.widths[3]),
        UPW: (grads[2], p.shard_rows[2], p.widths[2]),
        PR: (grads[1], p.shard_rows[1], p.widths[1]),
        QK: (grads[0], p.shard_rows[0], p.widths[0]),
    }
    sums[...] = jnp.zeros_like(sums)

    def core_copy(k, chip):
        ref, size, _ = red[k]
        at = (chip * CORES + (1 - core)) * depth * size
        return remote(
            ref.at[pl.ds(aligned(at, 16), depth * size)],
            core_in[k].at[chip],
            r_send.at[k, chip],
            r_recv.at[k, chip],
            (partner_at, z),
        )

    def feed(j, carry):
        at = pl.ds(aligned(j * tile, LANES), tile)
        pre = dot_plain(h2_b[...], full[2][:, at]) + up_vec[:, at]
        cdf = 0.5 * (1.0 + lax.erf(pre * root_half))
        act = (pre * cdf).astype(jnp.bfloat16)
        slope = cdf + pre * (jnp.exp(-0.5 * pre * pre) * tau_factor)
        down_rows = full[3][at, :]
        ys[...] += dot_plain(act, down_rows)
        dpre = dot_nt(gy_b[...], down_rows) * slope
        sums_up[:, at] = jnp.sum(dpre, axis=0, keepdims=True)
        dpre_low = dpre.astype(jnp.bfloat16)
        dh2[...] += dot_nt(dpre_low, full[2][:, at])
        grads[3][at, :] = dot_tn(act, gy_b[...]).astype(jnp.bfloat16)
        grads[2][:, at] = dot_tn(h2_b[...], dpre_low).astype(jnp.bfloat16)
        core_copy(DN, j).start()
        return carry

    lax.fori_loop(0, tiles, feed, 0)
    for chip in range(tiles):
        core_copy(UPW, chip).start()

    r_hops = {}

    def r_copy(k, slot, src, dst, device):
        r_hops[k, slot] = launch(src, dst, r_send.at[k, slot], r_recv.at[k, slot], device)

    def add_into(dst, parts, width_at, width):
        count = dst.shape[0]
        step = 16 if count % 32 else 32

        def body(i, carry):
            at = pl.ds(aligned(i * step, 16), step)
            cols = pl.ds(width_at, width)
            total = dst[at, cols].astype(jnp.float32)
            for part in parts:
                total = total + part[at, :].astype(jnp.float32)
            dst[at, cols] = total.astype(jnp.bfloat16)
            return carry

        lax.fori_loop(0, count // step, body, 0)

    def reduce_core(k):
        ref, size, width = red[k]
        middle = width // 2
        for chip in range(tiles):
            core_copy(k, chip).wait_recv()
        for chip in range(tiles):
            at = (chip * CORES + core) * depth * size
            add_into(
                core_in[k].at[chip],
                [ref.at[pl.ds(aligned(at, 16), depth * size)]],
                0,
                width,
            )
        corner = core_in[k].at[chip_d]
        r_copy(k, 4, corner.at[:, pl.ds(0, middle)], a_in[k], (y_at, z))
        r_copy(k, 5, corner.at[:, pl.ds(middle, middle)], b_in[k], (x_at, z))

    def reduce_cross(k):
        middle = red[k][2] // 2
        to_x, to_y = core_in[k].at[chip_x], core_in[k].at[chip_y]
        r_hops[k, 4].wait_recv()
        add_into(to_x, [a_in[k]], 0, middle)
        r_copy(k, 6, to_x, x_in[k], (x_at, z))
        r_hops[k, 5].wait_recv()
        add_into(to_y, [b_in[k]], middle, middle)
        r_copy(k, 7, to_y, y_in[k], (y_at, z))

    def reduce_chip(k):
        _, size, width = red[k]
        own = core_in[k].at[chip_own]
        r_hops[k, 6].wait_recv()
        r_hops[k, 7].wait_recv()
        add_into(own, [x_in[k], y_in[k]], 0, width)
        for s in range(1, depth):
            there = lax.rem(z + s, depth)
            r_copy(
                k,
                7 + s,
                own.at[pl.ds(aligned(there * size, 16), size)],
                z_in[k].at[s - 1],
                (row, there),
            )

    def reduce_end(k):
        _, size, width = red[k]
        for s in range(1, depth):
            r_hops[k, 7 + s].wait_recv()
        total = core_in[k][chip_own, pl.ds(aligned(z * size, 16), size), :].astype(jnp.float32)
        for s in range(1, depth):
            total = total + z_in[k][s - 1].astype(jnp.float32)
        out_w[order[k]][...] = total

    def norm_grad(d_ref, n_ref, inv_ref, gain_at, dst, base, keep_sums):
        gain_row, bias_row = keep_sums

        def body(w, carry):
            at = span_at(w)
            d_val, n_val = d_ref[at, :], n_ref[at, :]
            scaled = d_val * vector(gain_at)
            inner = (
                scaled
                - jnp.mean(scaled, axis=-1, keepdims=True)
                - n_val * jnp.mean(scaled * n_val, axis=-1, keepdims=True)
            )
            dst[at, :] = base[at, :] + inv_ref[at, :][:, :1] * inner
            sums[gain_row : gain_row + 1, :] += jnp.sum(d_val * n_val, axis=0, keepdims=True)
            sums[bias_row : bias_row + 1, :] += jnp.sum(d_val, axis=0, keepdims=True)
            return carry

        spans(body)

    def read_span(ref):
        return lambda b, i, c: ref[
            pl.ds(aligned(b * span + i * pitch, 8), pitch), :
        ][c : c + keep]

    first_rows, last_rows = list(range(keep)), list(range(keep, side))
    pieces_out = [(last_rows, 0, keep), (first_rows, keep, SHIFT), (last_rows, keep, SHIFT)]

    def halo_out(ref, src, dst, base):
        pack(
            read_span(ref),
            lambda piece, b: src.at[piece, pl.ds(aligned(b * halo_rows, 16), halo_rows)],
            pieces_out,
        )
        return [
            launch(
                src.at[piece], dst.at[piece], h_send.at[base + piece], h_recv.at[base + piece],
                device,
            )
            for piece, device in enumerate(((row_down, z), (row, col_down), (row_down, col_down)))
        ]

    def halo_land(copies, ref, dst, out):
        for copy in copies:
            copy.wait_recv()

        def body(b, carry):
            at = pl.ds(aligned(b * halo_rows, 16), halo_rows)
            by_row = dst[0, at].astype(jnp.float32)
            by_col = dst[1, at].astype(jnp.float32)
            by_both = dst[2, at].astype(jnp.float32)
            for i in range(side):
                if i < SHIFT:
                    left = by_both[keep * i : keep * i + SHIFT]
                    right = by_row[keep * i : keep * i + keep]
                else:
                    k = i - SHIFT
                    left = by_col[keep * k : keep * k + SHIFT]
                    right = ref[pl.ds(aligned(b * span + k * pitch, 8), pitch), :][:keep]
                out[b, i] = jnp.concatenate([left, right], axis=0)
            return carry

        spans(body)

    y_copies = halo_out(ys, halo_y_src, halo_y_dst, 3)
    norm_grad(dh2, normed2, inv2, 5, dx1, gs, (5, 6))
    dx1_b[...] = dx1[...].astype(jnp.bfloat16)
    dattn[...] = dot_nt(dx1_b[...], full[1][...])
    reduce_core(DN)
    grads[1][...] = dot_tn(attn_b[...], dx1_b[...]).astype(jnp.bfloat16)
    for chip in range(tiles):
        core_copy(PR, chip).start()
    sums[4:5, :] = jnp.sum(dx1[...], axis=0, keepdims=True)
    sums[7:8, :] = jnp.sum(gs[...], axis=0, keepdims=True)
    reduce_core(UPW)

    dbias[...] = jnp.zeros_like(dbias)

    def attend_back(w):
        def body(g, carry):
            at = span_at(w)
            query = expand(qkv[at, lanes_at(g, 0)])
            key = qkv[at, lanes_at(g, 1)].astype(jnp.bfloat16)
            value = qkv[at, lanes_at(g, 2)].astype(jnp.bfloat16)
            grad = expand(dattn[at, lanes_at(g)])
            prob = probs[w * p.groups + g]
            dprob = dot_nt(value, grad)
            dscore = prob * (dprob - jnp.sum(prob * dprob, axis=0, keepdims=True))
            dbias[g] += dscore
            dlow = dscore.astype(jnp.bfloat16)
            dqkv[at, lanes_at(g, 2)] = dot_plain(prob.astype(jnp.bfloat16), grad)
            dqkv[at, lanes_at(g, 1)] = dot_plain(dlow, query)
            dqkv[at, lanes_at(g, 0)] = fold(dot_tn(dlow, key)) * scale
            return carry

        lax.fori_loop(0, p.groups, body, 0)

    back_steps = {
        0: [lambda: reduce_cross(DN)],
        1: [lambda: reduce_core(PR), lambda: reduce_cross(UPW)],
        2: [lambda: reduce_chip(DN)],
        3: [lambda: reduce_cross(PR)],
    }
    for w in range(p.images):
        attend_back(w)
        for step in back_steps.get(w, []):
            step()

    dqkv_b[...] = dqkv[...].astype(jnp.bfloat16)
    for n in range(3):
        cols = slice(n * features, (n + 1) * features)
        grads[0][:, cols] = dot_tn(h_b[...], dqkv_b[:, cols]).astype(jnp.bfloat16)
    for chip in range(tiles):
        core_copy(QK, chip).start()
    dh1[...] = dot_nt(dqkv_b[...], full[0][...])
    reduce_core(QK)
    norm_grad(dh1, normed, inv, 0, work, dx1, (0, 1))
    g_copies = halo_out(work, halo_g_src, halo_g_dst, 6)
    sums[2:3, :] = jnp.sum(dqkv[:, :features], axis=0, keepdims=True)
    sums[3:4, :] = jnp.sum(dqkv[:, 2 * features :], axis=0, keepdims=True)
    reduce_chip(UPW)
    reduce_chip(PR)

    for g in range(p.groups):
        for h in range(p.group_heads):
            dcube[g * p.group_heads + h, :, :span] = dbias[g][:, h * span : (h + 1) * span]
    dtab[...] = jnp.zeros_like(dtab)

    def table_step(c, carry):
        value = dcube[:, c, :][:, :span]
        high = value.astype(jnp.bfloat16)
        low = (value - high.astype(jnp.float32)).astype(jnp.bfloat16)
        hot = onehot[c][:, :span]
        dtab[...] += dot_nt(high, hot) + dot_nt(low, hot)
        return carry

    lax.fori_loop(0, span, table_step, 0)
    reduce_cross(QK)

    small[...] = jnp.zeros_like(small)
    wide = small.shape[1]
    at = 0
    for k in range(8):
        for t in range(features // wide):
            small[at : at + 1, :] = sums[k : k + 1, t * wide : (t + 1) * wide]
            at += 1
    for t in range(p.hidden // wide):
        small[at : at + 1, :] = sums_up[:, t * wide : (t + 1) * wide]
        at += 1
    small[at : at + p.heads, : p.table_rows] = dtab[...]
    share = small.shape[0] // dims[0] // dims[1] // dims[2]
    own_rows = pl.ds(aligned(row * share, 8), share)
    s_copies = []
    for s in range(1, dims[0] * dims[1] * dims[2]):
        there = lax.rem(row + s, rows_total)
        s_copies.append(
            launch(
                small.at[pl.ds(aligned(there * share, 8), share)],
                small_in.at[s - 1],
                s_send.at[0, s],
                s_recv.at[0, s],
                (there, z),
            )
        )
    for copy in s_copies:
        copy.wait_recv()
    total = small[own_rows, :]
    for s in range(1, dims[0] * dims[1] * dims[2]):
        total = total + small_in[s - 1]
    small_mid[...] = total
    small_z[z] = total
    s_copies = [
        launch(
            small_mid,
            small_z.at[z],
            s_send.at[1, s],
            s_recv.at[1, s],
            (row, lax.rem(z + s, depth)),
        )
        for s in range(1, depth)
    ]
    reduce_chip(QK)
    reduce_end(DN)
    for copy in s_copies:
        copy.wait_recv()
    total = small_z[0]
    for s in range(1, depth):
        total = total + small_z[s]
    small_out[own_rows, :] = total
    s_copies = [
        launch(
            small_out.at[own_rows],
            small_out.at[own_rows],
            s_send.at[2, s],
            s_recv.at[2, s],
            (lax.rem(row + s, rows_total), z),
        )
        for s in range(1, dims[0] * dims[1] * dims[2])
    ]
    halo_land(y_copies, ys, halo_y_dst, out_y)
    reduce_end(UPW)
    halo_land(g_copies, work, halo_g_dst, out_g)
    reduce_end(PR)
    reduce_end(QK)
    for copy in s_copies:
        copy.wait_recv()
    for k in range(4):
        for chip in range(tiles):
            core_copy(k, chip).wait_send()
    for copy in started:
        copy.wait_send()


def fused_block(dims, images, cotangent, rel_index, rel_table, weights, vectors):
    p = Plan(dims, images, rel_table, weights, vectors)
    f32, bf16 = jnp.float32, jnp.bfloat16
    rows, feats, hidden, span = p.rows, p.features, p.hidden, p.span
    tiles, depth, plane = dims[0] * dims[1], p.depth, dims[0] * dims[1] * dims[2]
    wide = 2 * LANES
    small_rows = (8 * feats + hidden) // wide + p.heads
    small_rows = -(-small_rows // (8 * plane)) * 8 * plane

    def v(*shape, dtype=f32):
        return pltpu.VMEM(shape, dtype)

    scratch = [
        v(16, LANES),
        v(p.devices * 16, LANES, dtype=bf16),
        v(16, feats),
        v(1, hidden),
        v(rows, feats),
        v(rows, feats),
        v(rows, feats),
        v(rows, LANES),
        v(rows, feats, dtype=bf16),
        v(rows, 3 * feats),
        v(p.images * p.groups, span, p.lanes),
        v(rows, feats),
        v(rows, feats, dtype=bf16),
        v(rows, feats),
        v(rows, feats),
        v(rows, LANES),
        v(rows, feats, dtype=bf16),
        v(rows, feats, dtype=bf16),
        v(8, LANES),
        v(8, LANES),
        v(rows, feats),
        v(rows, feats),
        v(rows, feats),
        v(rows, feats, dtype=bf16),
        v(rows, feats),
        v(rows, 3 * feats),
        v(rows, 3 * feats, dtype=bf16),
        v(rows, feats),
        v(rows, feats),
        v(LANES, LANES),
        v(LANES, LANES),
        v(8, LANES),
        v(span, LANES),
        v(p.table_rows, LANES),
        v(2, p.table_rows, LANES, dtype=bf16),
        v(span, p.table_rows, LANES, dtype=bf16),
        v(p.heads, span, LANES),
        v(p.groups, span, p.lanes),
        v(p.groups, span, p.lanes),
        v(p.heads, span, LANES),
        v(p.heads, p.table_rows),
        v(8, feats),
        v(1, hidden),
        v(small_rows, wide),
        v(plane - 1, small_rows // plane, wide),
        v(small_rows // plane, wide),
        v(depth, small_rows // plane, wide),
    ]
    sizes = [(w.shape[0], w.shape[1]) for w in weights]
    scratch += [v(p.devices * m, n, dtype=bf16) for m, n in sizes]
    scratch += [v(p.devices * m, n, dtype=bf16) for m, n in sizes]
    turned = [sizes[3], sizes[2], sizes[1], sizes[0]]
    scratch += [v(tiles, depth * m, n, dtype=bf16) for m, n in turned]
    scratch += [v(depth * m, n, dtype=bf16) for m, n in turned] * 2
    scratch += [v(depth * m, n // 2, dtype=bf16) for m, n in turned] * 2
    scratch += [v(depth - 1, m, n, dtype=bf16) for m, n in turned]
    halo_rows = p.images * 4 * p.keep
    scratch += [v(3, 2, halo_rows, feats, dtype=bf16)] * 2
    scratch += [v(3, halo_rows, feats, dtype=bf16)] * 4
    dma = pltpu.SemaphoreType.DMA
    scratch += [dma((5, 12 + depth))] * 2 + [dma((4, 7 + depth))] * 2
    scratch += [dma((9,))] * 2 + [dma((3, plane + depth))] * 2
    out_shape = [
        jax.ShapeDtypeStruct(images.shape, f32),
        jax.ShapeDtypeStruct(images.shape, f32),
    ]
    out_shape += [jax.ShapeDtypeStruct(w.shape, f32) for w in weights]
    out_shape += [jax.ShapeDtypeStruct((small_rows, wide), f32)]
    spec = pl.BlockSpec(memory_space=pltpu.VMEM)
    outs = pl.pallas_call(
        functools.partial(block_kernel, p),
        name="block",
        out_shape=out_shape,
        in_specs=[spec] * 17,
        out_specs=[spec] * 7,
        scratch_shapes=scratch,
        compiler_params=pltpu.CompilerParams(
            collective_id=2, has_side_effects=True, vmem_limit_bytes=60 * 1024 * 1024
        ),
    )(
        images,
        cotangent,
        rel_index,
        rel_table,
        *[vector.reshape(1, -1) for vector in vectors],
        *weights,
    )
    small = outs[6]
    me = lax.axis_index("rows") * depth + lax.axis_index("cols")
    size, size_up = vectors[0].shape[0], vectors[7].shape[0]
    count = 8 * feats // wide
    lines = small[:count].reshape(8, feats)
    mine = lax.dynamic_slice(lines, (0, me * size), (8, size))
    ups = small[count : count + hidden // wide].reshape(hidden)
    up_mine = lax.dynamic_slice(ups, (me * size_up,), (size_up,))
    count += hidden // wide
    table = small[count : count + p.heads, : p.table_size].T
    vector_outs = [mine[k] for k in range(7)] + [up_mine, mine[7]]
    return (outs[0], outs[1], *outs[2:6], *vector_outs, table)


def per_device(images, cotangent, rel_index, rel_table, *params):
    dims = sizes_here()
    weights, vectors = params[:4], params[4:]
    if fits_fused(dims, images, weights, vectors):
        return fused_block(dims, images, cotangent, rel_index, rel_table, weights, vectors)
    return plain_block(images, cotangent, rel_index, rel_table, *params)


def solution(mesh):
    in_specs = (
        P(None, "rows", "cols", None),
        P(None, "rows", "cols", None),
        P(),
        P(),
        P(("rows", "cols"), None),
        P(("rows", "cols"), None),
        P(("rows", "cols"), None),
        P(("rows", "cols"), None),
        P(("rows", "cols")),
        P(("rows", "cols")),
        P(("rows", "cols")),
        P(("rows", "cols")),
        P(("rows", "cols")),
        P(("rows", "cols")),
        P(("rows", "cols")),
        P(("rows", "cols")),
        P(("rows", "cols")),
    )
    out_specs = (
        P(None, "rows", "cols", None),
        P(None, "rows", "cols", None),
        P(("rows", "cols"), None),
        P(("rows", "cols"), None),
        P(("rows", "cols"), None),
        P(("rows", "cols"), None),
        P(("rows", "cols")),
        P(("rows", "cols")),
        P(("rows", "cols")),
        P(("rows", "cols")),
        P(("rows", "cols")),
        P(("rows", "cols")),
        P(("rows", "cols")),
        P(("rows", "cols")),
        P(("rows", "cols")),
        P(),
    )
    return jax.shard_map(
        per_device, mesh=mesh, in_specs=in_specs, out_specs=out_specs, check_vma=False
    )
```

```python
import functools

import jax
import jax.numpy as jnp
from jax import lax
from jax.experimental import pallas as pl
from jax.experimental.pallas import tpu as pltpu
from jax.sharding import PartitionSpec as P

WIN = 7
SHIFT = 3


norm_eps = 1e-05
root_half = 0.7071067811865476
tau_factor = 0.3989422804014327
big_negative = -1e30


def shifted(array, axis, by):
    length = lax.axis_size(axis)
    return lax.ppermute(array, axis, [(i, (i + by) % length) for i in range(length)])


def as_sent(array):

    def short(part):
        return part.astype(jnp.bfloat16) if part.dtype == jnp.float32 else part

    return jax.tree.map(short, array)


def layer_norm(values, gain_vec, offset):
    mean_val = jnp.mean(values, axis=-1, keepdims=True)
    centred = values - mean_val
    inv_std = lax.rsqrt(jnp.mean(centred * centred, axis=-1, keepdims=True) + norm_eps)
    normed = centred * inv_std
    return (normed * gain_vec + offset, normed, inv_std)


def norm_back(grad_out, normed, inv_std, gain_vec):
    scaled = grad_out * gain_vec
    row_inner = (
        scaled
        - jnp.mean(scaled, axis=-1, keepdims=True)
        - normed * jnp.mean(scaled * normed, axis=-1, keepdims=True)
    )
    return (inv_std * row_inner, jnp.sum(grad_out * normed, axis=0), jnp.sum(grad_out, axis=0))


def dot_plain(former, latter):
    return jnp.dot(former, latter, preferred_element_type=jnp.float32)


def dot_lead(former, latter):
    return lax.dot_general(
        former, latter, (((0,), (0,)), ((), ())), preferred_element_type=jnp.float32
    )


def dot_tail(former, latter):
    return lax.dot_general(
        former, latter, (((1,), (1,)), ((), ())), preferred_element_type=jnp.float32
    )


def band_of(positions, length):
    return (positions >= length - WIN).astype(jnp.int32) + (positions >= length - SHIFT).astype(
        jnp.int32
    )


def roll_in(images, cotangent):
    from_below = shifted((images[:, :SHIFT], cotangent[:, :SHIFT]), "rows", -1)
    tall_tokens = jnp.concatenate([images[:, SHIFT:], from_below[0]], axis=1)
    tall_grads = jnp.concatenate([cotangent[:, SHIFT:], from_below[1]], axis=1)
    beside = shifted((tall_tokens[:, :, :SHIFT], tall_grads[:, :, :SHIFT]), "cols", -1)
    return (
        jnp.concatenate([tall_tokens[:, :, SHIFT:], beside[0]], axis=2),
        jnp.concatenate([tall_grads[:, :, SHIFT:], beside[1]], axis=2),
    )


def roll_out(result, grad_tokens):
    from_above = (
        shifted(result[:, -SHIFT:].astype(jnp.bfloat16), "rows", 1).astype(jnp.float32),
        shifted(grad_tokens[:, -SHIFT:].astype(jnp.bfloat16), "rows", 1).astype(jnp.float32),
    )
    tall_result = jnp.concatenate([from_above[0], result[:, :-SHIFT]], axis=1)
    tall_grads = jnp.concatenate([from_above[1], grad_tokens[:, :-SHIFT]], axis=1)
    beside = (
        shifted(tall_result[:, :, -SHIFT:].astype(jnp.bfloat16), "cols", 1).astype(jnp.float32),
        shifted(as_sent(tall_grads[:, :, -SHIFT:]), "cols", 1),
    )
    return (
        jnp.concatenate([beside[0], tall_result[:, :, :-SHIFT]], axis=2),
        jnp.concatenate([beside[1], tall_grads[:, :, :-SHIFT]], axis=2),
    )


MESH = pl.DeviceIdType.MESH
CORES = 2


def grid_of(rows):
    chips = rows // CORES
    across = 1
    for size in range(1, chips + 1):
        if chips % size == 0 and size * size <= chips:
            across = size
    return chips // across, across


def whereabouts(dims):
    height, width = dims[0], dims[1]
    row, depth_at = lax.axis_index("rows"), lax.axis_index("cols")
    core = lax.rem(row, CORES)
    chip = row // CORES
    return chip // width, lax.rem(chip, width), core, depth_at


def device_at(dims, y, x, core, z):
    return ((y * dims[1] + x) * CORES + core, z)


def greet(dims, here):
    barrier = pltpu.get_barrier_semaphore()
    total = 0
    for axis in range(4):
        for step in range(1, dims[axis]):
            there = list(here)
            there[axis] = lax.rem(here[axis] + step, dims[axis])
            pl.semaphore_signal(
                barrier, inc=1, device_id=device_at(dims, *there), device_id_type=MESH
            )
            total += 1
    pl.semaphore_wait(barrier, total)


def moved(here, axis, step, dims):
    there = list(here)
    there[axis] = lax.rem(here[axis] + step, dims[axis])
    return there


def gather_kernel(dims, count, *refs):
    ins, outs = refs[:count], refs[count : 2 * count]
    local_sem, send_sem, recv_sem = refs[2 * count :]
    height, width, _, depth = dims
    here = whereabouts(dims)
    y, x, core, z = here
    greet(dims, here)
    used = [0] * count

    def send(stream, src, dst, there):
        slot = used[stream]
        used[stream] += 1
        copy = pltpu.make_async_remote_copy(
            src_ref=src,
            dst_ref=dst,
            send_sem=send_sem.at[stream, slot],
            recv_sem=recv_sem.at[stream, slot],
            device_id=device_at(dims, *there),
            device_id_type=MESH,
        )
        copy.start()
        return copy

    started = []
    along_z, locals_ = [], []
    for k in range(count):
        mine = pltpu.make_async_copy(ins[k], outs[k].at[y, x, core, z], local_sem.at[k])
        mine.start()
        locals_.append(mine)
        along_z.append(
            [
                send(k, ins[k], outs[k].at[y, x, core, z], moved(here, 3, step, dims))
                for step in range(1, depth)
            ]
        )
        started += along_z[k]
    first, second, partner = [], [], []
    other = moved(here, 2, 1, dims)
    for k in range(count):
        locals_[k].wait()
        for copy in along_z[k]:
            copy.wait_recv()
        axis = k % 2
        block = outs[k].at[y, x, core]
        first.append(
            [send(k, block, block, moved(here, axis, s, dims)) for s in range(1, dims[axis])]
        )
        partner.append([send(k, block, block, other)])
        started += first[k] + partner[k]
    for k in range(count):
        axis = k % 2
        cross = 1 - axis
        for copy in first[k]:
            copy.wait_recv()
        copies = []
        for lag in range(dims[axis]):
            at = moved(here, axis, lag, dims)
            block = outs[k].at[at[0], at[1], core]
            copies += [
                send(k, block, block, moved(here, cross, s, dims)) for s in range(1, dims[cross])
            ]
            if lag:
                partner[k].append(send(k, block, block, other))
                started.append(partner[k][-1])
        second.append(copies)
        started += copies
    for k in range(count):
        axis = k % 2
        cross = 1 - axis
        copies = iter(second[k])
        for lag in range(dims[axis]):
            for s in range(1, dims[cross]):
                next(copies).wait_recv()
                at = moved(here, axis, lag, dims)
                at[cross] = lax.rem(here[cross] + dims[cross] - s, dims[cross])
                block = outs[k].at[at[0], at[1], core]
                partner[k].append(send(k, block, block, other))
                started.append(partner[k][-1])
    for k in range(count):
        for copy in partner[k]:
            copy.wait_recv()
    for copy in started:
        copy.wait_send()


def reduce_kernel(dims, count, *refs):
    ins, table = refs[:count], refs[count]
    outs, table_out = refs[count + 1 : 2 * count + 1], refs[2 * count + 1]
    rest = refs[2 * count + 2 :]
    bufs = [rest[7 * k : 7 * k + 7] for k in range(count)]
    table_in = rest[7 * count : 7 * count + 4]
    table_sum = rest[7 * count + 4 : 7 * count + 7]
    send_sem, recv_sem = rest[7 * count + 7 :]
    height, width, _, depth = dims
    here = whereabouts(dims)
    y, x, core, z = here
    greet(dims, here)
    used = [0] * (count + 1)
    started = []

    def send(stream, src, dst, there):
        slot = used[stream]
        used[stream] += 1
        copy = pltpu.make_async_remote_copy(
            src_ref=src,
            dst_ref=dst,
            send_sem=send_sem.at[stream, slot],
            recv_sem=recv_sem.at[stream, slot],
            device_id=device_at(dims, *there),
            device_id_type=MESH,
        )
        copy.start()
        started.append(copy)
        return copy

    def add(dst, parts):
        def body(i, carry):
            total = parts[0][i].astype(jnp.float32)
            for part in parts[1:]:
                total = total + part[i].astype(jnp.float32)
            dst[i] = total.astype(dst.dtype)
            return carry

        lax.fori_loop(0, depth, body, 0)

    def table_step(stage, axis, src):
        table_in[stage][here[axis]] = src[...]
        return [
            send(count, src, table_in[stage].at[here[axis]], moved(here, axis, s, dims))
            for s in range(1, dims[axis])
        ]

    def table_add(stage, axis, copies, dst):
        for copy in copies:
            copy.wait_recv()
        total = table_in[stage][0]
        for j in range(1, dims[axis]):
            total = total + table_in[stage][j]
        dst[...] = total

    other = moved(here, 2, 1, dims)
    table_copies = table_step(0, 2, table)
    core_copies = []
    for k in range(count):
        axis = k % 2
        cross = 1 - axis
        group = {}
        for lag in list(range(1, dims[axis])) + [0]:
            for j in range(dims[cross]):
                at = moved(here, axis, lag, dims)
                at[cross] = j
                group[lag, j] = send(
                    k, ins[k].at[at[0], at[1], other[2]], bufs[k][0].at[at[0], at[1]], other
                )
        core_copies.append(group)
    table_add(0, 2, table_copies, table_sum[0])
    table_copies = table_step(1, 0, table_sum[0])
    first = []
    for k in range(count):
        axis = k % 2
        cross = 1 - axis
        from_core, sum_core, from_first = bufs[k][0], bufs[k][1], bufs[k][2]
        group = []
        for lag in list(range(1, dims[axis])) + [0]:
            for j in range(dims[cross]):
                at = moved(here, axis, lag, dims)
                at[cross] = j
                core_copies[k][lag, j].wait_recv()
                block = sum_core.at[at[0], at[1]]
                add(block, [ins[k].at[at[0], at[1], core], from_core.at[at[0], at[1]]])
                if lag:
                    group.append(
                        send(k, block, from_first.at[lag - 1, j], moved(here, axis, lag, dims))
                    )
        first.append(group)
    table_add(1, 0, table_copies, table_sum[1])
    table_copies = table_step(2, 1, table_sum[1])
    second = []
    for k in range(count):
        axis = k % 2
        cross = 1 - axis
        sum_core, from_first, sum_first, from_second = bufs[k][1:5]
        for copy in first[k]:
            copy.wait_recv()
        group = []
        for lag in list(range(1, dims[cross])) + [0]:
            at = moved(here, cross, lag, dims)
            j = at[cross]
            block = sum_first.at[j]
            add(
                block,
                [sum_core.at[at[0], at[1]]]
                + [from_first.at[s - 1, j] for s in range(1, dims[axis])],
            )
            if lag:
                group.append(send(k, block, from_second.at[lag - 1], at))
        second.append(group)
    table_add(2, 1, table_copies, table_sum[2])
    table_copies = table_step(3, 3, table_sum[2])
    third = []
    for k in range(count):
        axis = k % 2
        cross = 1 - axis
        sum_first, from_second, sum_second, from_third = bufs[k][3:7]
        for copy in second[k]:
            copy.wait_recv()
        add(
            sum_second,
            [sum_first.at[here[cross]]] + [from_second.at[s - 1] for s in range(1, dims[cross])],
        )
        group = []
        for step in range(1, depth):
            at = moved(here, 3, step, dims)
            group.append(send(k, sum_second.at[at[3]], from_third.at[step - 1], at))
        third.append(group)
    table_add(3, 3, table_copies, table_out)
    for k in range(count):
        sum_second, from_third = bufs[k][5:7]
        for copy in third[k]:
            copy.wait_recv()
        total = sum_second[z].astype(jnp.float32)
        for step in range(1, depth):
            total = total + from_third[step - 1].astype(jnp.float32)
        outs[k][...] = total
    for copy in started:
        copy.wait_send()


def sizes_here():
    rows, depth = lax.axis_size("rows"), lax.axis_size("cols")
    height, width = grid_of(rows)
    return height, width, CORES, depth


def blocked(rows, columns):
    if rows % 16 == 0:
        return rows, columns
    return rows * columns // 128, 128


def gather_all(shards):
    dims = sizes_here()
    height, width, cores, depth = dims
    count = len(shards)
    blocks = [blocked(*shard.shape) for shard in shards]
    slots = (depth - 1) + max(height, width) * 2 * height * width
    outs = pl.pallas_call(
        functools.partial(gather_kernel, dims, count),
        name="gather_all",
        out_shape=[
            jax.ShapeDtypeStruct(dims + block, shard.dtype)
            for block, shard in zip(blocks, shards)
        ],
        in_specs=[pl.BlockSpec(memory_space=pltpu.VMEM)] * count,
        out_specs=[pl.BlockSpec(memory_space=pl.ANY)] * count,
        scratch_shapes=[
            pltpu.SemaphoreType.DMA((count,)),
            pltpu.SemaphoreType.DMA((count, slots)),
            pltpu.SemaphoreType.DMA((count, slots)),
        ],
        compiler_params=pltpu.CompilerParams(collective_id=0, has_side_effects=True),
    )(*[shard.reshape(block) for block, shard in zip(blocks, shards)])
    total = height * width * cores * depth
    return [
        out.reshape(total * shard.shape[0], shard.shape[1]) for out, shard in zip(outs, shards)
    ]


def reduce_all(wholes, table):
    dims = sizes_here()
    height, width, cores, depth = dims
    total = height * width * cores * depth
    count = len(wholes)
    shares = [(whole.shape[0] // total, whole.shape[1]) for whole in wholes]
    blocks = [blocked(*share) for share in shares]
    scratch = []
    for k, (block, whole) in enumerate(zip(blocks, wholes)):
        along, cross = dims[k % 2], dims[1 - k % 2]
        for lead in (
            (height, width, depth),
            (height, width, depth),
            (max(along - 1, 1), cross, depth),
            (cross, depth),
            (max(cross - 1, 1), depth),
            (depth,),
            (max(depth - 1, 1),),
        ):
            scratch.append(pltpu.VMEM(lead + block, whole.dtype))
    for size in (cores, height, width, depth):
        scratch.append(pltpu.VMEM((size,) + table.shape, table.dtype))
    scratch += [pltpu.VMEM(table.shape, table.dtype)] * 3
    slots = 2 * height * width + height + width + depth
    scratch += [pltpu.SemaphoreType.DMA((count + 1, slots))] * 2
    outs = pl.pallas_call(
        functools.partial(reduce_kernel, dims, count),
        name="reduce_all",
        out_shape=[jax.ShapeDtypeStruct(block, jnp.float32) for block in blocks]
        + [jax.ShapeDtypeStruct(table.shape, table.dtype)],
        in_specs=[pl.BlockSpec(memory_space=pltpu.VMEM)] * (count + 1),
        out_specs=[pl.BlockSpec(memory_space=pltpu.VMEM)] * (count + 1),
        scratch_shapes=scratch,
        compiler_params=pltpu.CompilerParams(collective_id=1, has_side_effects=True),
    )(*[whole.reshape(dims + block) for block, whole in zip(blocks, wholes)], table)
    return [out.reshape(share) for out, share in zip(outs, shares)], outs[-1]


def padded(values, multiple):
    size = values.shape[-1]
    extra = -size % multiple
    return jnp.pad(values, [(0, 0)] * (values.ndim - 1) + [(0, extra)])


def plain_block(
    images,
    cotangent,
    rel_index,
    rel_table,
    qkv_weight,
    proj_weight,
    up_weight,
    down_weight,
    norm1_gain,
    norm1_bias,
    query_bias,
    value_bias,
    proj_bias,
    norm2_gain,
    norm2_bias,
    up_bias,
    down_bias,
):
    shards = (
        norm1_gain,
        norm1_bias,
        query_bias,
        value_bias,
        proj_bias,
        norm2_gain,
        norm2_bias,
        up_bias,
        down_bias,
    )
    vector_shard = padded(jnp.concatenate(shards)[None], 2048).reshape(-1, 128)
    qkv_full, down_full, up_full, proj_full, vector_full = gather_all(
        [qkv_weight, down_weight, up_weight, proj_weight, vector_shard]
    )
    device_count = lax.axis_size("rows") * lax.axis_size("cols")
    vector_full = vector_full.reshape(device_count, -1)
    vectors, offset = [], 0
    for shard in shards:
        size = shard.shape[0]
        vectors.append(vector_full[:, offset : offset + size].reshape(device_count * size))
        offset += size
    (
        gain_one_full,
        bias_one_full,
        query_add,
        value_add,
        proj_add,
        gain_two_full,
        bias_two_full,
        up_add,
        down_add,
    ) = vectors
    tokens_tile, grad_tile = roll_in(images, cotangent)
    image_count, tile_side, features = (
        tokens_tile.shape[0],
        tokens_tile.shape[1],
        tokens_tile.shape[3],
    )
    window = tile_side * tile_side
    row_total = image_count * window
    tokens = tokens_tile.reshape(row_total, features)
    grad_rows = grad_tile.reshape(row_total, features)
    local_pos = jnp.arange(tile_side, dtype=jnp.int32)
    band_rows = band_of(
        lax.axis_index("rows") * tile_side + local_pos, lax.axis_size("rows") * tile_side
    )
    band_cols = band_of(
        lax.axis_index("cols") * tile_side + local_pos, lax.axis_size("cols") * tile_side
    )
    region = (3 * band_rows[:, None] + band_cols[None, :]).reshape(window)
    allowed = (region[:, None] == region[None, :])[None, None]
    head_count = rel_table.shape[1]
    table_size = rel_table.shape[0]
    head_width = features // head_count
    score_scale = head_width ** (-0.5)
    onehot = (
        rel_index.reshape(window * window)[:, None]
        == jnp.arange(table_size, dtype=jnp.int32)[None, :]
    ).astype(jnp.float32)
    bias_flat = jnp.dot(
        onehot, rel_table, precision=lax.Precision.HIGHEST, preferred_element_type=jnp.float32
    )
    bias_heads = bias_flat.T.reshape(head_count, window, window)

    def split_heads(values):
        return values.reshape(image_count, window, head_count, head_width)

    def scores_of(query_b, key_b):
        raw_scores = jnp.einsum(
            "wqhd,wkhd->whqk",
            split_heads(query_b),
            split_heads(key_b),
            preferred_element_type=jnp.float32,
        )
        return jnp.where(allowed, raw_scores + bias_heads[None], big_negative)

    gain_one = gain_one_full.astype(jnp.float32)
    gain_two = gain_two_full.astype(jnp.float32)
    out_one, normed_one, inv_one = layer_norm(tokens, gain_one, bias_one_full.astype(jnp.float32))
    h_one = out_one.astype(jnp.bfloat16)
    projected = dot_plain(h_one, qkv_full)
    query_b = ((projected[:, :features] + query_add.astype(jnp.float32)) * score_scale).astype(
        jnp.bfloat16
    )
    key_b = projected[:, features : 2 * features].astype(jnp.bfloat16)
    value_b = (projected[:, 2 * features :] + value_add.astype(jnp.float32)).astype(jnp.bfloat16)
    scores = scores_of(query_b, key_b)
    row_top = jnp.max(scores, axis=-1, keepdims=True)
    log_total = row_top + jnp.log(jnp.sum(jnp.exp(scores - row_top), axis=-1, keepdims=True))
    attend_b = jnp.exp(scores - log_total).astype(jnp.bfloat16)
    attn_b = (
        jnp.einsum(
            "whqk,wkhd->wqhd", attend_b, split_heads(value_b), preferred_element_type=jnp.float32
        )
        .reshape(row_total, features)
        .astype(jnp.bfloat16)
    )
    residual = tokens + dot_plain(attn_b, proj_full) + proj_add.astype(jnp.float32)
    out_two, normed_two, inv_two = layer_norm(residual, gain_two, bias_two_full.astype(jnp.float32))
    h_two = out_two.astype(jnp.bfloat16)
    hidden_pre = dot_plain(h_two, up_full) + up_add.astype(jnp.float32)
    gauss_cdf = 0.5 * (1.0 + lax.erf(hidden_pre * root_half))
    act_b = (hidden_pre * gauss_cdf).astype(jnp.bfloat16)
    result = residual + dot_plain(act_b, down_full) + down_add.astype(jnp.float32)
    grad_b = grad_rows.astype(jnp.bfloat16)
    grad_down = dot_lead(act_b, grad_b)
    grad_down_add = jnp.sum(grad_rows, axis=0)
    grad_act = dot_tail(grad_b, down_full)
    density = jnp.exp(-0.5 * hidden_pre * hidden_pre) * tau_factor
    grad_pre = grad_act * (gauss_cdf + hidden_pre * density)
    grad_pre_b = grad_pre.astype(jnp.bfloat16)
    grad_up = dot_lead(h_two, grad_pre_b)
    grad_up_add = jnp.sum(grad_pre, axis=0)
    grad_h_two = dot_tail(grad_pre_b, up_full)
    grad_resid, grad_gain_two, grad_bias_two = norm_back(
        grad_h_two, normed_two, inv_two, gain_two
    )
    grad_resid = grad_resid + grad_rows
    grad_resid_b = grad_resid.astype(jnp.bfloat16)
    grad_proj = dot_lead(attn_b, grad_resid_b)
    grad_proj_add = jnp.sum(grad_resid, axis=0)
    grad_attn_b = dot_tail(grad_resid_b, proj_full).astype(jnp.bfloat16)
    grad_heads = split_heads(grad_attn_b)
    grad_attend = jnp.einsum(
        "wqhd,wkhd->whqk", grad_heads, split_heads(value_b), preferred_element_type=jnp.float32
    )
    attend = jnp.exp(scores_of(query_b, key_b) - log_total)
    grad_value = jnp.einsum(
        "whqk,wqhd->wkhd",
        attend.astype(jnp.bfloat16),
        grad_heads,
        preferred_element_type=jnp.float32,
    ).reshape(row_total, features)
    row_inner = jnp.sum(attend * grad_attend, axis=-1, keepdims=True)
    grad_scores = attend * (grad_attend - row_inner)
    grad_bias_heads = jnp.sum(grad_scores, axis=0).reshape(head_count, window * window)
    table_local = lax.dot_general(
        onehot,
        grad_bias_heads,
        (((0,), (1,)), ((), ())),
        precision=lax.Precision.HIGHEST,
        preferred_element_type=jnp.float32,
    )
    grad_scores_b = grad_scores.astype(jnp.bfloat16)
    grad_query = (
        jnp.einsum(
            "whqk,wkhd->wqhd", grad_scores_b, split_heads(key_b), preferred_element_type=jnp.float32
        )
        * score_scale
    ).reshape(row_total, features)
    grad_key = jnp.einsum(
        "whqk,wqhd->wkhd", grad_scores_b, split_heads(query_b), preferred_element_type=jnp.float32
    ).reshape(row_total, features)
    grad_query_add = jnp.sum(grad_query, axis=0)
    grad_value_add = jnp.sum(grad_value, axis=0)
    grad_mixed_b = jnp.concatenate([grad_query, grad_key, grad_value], axis=1).astype(jnp.bfloat16)
    grad_qkv = dot_lead(h_one, grad_mixed_b)
    grad_h_one = dot_tail(grad_mixed_b, qkv_full)
    grad_in, grad_gain_one, grad_bias_one = norm_back(
        grad_h_one, normed_one, inv_one, gain_one
    )
    grad_tokens = grad_resid + grad_in
    vector_grads = (
        grad_gain_one,
        grad_bias_one,
        grad_query_add,
        grad_value_add,
        grad_proj_add,
        grad_gain_two,
        grad_bias_two,
        grad_up_add,
        grad_down_add,
    )
    vector_rows = padded(
        jnp.concatenate([grad.reshape(device_count, -1) for grad in vector_grads], axis=1), 2048
    ).reshape(-1, 128)
    table_rows = padded(table_local.reshape(1, -1), 1024).reshape(-1, 128)
    (down_sum, up_sum, qkv_sum, proj_sum, vector_sum), table_sum = reduce_all(
        [
            grad_down.astype(jnp.bfloat16),
            grad_up.astype(jnp.bfloat16),
            grad_qkv.astype(jnp.bfloat16),
            grad_proj.astype(jnp.bfloat16),
            vector_rows,
        ],
        table_rows,
    )
    grad_table = table_sum.reshape(-1)[: table_local.size].reshape(table_local.shape)
    vector_sum = vector_sum.reshape(-1)
    vector_sums, offset = [], 0
    for shard in shards:
        size = shard.shape[0]
        vector_sums.append(vector_sum[offset : offset + size])
        offset += size
    shard_grads = (qkv_sum, proj_sum, up_sum, down_sum, *vector_sums)
    block_out, grad_images = roll_out(
        result.reshape(image_count, tile_side, tile_side, features),
        grad_tokens.reshape(image_count, tile_side, tile_side, features),
    )
    return (
        block_out,
        grad_images,
        shard_grads[0],
        shard_grads[1],
        shard_grads[2],
        shard_grads[3],
        shard_grads[4],
        shard_grads[5],
        shard_grads[6],
        shard_grads[7],
        shard_grads[8],
        shard_grads[9],
        shard_grads[10],
        shard_grads[11],
        shard_grads[12],
        grad_table,
    )


LANES = 128
HALF = 64


def dot_nt(former, latter):
    return lax.dot_general(
        former, latter, (((1,), (1,)), ((), ())), preferred_element_type=jnp.float32
    )


def dot_tn(former, latter):
    return lax.dot_general(
        former, latter, (((0,), (0,)), ((), ())), preferred_element_type=jnp.float32
    )


def iota(shape, dim):
    return lax.broadcasted_iota(jnp.int32, shape, dim)


def aligned(value, multiple):
    return pl.multiple_of(value, multiple)


class Plan:
    def __init__(self, dims, images, rel_table, weights, vectors):
        self.dims = dims
        self.depth = dims[3]
        self.side, _, self.images, self.features = images.shape
        self.keep = self.side - SHIFT
        self.pitch = self.side + 1
        self.span = self.side * self.pitch
        self.rows = self.images * self.span
        self.heads, self.table_size = rel_table.shape
        self.head_width = self.features // self.heads
        self.group_heads = LANES // self.head_width
        self.groups = self.features // LANES
        self.lanes = self.group_heads * self.span
        self.table_rows = -(-self.table_size // 16) * 16
        self.shard_rows = [w.shape[0] for w in weights]
        self.widths = [w.shape[1] for w in weights]
        self.devices = dims[0] * dims[1] * dims[2] * dims[3]
        self.hidden = weights[2].shape[1]
        self.stack = 4
        self.cuts = (1, 1, 2, 2)
        self.vector_sizes = [v.shape[0] for v in vectors]


def fits_fused(dims, images, weights, vectors):
    return (
        dims[0] == 2
        and dims[1] == 2
        and dims[2] == 2
        and dims[3] > 1
        and all(w.shape[0] % 16 == 0 for w in weights)
        and images.shape[1] == WIN
        and images.shape[2] == WIN
    )


def block_kernel(plan, *refs):
    p = plan
    take = iter(refs)

    def pull(count):
        return [next(take) for _ in range(count)]

    held = pull(13)
    shards = pull(4)
    out_y, out_g = pull(2)
    out_w = pull(4)
    (small_out,) = pull(1)
    (
        vec_shard,
        vec_full,
        vec,
        up_vec,
        xs,
        gs,
        normed,
        inv,
        h_b,
        qkv,
        probs,
        attn,
        attn_b,
        x1,
        normed2,
        inv2,
        h2_b,
        gy_b,
        act_b,
        dpre_b,
        ys,
        dh2,
        dx1,
        dx1_b,
        dattn,
        dqkv,
        dqkv_b,
        dh1,
        work,
        square,
        flipped,
        flipped_pad,
        index_t,
        index_q,
        tab,
        tab_b,
        onehot,
        bias_cube,
        bias,
        dbias,
        dcube,
        dtab,
        sums,
        sums_up,
        small,
        small_in,
        small_mid,
        small_z,
    ) = pull(48)
    full = pull(4)
    grads = pull(4)
    core_in = pull(4)
    x_in, y_in, a_in, b_in, z_in = pull(4), pull(4), pull(4), pull(4), pull(4)
    halo_in_src, halo_in_dst, halo_y_src, halo_y_dst, halo_g_src, halo_g_dst = pull(6)
    g_send, g_recv, r_send, r_recv, h_send, h_recv, s_send, s_recv = pull(8)
    local_sem = next(take)
    staged = pull(13)
    images, cotangent, rel_index, rel_table = staged[:4]
    vector_ins = staged[4:]

    dims, depth = p.dims, p.depth
    rows_total = lax.axis_size("rows")
    row, z = lax.axis_index("rows"), lax.axis_index("cols")
    here = whereabouts(dims)
    y, x, core = here[0], here[1], here[2]
    me = row * depth + z
    partner_at = (y * dims[1] + x) * CORES + (1 - core)
    x_at = (y * dims[1] + (1 - x)) * CORES + core
    y_at = ((1 - y) * dims[1] + x) * CORES + core
    chip_own = y * dims[1] + x
    chip_x = y * dims[1] + (1 - x)
    chip_y = (1 - y) * dims[1] + x
    chip_d = (1 - y) * dims[1] + (1 - x)
    row_up, row_down = lax.rem(row + rows_total - 1, rows_total), lax.rem(row + 1, rows_total)
    col_up, col_down = lax.rem(z + depth - 1, depth), lax.rem(z + 1, depth)
    started = []

    def remote(src, dst, send_sem, recv_sem, device):
        return pltpu.make_async_remote_copy(
            src_ref=src,
            dst_ref=dst,
            send_sem=send_sem,
            recv_sem=recv_sem,
            device_id=device,
            device_id_type=MESH,
        )

    def launch(*args):
        copy = remote(*args)
        copy.start()
        started.append(copy)
        return copy

    loads = [
        pltpu.make_async_copy(src, dst, local_sem.at[n])
        for n, (src, dst) in enumerate(zip(held, staged))
    ]
    for k in range(4):
        size = p.shard_rows[k]
        mine = full[k].at[pl.ds(aligned(me * size, 16), size)]
        loads.append(pltpu.make_async_copy(shards[k], mine, local_sem.at[13 + k]))
    for copy in loads:
        copy.start()

    barrier = pltpu.get_barrier_semaphore()
    peers = [(lax.rem(row + s, rows_total), z) for s in range(1, rows_total)]
    peers += [(row, lax.rem(z + s, depth)) for s in range(1, depth)]
    peers += [(row_up, col_up), (row_down, col_down)]
    for peer in peers:
        pl.semaphore_signal(barrier, inc=1, device_id=peer, device_id_type=MESH)

    span, pitch, keep, side = p.span, p.pitch, p.keep, p.side
    halo_rows = 4 * keep

    def pack(read, dst, slot_of):
        for piece, (row_list, col_at, cols) in enumerate(slot_of):

            def body(b, carry):
                parts = [read(b, i, col_at) for i in row_list]
                parts += [jnp.zeros_like(parts[0])] * (4 - len(parts))
                value = jnp.concatenate(parts, axis=0)
                if cols < keep:
                    value = jnp.where(lax.rem(iota(value.shape, 0), keep) < cols, value, 0.0)
                dst(piece, b)[...] = value.astype(jnp.bfloat16)
                return carry

            lax.fori_loop(0, p.images, body, 0)

    for copy in loads:
        copy.wait()
    head, rest = list(range(SHIFT)), list(range(SHIFT, side))
    pieces_in = [(head, SHIFT, keep), (rest, 0, SHIFT), (head, 0, SHIFT)]
    for n, source in enumerate((images, cotangent)):
        pack(
            lambda b, i, c, source=source: source[i, pl.ds(c, keep), b, :],
            lambda piece, b, n=n: halo_in_src.at[
                piece, n, pl.ds(aligned(b * halo_rows, 16), halo_rows)
            ],
            pieces_in,
        )

    vec_shard[...] = jnp.zeros_like(vec_shard)
    for k, ref in enumerate(vector_ins):
        vec_shard[k : k + 1, : p.vector_sizes[k]] = ref[...].astype(jnp.float32)
    vec_b = vec_full.at[pl.ds(aligned(me * 16, 16), 16)]
    vec_b[...] = vec_shard[...].astype(jnp.bfloat16)

    streams = [(vec_full, 16, 0, LANES)]
    for k, cuts in enumerate(p.cuts):
        width = p.widths[k] // cuts
        streams += [(full[k], p.shard_rows[k], t * width, width) for t in range(cuts)]
    pl.semaphore_wait(barrier, len(peers))

    halo_in = []
    for piece, device in enumerate(((row_up, z), (row, col_up), (row_up, col_up))):
        halo_in.append(
            launch(
                halo_in_src.at[piece], halo_in_dst.at[piece], h_send.at[piece], h_recv.at[piece],
                device,
            )
        )

    along_z = {}
    hops = {}

    def g_copy(k, slot, src, device):
        copy = launch(src, src, g_send.at[k, slot], g_recv.at[k, slot], device)
        hops[k, slot] = copy

    def block_of(k, row_at):
        ref, size, left, width = streams[k]
        rows_at = pl.ds(aligned(row_at * depth * size, 16), depth * size)
        return ref.at[rows_at, pl.ds(left, width)]

    def chip_row(chip):
        return chip * CORES + core

    def half_of(k, row_at, which):
        ref, size, left, width = streams[k]
        rows_at = pl.ds(aligned(row_at * depth * size, 16), depth * size)
        if width == LANES:
            return ref.at[rows_at, pl.ds(left, width)]
        middle = width // 2
        return ref.at[rows_at, pl.ds(left + which * middle, middle)]

    def gather_z(k):
        ref, size, left, width = streams[k]
        mine = ref.at[pl.ds(aligned(me * size, 16), size), pl.ds(left, width)]
        for s in range(1, depth):
            g_copy(k, 12 + s, mine, (row, lax.rem(z + s, depth)))

    def gather_one(k):
        for s in range(1, depth):
            hops[k, 12 + s].wait_recv()
        block = block_of(k, row)
        g_copy(k, 0, block, (x_at, z))
        g_copy(k, 1, block, (y_at, z))
        g_copy(k, 4, block, (partner_at, z))

    def gather_two(k):
        single = streams[k][3] == LANES
        row_x, row_y = chip_row(chip_x), chip_row(chip_y)
        hops[k, 0].wait_recv()
        g_copy(k, 2, half_of(k, row_x, 0), (y_at, z))
        g_copy(k, 5, block_of(k, row_x), (partner_at, z))
        hops[k, 1].wait_recv()
        if not single:
            g_copy(k, 3, half_of(k, row_y, 1), (x_at, z))
        g_copy(k, 6, block_of(k, row_y), (partner_at, z))

    def gather_three(k):
        single = streams[k][3] == LANES
        row_d = chip_row(chip_d)
        hops[k, 2].wait_recv()
        g_copy(k, 7, half_of(k, row_d, 0), (partner_at, z))
        if not single:
            hops[k, 3].wait_recv()
            g_copy(k, 8, half_of(k, row_d, 1), (partner_at, z))

    def gather_end(k):
        for slot in (4, 5, 6, 7, 8):
            if (k, slot) in hops:
                hops[k, slot].wait_recv()

    VEC, QKV, PROJ, UP0, UP1, DOWN0, DOWN1 = range(7)
    for k in range(7):
        gather_z(k)

    window = side * side
    square[...] = jnp.full(square.shape, -1.0, jnp.float32)
    raw_index = rel_index[...].astype(jnp.float32)
    for i in range(side):
        square[i * pitch : i * pitch + side, :window] = raw_index[i * side : (i + 1) * side]
    flipped[...] = square[...].T
    index_t[...] = jnp.full(index_t.shape, -1.0, jnp.float32)
    for i in range(side):
        index_t[i * pitch : i * pitch + side, :] = flipped[i * side : (i + 1) * side, :]
    for t in range(p.stack):
        index_q[:, t * HALF : (t + 1) * HALF] = index_t[
            pl.ds(t, span // p.stack, stride=p.stack), :HALF
        ]
    tab[...] = jnp.zeros_like(tab)
    tab[: p.heads, : p.table_size] = rel_table[...]
    tab_high = tab[...].astype(jnp.bfloat16).astype(jnp.float32)
    tab_b[...] = jnp.concatenate([tab_high, tab[...] - tab_high], axis=0).astype(jnp.bfloat16)

    def bias_step(q, carry):
        wanted = index_q[pl.ds(q, 1), :]
        places = iota((p.table_rows, p.stack * HALF), 0).astype(jnp.float32)
        hot = (places == wanted).astype(jnp.float32).astype(jnp.bfloat16)
        onehot[q] = hot
        entry = dot_plain(tab_b[...], hot)
        entry = entry[: p.heads] + entry[p.heads :]
        for t in range(p.stack):
            bias_cube[:, q * p.stack + t, :HALF] = entry[:, t * HALF : (t + 1) * HALF]
        return carry

    def bias_part(first, last):
        lax.fori_loop(first, last, bias_step, 0)

    def band(local, tile, axis):
        length = lax.axis_size(axis) * side
        at = tile * side + local
        return jnp.where(at >= length - WIN, 1, 0) + jnp.where(at >= length - SHIFT, 1, 0)

    def region_of(token):
        return 3 * band(token // pitch, row, "rows") + band(lax.rem(token, pitch), z, "cols")

    key_token = iota((span, p.lanes), 0)
    query_token = lax.rem(iota((span, p.lanes), 1), span)
    allowed = (region_of(key_token) == region_of(query_token)) & (
        lax.rem(key_token, pitch) < side
    )
    def bias_end():
        for g in range(p.groups):
            parts = [bias_cube[g * p.group_heads + h][:, :span] for h in range(p.group_heads)]
            bias[g] = jnp.where(allowed, jnp.concatenate(parts, axis=1), big_negative)

    gather_one(VEC)
    gather_one(QKV)

    def arrive(b, carry):
        for n, (source, dst) in enumerate(((images, xs), (cotangent, gs))):
            at = pl.ds(aligned(b * halo_rows, 16), halo_rows)
            by_row = halo_in_dst[0, n, at].astype(jnp.float32)
            by_col = halo_in_dst[1, n, at].astype(jnp.float32)
            by_both = halo_in_dst[2, n, at].astype(jnp.float32)
            for i in range(side):
                if i < keep:
                    left = source[i + SHIFT, SHIFT:side, b, :]
                    right = by_col[keep * i : keep * i + keep]
                else:
                    left = by_row[keep * (i - keep) : keep * (i - keep) + keep]
                    right = by_both[keep * (i - keep) : keep * (i - keep) + keep]
                dst[pl.ds(aligned(b * span + i * pitch, 8), pitch), :] = jnp.concatenate(
                    [left, right], axis=0
                )
        return carry

    def spans(body, count=None):
        lax.fori_loop(0, p.images if count is None else count, body, 0)

    def span_at(w):
        return pl.ds(aligned(w * span, 8), span)

    for copy in halo_in:
        copy.wait_recv()
    spans(arrive)
    gy_b[...] = gs[...].astype(jnp.bfloat16)

    def center(ref, dst, inv_ref):
        def body(w, carry):
            value = ref[span_at(w), :]
            mean_val = jnp.mean(value, axis=-1, keepdims=True)
            centred = value - mean_val
            inv_std = lax.rsqrt(
                jnp.mean(centred * centred, axis=-1, keepdims=True) + norm_eps
            )
            dst[span_at(w), :] = centred * inv_std
            inv_ref[span_at(w), :] = jnp.broadcast_to(inv_std, (span, LANES))
            return carry

        spans(body)

    center(xs, normed, inv)
    gather_one(PROJ)
    gather_two(VEC)
    gather_two(QKV)
    gather_one(UP0)
    gather_two(PROJ)
    gather_three(VEC)
    gather_three(QKV)
    gather_one(UP1)
    bias_part(0, span // p.stack)
    bias_end()
    gather_two(UP0)
    gather_end(VEC)

    size = p.vector_sizes[0]
    per = LANES // size
    for t in range(p.features // LANES):
        spread = (lax.rem(iota((LANES, LANES), 1), size) == iota((LANES, LANES), 0)).astype(
            jnp.float32
        ).astype(jnp.bfloat16)
        value = dot_plain(vec_full[t * per * 16 : (t + 1) * per * 16, :], spread)
        mine = iota(value.shape, 0) // 16 == iota(value.shape, 1) // size
        value = jnp.where(mine, value, 0.0)
        total = value[0:16]
        for d in range(1, per):
            total = total + value[d * 16 : (d + 1) * 16]
        vec[:, t * LANES : (t + 1) * LANES] = total
    size_up = p.vector_sizes[7]
    per_up = LANES // size_up
    for t in range(p.hidden // LANES):
        spread = (lax.rem(iota((LANES, LANES), 1), size_up) == iota((LANES, LANES), 0)).astype(
            jnp.float32
        ).astype(jnp.bfloat16)
        value = dot_plain(vec_full[t * per_up * 16 : (t + 1) * per_up * 16, :], spread)
        mine = iota(value.shape, 0) == 16 * (iota(value.shape, 1) // size_up) + 7
        value = jnp.where(mine, value, 0.0)
        up_vec[:, t * LANES : (t + 1) * LANES] = jnp.sum(value, axis=0, keepdims=True)

    def vector(k):
        return vec[k : k + 1, :]

    h_b[...] = (normed[...] * vector(0) + vector(1)).astype(jnp.bfloat16)
    gather_end(QKV)

    scale = p.head_width ** (-0.5)
    features = p.features
    for n in range(3):
        cols = slice(n * features, (n + 1) * features)
        value = dot_plain(h_b[...], full[0][:, cols])
        if n == 0:
            value = (value + vector(2)) * scale
        if n == 2:
            value = value + vector(3)
        qkv[:, cols] = value
    gather_three(PROJ)
    gather_one(DOWN0)
    gather_two(UP1)
    gather_three(UP0)

    def expand(value):
        lane = iota(value.shape, 1) // p.head_width
        parts = [jnp.where(lane == h, value, 0.0) for h in range(p.group_heads)]
        return jnp.concatenate(parts, axis=0).astype(jnp.bfloat16)

    def fold(value):
        total = None
        for h in range(p.group_heads):
            part = value[h * span : (h + 1) * span]
            part = jnp.where(iota(part.shape, 1) // p.head_width == h, part, 0.0)
            total = part if total is None else total + part
        return total

    def lanes_at(g, third=0):
        return pl.ds(aligned(third * features + g * LANES, LANES), LANES)

    def attend(w):
        def body(g, carry):
            at = span_at(w)
            query = qkv[at, lanes_at(g, 0)]
            key = qkv[at, lanes_at(g, 1)].astype(jnp.bfloat16)
            value = qkv[at, lanes_at(g, 2)].astype(jnp.bfloat16)
            scores = dot_nt(key, expand(query)) + bias[g]
            top = jnp.max(scores, axis=0, keepdims=True)
            weight = jnp.exp(scores - top)
            prob = weight / jnp.sum(weight, axis=0, keepdims=True)
            probs[w * p.groups + g] = prob
            attn[at, lanes_at(g)] = fold(dot_tn(prob.astype(jnp.bfloat16), value))
            return carry

        lax.fori_loop(0, p.groups, body, 0)

    steps = {
        0: [lambda: gather_one(DOWN1), lambda: gather_two(DOWN0), lambda: gather_three(UP1)],
        1: [lambda: gather_two(DOWN1), lambda: gather_end(PROJ)],
        2: [lambda: gather_three(DOWN0)],
    }
    for w in range(p.images):
        attend(w)
        for step in steps.get(w, []):
            step()
    attn_b[...] = attn[...].astype(jnp.bfloat16)
    x1[...] = xs[...] + dot_plain(attn_b[...], full[1][...]) + vector(4)
    center(x1, normed2, inv2)
    h2_b[...] = (normed2[...] * vector(5) + vector(6)).astype(jnp.bfloat16)
    gather_three(DOWN1)
    for k in (UP0, UP1, DOWN0, DOWN1):
        gather_end(k)

    ys[...] = x1[...] + vector(8)
    dh2[...] = jnp.zeros_like(dh2)
    tiles = dims[0] * dims[1]
    tile = p.hidden // tiles
    DN, UPW, PR, QK = 0, 1, 2, 3
    order = [3, 2, 1, 0]
    red = {
        DN: (grads[3], p.shard_rows[3], p.widths[3]),
        UPW: (grads[2], p.shard_rows[2], p.widths[2]),
        PR: (grads[1], p.shard_rows[1], p.widths[1]),
        QK: (grads[0], p.shard_rows[0], p.widths[0]),
    }
    sums[...] = jnp.zeros_like(sums)

    def core_copy(k, chip):
        ref, size, _ = red[k]
        at = (chip * CORES + (1 - core)) * depth * size
        return remote(
            ref.at[pl.ds(aligned(at, 16), depth * size)],
            core_in[k].at[chip],
            r_send.at[k, chip],
            r_recv.at[k, chip],
            (partner_at, z),
        )

    def feed(j, carry):
        at = pl.ds(aligned(j * tile, LANES), tile)
        pre = dot_plain(h2_b[...], full[2][:, at]) + up_vec[:, at]
        cdf = 0.5 * (1.0 + lax.erf(pre * root_half))
        act = (pre * cdf).astype(jnp.bfloat16)
        slope = cdf + pre * (jnp.exp(-0.5 * pre * pre) * tau_factor)
        down_rows = full[3][at, :]
        ys[...] += dot_plain(act, down_rows)
        dpre = dot_nt(gy_b[...], down_rows) * slope
        sums_up[:, at] = jnp.sum(dpre, axis=0, keepdims=True)
        dpre_low = dpre.astype(jnp.bfloat16)
        dh2[...] += dot_nt(dpre_low, full[2][:, at])
        grads[3][at, :] = dot_tn(act, gy_b[...]).astype(jnp.bfloat16)
        grads[2][:, at] = dot_tn(h2_b[...], dpre_low).astype(jnp.bfloat16)
        core_copy(DN, j).start()
        return carry

    lax.fori_loop(0, tiles, feed, 0)
    for chip in range(tiles):
        core_copy(UPW, chip).start()

    r_hops = {}

    def r_copy(k, slot, src, dst, device):
        r_hops[k, slot] = launch(src, dst, r_send.at[k, slot], r_recv.at[k, slot], device)

    def add_into(dst, parts, width_at, width):
        count = dst.shape[0]
        step = 16 if count % 32 else 32

        def body(i, carry):
            at = pl.ds(aligned(i * step, 16), step)
            cols = pl.ds(width_at, width)
            total = dst[at, cols].astype(jnp.float32)
            for part in parts:
                total = total + part[at, :].astype(jnp.float32)
            dst[at, cols] = total.astype(jnp.bfloat16)
            return carry

        lax.fori_loop(0, count // step, body, 0)

    def reduce_core(k):
        ref, size, width = red[k]
        middle = width // 2
        for chip in range(tiles):
            core_copy(k, chip).wait_recv()
        for chip in range(tiles):
            at = (chip * CORES + core) * depth * size
            add_into(
                core_in[k].at[chip],
                [ref.at[pl.ds(aligned(at, 16), depth * size)]],
                0,
                width,
            )
        corner = core_in[k].at[chip_d]
        r_copy(k, 4, corner.at[:, pl.ds(0, middle)], a_in[k], (y_at, z))
        r_copy(k, 5, corner.at[:, pl.ds(middle, middle)], b_in[k], (x_at, z))

    def reduce_cross(k):
        middle = red[k][2] // 2
        to_x, to_y = core_in[k].at[chip_x], core_in[k].at[chip_y]
        r_hops[k, 4].wait_recv()
        add_into(to_x, [a_in[k]], 0, middle)
        r_copy(k, 6, to_x, x_in[k], (x_at, z))
        r_hops[k, 5].wait_recv()
        add_into(to_y, [b_in[k]], middle, middle)
        r_copy(k, 7, to_y, y_in[k], (y_at, z))

    def reduce_chip(k):
        _, size, width = red[k]
        own = core_in[k].at[chip_own]
        r_hops[k, 6].wait_recv()
        r_hops[k, 7].wait_recv()
        add_into(own, [x_in[k], y_in[k]], 0, width)
        for s in range(1, depth):
            there = lax.rem(z + s, depth)
            r_copy(
                k,
                7 + s,
                own.at[pl.ds(aligned(there * size, 16), size)],
                z_in[k].at[s - 1],
                (row, there),
            )

    def reduce_end(k):
        _, size, width = red[k]
        for s in range(1, depth):
            r_hops[k, 7 + s].wait_recv()
        total = core_in[k][chip_own, pl.ds(aligned(z * size, 16), size), :].astype(jnp.float32)
        for s in range(1, depth):
            total = total + z_in[k][s - 1].astype(jnp.float32)
        out_w[order[k]][...] = total

    def norm_grad(d_ref, n_ref, inv_ref, gain_at, dst, base, keep_sums):
        gain_row, bias_row = keep_sums

        def body(w, carry):
            at = span_at(w)
            d_val, n_val = d_ref[at, :], n_ref[at, :]
            scaled = d_val * vector(gain_at)
            inner = (
                scaled
                - jnp.mean(scaled, axis=-1, keepdims=True)
                - n_val * jnp.mean(scaled * n_val, axis=-1, keepdims=True)
            )
            dst[at, :] = base[at, :] + inv_ref[at, :][:, :1] * inner
            sums[gain_row : gain_row + 1, :] += jnp.sum(d_val * n_val, axis=0, keepdims=True)
            sums[bias_row : bias_row + 1, :] += jnp.sum(d_val, axis=0, keepdims=True)
            return carry

        spans(body)

    def read_span(ref):
        return lambda b, i, c: ref[
            pl.ds(aligned(b * span + i * pitch, 8), pitch), :
        ][c : c + keep]

    first_rows, last_rows = list(range(keep)), list(range(keep, side))
    pieces_out = [(last_rows, 0, keep), (first_rows, keep, SHIFT), (last_rows, keep, SHIFT)]

    def halo_out(ref, src, dst, base):
        pack(
            read_span(ref),
            lambda piece, b: src.at[piece, pl.ds(aligned(b * halo_rows, 16), halo_rows)],
            pieces_out,
        )
        return [
            launch(
                src.at[piece], dst.at[piece], h_send.at[base + piece], h_recv.at[base + piece],
                device,
            )
            for piece, device in enumerate(((row_down, z), (row, col_down), (row_down, col_down)))
        ]

    def halo_land(copies, ref, dst, out):
        for copy in copies:
            copy.wait_recv()

        def body(b, carry):
            at = pl.ds(aligned(b * halo_rows, 16), halo_rows)
            by_row = dst[0, at].astype(jnp.float32)
            by_col = dst[1, at].astype(jnp.float32)
            by_both = dst[2, at].astype(jnp.float32)
            for i in range(side):
                if i < SHIFT:
                    left = by_both[keep * i : keep * i + SHIFT]
                    right = by_row[keep * i : keep * i + keep]
                else:
                    k = i - SHIFT
                    left = by_col[keep * k : keep * k + SHIFT]
                    right = ref[pl.ds(aligned(b * span + k * pitch, 8), pitch), :][:keep]
                out[i, :, b, :] = jnp.concatenate([left, right], axis=0)
            return carry

        spans(body)

    reduce_core(DN)
    reduce_core(UPW)
    y_copies = halo_out(ys, halo_y_src, halo_y_dst, 3)
    norm_grad(dh2, normed2, inv2, 5, dx1, gs, (5, 6))
    dx1_b[...] = dx1[...].astype(jnp.bfloat16)
    dattn[...] = dot_nt(dx1_b[...], full[1][...])
    grads[1][...] = dot_tn(attn_b[...], dx1_b[...]).astype(jnp.bfloat16)
    for chip in range(tiles):
        core_copy(PR, chip).start()
    sums[4:5, :] = jnp.sum(dx1[...], axis=0, keepdims=True)
    sums[7:8, :] = jnp.sum(gs[...], axis=0, keepdims=True)

    dbias[...] = jnp.zeros_like(dbias)
    dcube[...] = jnp.zeros_like(dcube)

    def attend_back(w):
        def body(g, carry):
            at = span_at(w)
            query = expand(qkv[at, lanes_at(g, 0)])
            key = qkv[at, lanes_at(g, 1)].astype(jnp.bfloat16)
            value = qkv[at, lanes_at(g, 2)].astype(jnp.bfloat16)
            grad = expand(dattn[at, lanes_at(g)])
            prob = probs[w * p.groups + g]
            dprob = dot_nt(value, grad)
            dscore = prob * (dprob - jnp.sum(prob * dprob, axis=0, keepdims=True))
            dbias[g] += dscore
            dlow = dscore.astype(jnp.bfloat16)
            dqkv[at, lanes_at(g, 2)] = dot_plain(prob.astype(jnp.bfloat16), grad)
            dqkv[at, lanes_at(g, 1)] = dot_plain(dlow, query)
            dqkv[at, lanes_at(g, 0)] = fold(dot_tn(dlow, key)) * scale
            return carry

        lax.fori_loop(0, p.groups, body, 0)

    back_steps = {
        0: [lambda: reduce_cross(DN)],
        1: [lambda: reduce_core(PR)],
        2: [lambda: reduce_cross(UPW)],
        3: [lambda: reduce_cross(PR)],
    }
    for w in range(p.images):
        attend_back(w)
        for step in back_steps.get(w, []):
            step()

    dqkv_b[...] = dqkv[...].astype(jnp.bfloat16)
    for n in range(3):
        cols = slice(n * features, (n + 1) * features)
        grads[0][:, cols] = dot_tn(h_b[...], dqkv_b[:, cols]).astype(jnp.bfloat16)
    for chip in range(tiles):
        core_copy(QK, chip).start()
    reduce_chip(DN)
    reduce_core(QK)
    dh1[...] = dot_nt(dqkv_b[...], full[0][...])
    norm_grad(dh1, normed, inv, 0, work, dx1, (0, 1))
    g_copies = halo_out(work, halo_g_src, halo_g_dst, 6)
    sums[2:3, :] = jnp.sum(dqkv[:, :features], axis=0, keepdims=True)
    sums[3:4, :] = jnp.sum(dqkv[:, 2 * features :], axis=0, keepdims=True)
    reduce_chip(UPW)
    reduce_chip(PR)

    for g in range(p.groups):
        for h in range(p.group_heads):
            dcube[g * p.group_heads + h, :, :span] = dbias[g][:, h * span : (h + 1) * span]
    dtab[...] = jnp.zeros_like(dtab)

    def table_step(q, carry):
        parts = [dcube[:, q * p.stack + t, :][:, :HALF] for t in range(p.stack)]
        value = jnp.concatenate(parts, axis=1)
        high = value.astype(jnp.bfloat16).astype(jnp.float32)
        both = jnp.concatenate([high, value - high], axis=0).astype(jnp.bfloat16)
        dtab[...] += dot_nt(both, onehot[q])
        return carry

    lax.fori_loop(0, span // p.stack, table_step, 0)
    reduce_cross(QK)

    small[...] = jnp.zeros_like(small)
    wide = small.shape[1]
    at = 0
    for k in range(8):
        for t in range(features // wide):
            small[at : at + 1, :] = sums[k : k + 1, t * wide : (t + 1) * wide]
            at += 1
    for t in range(p.hidden // wide):
        small[at : at + 1, :] = sums_up[:, t * wide : (t + 1) * wide]
        at += 1
    small[at : at + p.heads, : p.table_rows] = dtab[: p.heads] + dtab[p.heads :]
    share = small.shape[0] // dims[0] // dims[1] // dims[2]
    own_rows = pl.ds(aligned(row * share, 8), share)
    s_copies = []
    for s in range(1, dims[0] * dims[1] * dims[2]):
        there = lax.rem(row + s, rows_total)
        s_copies.append(
            launch(
                small.at[pl.ds(aligned(there * share, 8), share)],
                small_in.at[s - 1],
                s_send.at[0, s],
                s_recv.at[0, s],
                (there, z),
            )
        )
    for copy in s_copies:
        copy.wait_recv()
    total = small[own_rows, :]
    for s in range(1, dims[0] * dims[1] * dims[2]):
        total = total + small_in[s - 1]
    small_mid[...] = total
    small_z[z] = total
    s_copies = [
        launch(
            small_mid,
            small_z.at[z],
            s_send.at[1, s],
            s_recv.at[1, s],
            (row, lax.rem(z + s, depth)),
        )
        for s in range(1, depth)
    ]
    reduce_chip(QK)
    reduce_end(DN)
    for copy in s_copies:
        copy.wait_recv()
    total = small_z[0]
    for s in range(1, depth):
        total = total + small_z[s]
    small_out[own_rows, :] = total
    s_copies = [
        launch(
            small_out.at[own_rows],
            small_out.at[own_rows],
            s_send.at[2, s],
            s_recv.at[2, s],
            (lax.rem(row + s, rows_total), z),
        )
        for s in range(1, dims[0] * dims[1] * dims[2])
    ]
    halo_land(y_copies, ys, halo_y_dst, out_y)
    reduce_end(UPW)
    halo_land(g_copies, work, halo_g_dst, out_g)
    reduce_end(PR)
    reduce_end(QK)
    for copy in s_copies:
        copy.wait_recv()
    for k in range(4):
        for chip in range(tiles):
            core_copy(k, chip).wait_send()
    for copy in started:
        copy.wait_send()


def fused_block(dims, images, cotangent, rel_index, rel_table, weights, vectors):
    images, cotangent = images.transpose(1, 2, 0, 3), cotangent.transpose(1, 2, 0, 3)
    rel_table = rel_table.T
    p = Plan(dims, images, rel_table, weights, vectors)
    f32, bf16 = jnp.float32, jnp.bfloat16
    rows, feats, hidden, span = p.rows, p.features, p.hidden, p.span
    tiles, depth, plane = dims[0] * dims[1], p.depth, dims[0] * dims[1] * dims[2]
    wide = 2 * LANES
    small_rows = (8 * feats + hidden) // wide + p.heads
    small_rows = -(-small_rows // (8 * plane)) * 8 * plane

    def v(*shape, dtype=f32):
        return pltpu.VMEM(shape, dtype)

    scratch = [
        v(16, LANES),
        v(p.devices * 16, LANES, dtype=bf16),
        v(16, feats),
        v(1, hidden),
        v(rows, feats),
        v(rows, feats),
        v(rows, feats),
        v(rows, LANES),
        v(rows, feats, dtype=bf16),
        v(rows, 3 * feats),
        v(p.images * p.groups, span, p.lanes),
        v(rows, feats),
        v(rows, feats, dtype=bf16),
        v(rows, feats),
        v(rows, feats),
        v(rows, LANES),
        v(rows, feats, dtype=bf16),
        v(rows, feats, dtype=bf16),
        v(8, LANES),
        v(8, LANES),
        v(rows, feats),
        v(rows, feats),
        v(rows, feats),
        v(rows, feats, dtype=bf16),
        v(rows, feats),
        v(rows, 3 * feats),
        v(rows, 3 * feats, dtype=bf16),
        v(rows, feats),
        v(rows, feats),
        v(LANES, LANES),
        v(LANES, LANES),
        v(8, LANES),
        v(span, LANES),
        v(span // p.stack, p.stack * HALF),
        v(p.heads, p.table_rows),
        v(2 * p.heads, p.table_rows, dtype=bf16),
        v(span // p.stack, p.table_rows, p.stack * HALF, dtype=bf16),
        v(p.heads, span, LANES),
        v(p.groups, span, p.lanes),
        v(p.groups, span, p.lanes),
        v(p.heads, span, LANES),
        v(2 * p.heads, p.table_rows),
        v(8, feats),
        v(1, hidden),
        v(small_rows, wide),
        v(plane - 1, small_rows // plane, wide),
        v(small_rows // plane, wide),
        v(depth, small_rows // plane, wide),
    ]
    sizes = [(w.shape[0], w.shape[1]) for w in weights]
    scratch += [v(p.devices * m, n, dtype=bf16) for m, n in sizes]
    scratch += [v(p.devices * m, n, dtype=bf16) for m, n in sizes]
    turned = [sizes[3], sizes[2], sizes[1], sizes[0]]
    scratch += [v(tiles, depth * m, n, dtype=bf16) for m, n in turned]
    scratch += [v(depth * m, n, dtype=bf16) for m, n in turned] * 2
    scratch += [v(depth * m, n // 2, dtype=bf16) for m, n in turned] * 2
    scratch += [v(depth - 1, m, n, dtype=bf16) for m, n in turned]
    halo_rows = p.images * 4 * p.keep
    scratch += [v(3, 2, halo_rows, feats, dtype=bf16)] * 2
    scratch += [v(3, halo_rows, feats, dtype=bf16)] * 4
    dma = pltpu.SemaphoreType.DMA
    scratch += [dma((7, 12 + depth))] * 2 + [dma((4, 7 + depth))] * 2
    scratch += [dma((9,))] * 2 + [dma((3, plane + depth))] * 2 + [dma((17,))]
    scratch += [v(*images.shape)] * 2 + [v(*rel_index.shape, dtype=rel_index.dtype)]
    scratch += [v(*rel_table.shape)]
    scratch += [v(1, vector.shape[0], dtype=bf16) for vector in vectors]
    out_shape = [
        jax.ShapeDtypeStruct(images.shape, f32),
        jax.ShapeDtypeStruct(images.shape, f32),
    ]
    out_shape += [jax.ShapeDtypeStruct(w.shape, f32) for w in weights]
    out_shape += [jax.ShapeDtypeStruct((small_rows, wide), f32)]
    spec = pl.BlockSpec(memory_space=pltpu.VMEM)
    outs = pl.pallas_call(
        functools.partial(block_kernel, p),
        name="block",
        out_shape=out_shape,
        in_specs=[pl.BlockSpec(memory_space=pltpu.HBM)] * 17,
        out_specs=[spec] * 7,
        scratch_shapes=scratch,
        compiler_params=pltpu.CompilerParams(
            collective_id=2, has_side_effects=True, vmem_limit_bytes=60 * 1024 * 1024
        ),
    )(
        images,
        cotangent,
        rel_index,
        rel_table,
        *[vector.reshape(1, -1) for vector in vectors],
        *weights,
    )
    sizes_small = [vector.shape[0] for vector in vectors]
    held = pl.BlockSpec(memory_space=pl.ANY)
    last_shape = [jax.ShapeDtypeStruct(out.shape, f32) for out in outs[:6]]
    last_shape += [jax.ShapeDtypeStruct((1, size), f32) for size in sizes_small]
    last_shape += [jax.ShapeDtypeStruct((p.heads, p.table_size), f32)]
    last = pl.pallas_call(
        functools.partial(emit_kernel, p, sizes_small),
        name="emit",
        out_shape=last_shape,
        in_specs=[spec] * 7,
        out_specs=[held] * 6 + [spec] * 10,
        scratch_shapes=[dma((6,))],
        compiler_params=pltpu.CompilerParams(vmem_limit_bytes=60 * 1024 * 1024),
    )(*outs)
    tokens = [out.transpose(2, 0, 1, 3) for out in last[:2]]
    vector_outs = [out.reshape(-1) for out in last[6:15]]
    return (*tokens, *last[2:6], *vector_outs, last[15].T)


def emit_kernel(plan, sizes, *refs):
    p = plan
    big, small, big_out = refs[:6], refs[6], refs[7:13]
    vector_outs, table_out, sems = refs[13:22], refs[22], refs[23]
    copies = [pltpu.make_async_copy(big[k], big_out[k], sems.at[k]) for k in range(6)]
    for copy in copies:
        copy.start()
    wide = small.shape[1]
    me = lax.axis_index("rows") * p.depth + lax.axis_index("cols")
    size, size_up = sizes[0], sizes[7]
    per = p.features // wide
    line, turn = me * size // wide, lax.rem(me * size, wide)
    lines = jnp.concatenate([small[pl.ds(k * per + line, 1), :] for k in range(8)], axis=0)
    lines = pltpu.roll(lines, wide - turn, 1)
    for k in range(9):
        if k != 7:
            at = k if k < 7 else 7
            vector_outs[k][...] = lines[at : at + 1, :size]
    line, turn = me * size_up // wide, lax.rem(me * size_up, wide)
    up = small[pl.ds(8 * per + line, 1), :]
    up = pltpu.roll(jnp.broadcast_to(up, (8, wide)), wide - turn, 1)
    vector_outs[7][...] = up[:1, :size_up]
    at = 8 * per + p.hidden // wide
    table_out[...] = small[at : at + p.heads, : p.table_size]
    for copy in copies:
        copy.wait()


def per_device(images, cotangent, rel_index, rel_table, *params):
    dims = sizes_here()
    weights, vectors = params[:4], params[4:]
    if fits_fused(dims, images, weights, vectors):
        return fused_block(dims, images, cotangent, rel_index, rel_table, weights, vectors)
    return plain_block(images, cotangent, rel_index, rel_table, *params)


def solution(mesh):
    in_specs = (
        P(None, "rows", "cols", None),
        P(None, "rows", "cols", None),
        P(),
        P(),
        P(("rows", "cols"), None),
        P(("rows", "cols"), None),
        P(("rows", "cols"), None),
        P(("rows", "cols"), None),
        P(("rows", "cols")),
        P(("rows", "cols")),
        P(("rows", "cols")),
        P(("rows", "cols")),
        P(("rows", "cols")),
        P(("rows", "cols")),
        P(("rows", "cols")),
        P(("rows", "cols")),
        P(("rows", "cols")),
    )
    out_specs = (
        P(None, "rows", "cols", None),
        P(None, "rows", "cols", None),
        P(("rows", "cols"), None),
        P(("rows", "cols"), None),
        P(("rows", "cols"), None),
        P(("rows", "cols"), None),
        P(("rows", "cols")),
        P(("rows", "cols")),
        P(("rows", "cols")),
        P(("rows", "cols")),
        P(("rows", "cols")),
        P(("rows", "cols")),
        P(("rows", "cols")),
        P(("rows", "cols")),
        P(("rows", "cols")),
        P(),
    )
    return jax.shard_map(
        per_device, mesh=mesh, in_specs=in_specs, out_specs=out_specs, check_vma=False
    )
```

```python
import functools

import jax
import jax.numpy as jnp
from jax import lax
from jax.experimental import pallas as pl
from jax.experimental.pallas import tpu as pltpu
from jax.sharding import PartitionSpec as P

WIN = 7
SHIFT = 3


norm_eps = 1e-05
root_half = 0.7071067811865476
tau_factor = 0.3989422804014327
big_negative = -1e30


def shifted(array, axis, by):
    length = lax.axis_size(axis)
    return lax.ppermute(array, axis, [(i, (i + by) % length) for i in range(length)])


def as_sent(array):

    def short(part):
        return part.astype(jnp.bfloat16) if part.dtype == jnp.float32 else part

    return jax.tree.map(short, array)


def layer_norm(values, gain_vec, offset):
    mean_val = jnp.mean(values, axis=-1, keepdims=True)
    centred = values - mean_val
    inv_std = lax.rsqrt(jnp.mean(centred * centred, axis=-1, keepdims=True) + norm_eps)
    normed = centred * inv_std
    return (normed * gain_vec + offset, normed, inv_std)


def norm_back(grad_out, normed, inv_std, gain_vec):
    scaled = grad_out * gain_vec
    row_inner = (
        scaled
        - jnp.mean(scaled, axis=-1, keepdims=True)
        - normed * jnp.mean(scaled * normed, axis=-1, keepdims=True)
    )
    return (inv_std * row_inner, jnp.sum(grad_out * normed, axis=0), jnp.sum(grad_out, axis=0))


def dot_plain(former, latter):
    return jnp.dot(former, latter, preferred_element_type=jnp.float32)


def dot_lead(former, latter):
    return lax.dot_general(
        former, latter, (((0,), (0,)), ((), ())), preferred_element_type=jnp.float32
    )


def dot_tail(former, latter):
    return lax.dot_general(
        former, latter, (((1,), (1,)), ((), ())), preferred_element_type=jnp.float32
    )


def band_of(positions, length):
    return (positions >= length - WIN).astype(jnp.int32) + (positions >= length - SHIFT).astype(
        jnp.int32
    )


def roll_in(images, cotangent):
    from_below = shifted((images[:, :SHIFT], cotangent[:, :SHIFT]), "rows", -1)
    tall_tokens = jnp.concatenate([images[:, SHIFT:], from_below[0]], axis=1)
    tall_grads = jnp.concatenate([cotangent[:, SHIFT:], from_below[1]], axis=1)
    beside = shifted((tall_tokens[:, :, :SHIFT], tall_grads[:, :, :SHIFT]), "cols", -1)
    return (
        jnp.concatenate([tall_tokens[:, :, SHIFT:], beside[0]], axis=2),
        jnp.concatenate([tall_grads[:, :, SHIFT:], beside[1]], axis=2),
    )


def roll_out(result, grad_tokens):
    from_above = (
        shifted(result[:, -SHIFT:].astype(jnp.bfloat16), "rows", 1).astype(jnp.float32),
        shifted(grad_tokens[:, -SHIFT:].astype(jnp.bfloat16), "rows", 1).astype(jnp.float32),
    )
    tall_result = jnp.concatenate([from_above[0], result[:, :-SHIFT]], axis=1)
    tall_grads = jnp.concatenate([from_above[1], grad_tokens[:, :-SHIFT]], axis=1)
    beside = (
        shifted(tall_result[:, :, -SHIFT:].astype(jnp.bfloat16), "cols", 1).astype(jnp.float32),
        shifted(as_sent(tall_grads[:, :, -SHIFT:]), "cols", 1),
    )
    return (
        jnp.concatenate([beside[0], tall_result[:, :, :-SHIFT]], axis=2),
        jnp.concatenate([beside[1], tall_grads[:, :, :-SHIFT]], axis=2),
    )


MESH = pl.DeviceIdType.MESH
CORES = 2


def grid_of(rows):
    chips = rows // CORES
    across = 1
    for size in range(1, chips + 1):
        if chips % size == 0 and size * size <= chips:
            across = size
    return chips // across, across


def whereabouts(dims):
    height, width = dims[0], dims[1]
    row, depth_at = lax.axis_index("rows"), lax.axis_index("cols")
    core = lax.rem(row, CORES)
    chip = row // CORES
    return chip // width, lax.rem(chip, width), core, depth_at


def device_at(dims, y, x, core, z):
    return ((y * dims[1] + x) * CORES + core, z)


def greet(dims, here):
    barrier = pltpu.get_barrier_semaphore()
    total = 0
    for axis in range(4):
        for step in range(1, dims[axis]):
            there = list(here)
            there[axis] = lax.rem(here[axis] + step, dims[axis])
            pl.semaphore_signal(
                barrier, inc=1, device_id=device_at(dims, *there), device_id_type=MESH
            )
            total += 1
    pl.semaphore_wait(barrier, total)


def moved(here, axis, step, dims):
    there = list(here)
    there[axis] = lax.rem(here[axis] + step, dims[axis])
    return there


def gather_kernel(dims, count, *refs):
    ins, outs = refs[:count], refs[count : 2 * count]
    local_sem, send_sem, recv_sem = refs[2 * count :]
    height, width, _, depth = dims
    here = whereabouts(dims)
    y, x, core, z = here
    greet(dims, here)
    used = [0] * count

    def send(stream, src, dst, there):
        slot = used[stream]
        used[stream] += 1
        copy = pltpu.make_async_remote_copy(
            src_ref=src,
            dst_ref=dst,
            send_sem=send_sem.at[stream, slot],
            recv_sem=recv_sem.at[stream, slot],
            device_id=device_at(dims, *there),
            device_id_type=MESH,
        )
        copy.start()
        return copy

    started = []
    along_z, locals_ = [], []
    for k in range(count):
        mine = pltpu.make_async_copy(ins[k], outs[k].at[y, x, core, z], local_sem.at[k])
        mine.start()
        locals_.append(mine)
        along_z.append(
            [
                send(k, ins[k], outs[k].at[y, x, core, z], moved(here, 3, step, dims))
                for step in range(1, depth)
            ]
        )
        started += along_z[k]
    first, second, partner = [], [], []
    other = moved(here, 2, 1, dims)
    for k in range(count):
        locals_[k].wait()
        for copy in along_z[k]:
            copy.wait_recv()
        axis = k % 2
        block = outs[k].at[y, x, core]
        first.append(
            [send(k, block, block, moved(here, axis, s, dims)) for s in range(1, dims[axis])]
        )
        partner.append([send(k, block, block, other)])
        started += first[k] + partner[k]
    for k in range(count):
        axis = k % 2
        cross = 1 - axis
        for copy in first[k]:
            copy.wait_recv()
        copies = []
        for lag in range(dims[axis]):
            at = moved(here, axis, lag, dims)
            block = outs[k].at[at[0], at[1], core]
            copies += [
                send(k, block, block, moved(here, cross, s, dims)) for s in range(1, dims[cross])
            ]
            if lag:
                partner[k].append(send(k, block, block, other))
                started.append(partner[k][-1])
        second.append(copies)
        started += copies
    for k in range(count):
        axis = k % 2
        cross = 1 - axis
        copies = iter(second[k])
        for lag in range(dims[axis]):
            for s in range(1, dims[cross]):
                next(copies).wait_recv()
                at = moved(here, axis, lag, dims)
                at[cross] = lax.rem(here[cross] + dims[cross] - s, dims[cross])
                block = outs[k].at[at[0], at[1], core]
                partner[k].append(send(k, block, block, other))
                started.append(partner[k][-1])
    for k in range(count):
        for copy in partner[k]:
            copy.wait_recv()
    for copy in started:
        copy.wait_send()


def reduce_kernel(dims, count, *refs):
    ins, table = refs[:count], refs[count]
    outs, table_out = refs[count + 1 : 2 * count + 1], refs[2 * count + 1]
    rest = refs[2 * count + 2 :]
    bufs = [rest[7 * k : 7 * k + 7] for k in range(count)]
    table_in = rest[7 * count : 7 * count + 4]
    table_sum = rest[7 * count + 4 : 7 * count + 7]
    send_sem, recv_sem = rest[7 * count + 7 :]
    height, width, _, depth = dims
    here = whereabouts(dims)
    y, x, core, z = here
    greet(dims, here)
    used = [0] * (count + 1)
    started = []

    def send(stream, src, dst, there):
        slot = used[stream]
        used[stream] += 1
        copy = pltpu.make_async_remote_copy(
            src_ref=src,
            dst_ref=dst,
            send_sem=send_sem.at[stream, slot],
            recv_sem=recv_sem.at[stream, slot],
            device_id=device_at(dims, *there),
            device_id_type=MESH,
        )
        copy.start()
        started.append(copy)
        return copy

    def add(dst, parts):
        def body(i, carry):
            total = parts[0][i].astype(jnp.float32)
            for part in parts[1:]:
                total = total + part[i].astype(jnp.float32)
            dst[i] = total.astype(dst.dtype)
            return carry

        lax.fori_loop(0, depth, body, 0)

    def table_step(stage, axis, src):
        table_in[stage][here[axis]] = src[...]
        return [
            send(count, src, table_in[stage].at[here[axis]], moved(here, axis, s, dims))
            for s in range(1, dims[axis])
        ]

    def table_add(stage, axis, copies, dst):
        for copy in copies:
            copy.wait_recv()
        total = table_in[stage][0]
        for j in range(1, dims[axis]):
            total = total + table_in[stage][j]
        dst[...] = total

    other = moved(here, 2, 1, dims)
    table_copies = table_step(0, 2, table)
    core_copies = []
    for k in range(count):
        axis = k % 2
        cross = 1 - axis
        group = {}
        for lag in list(range(1, dims[axis])) + [0]:
            for j in range(dims[cross]):
                at = moved(here, axis, lag, dims)
                at[cross] = j
                group[lag, j] = send(
                    k, ins[k].at[at[0], at[1], other[2]], bufs[k][0].at[at[0], at[1]], other
                )
        core_copies.append(group)
    table_add(0, 2, table_copies, table_sum[0])
    table_copies = table_step(1, 0, table_sum[0])
    first = []
    for k in range(count):
        axis = k % 2
        cross = 1 - axis
        from_core, sum_core, from_first = bufs[k][0], bufs[k][1], bufs[k][2]
        group = []
        for lag in list(range(1, dims[axis])) + [0]:
            for j in range(dims[cross]):
                at = moved(here, axis, lag, dims)
                at[cross] = j
                core_copies[k][lag, j].wait_recv()
                block = sum_core.at[at[0], at[1]]
                add(block, [ins[k].at[at[0], at[1], core], from_core.at[at[0], at[1]]])
                if lag:
                    group.append(
                        send(k, block, from_first.at[lag - 1, j], moved(here, axis, lag, dims))
                    )
        first.append(group)
    table_add(1, 0, table_copies, table_sum[1])
    table_copies = table_step(2, 1, table_sum[1])
    second = []
    for k in range(count):
        axis = k % 2
        cross = 1 - axis
        sum_core, from_first, sum_first, from_second = bufs[k][1:5]
        for copy in first[k]:
            copy.wait_recv()
        group = []
        for lag in list(range(1, dims[cross])) + [0]:
            at = moved(here, cross, lag, dims)
            j = at[cross]
            block = sum_first.at[j]
            add(
                block,
                [sum_core.at[at[0], at[1]]]
                + [from_first.at[s - 1, j] for s in range(1, dims[axis])],
            )
            if lag:
                group.append(send(k, block, from_second.at[lag - 1], at))
        second.append(group)
    table_add(2, 1, table_copies, table_sum[2])
    table_copies = table_step(3, 3, table_sum[2])
    third = []
    for k in range(count):
        axis = k % 2
        cross = 1 - axis
        sum_first, from_second, sum_second, from_third = bufs[k][3:7]
        for copy in second[k]:
            copy.wait_recv()
        add(
            sum_second,
            [sum_first.at[here[cross]]] + [from_second.at[s - 1] for s in range(1, dims[cross])],
        )
        group = []
        for step in range(1, depth):
            at = moved(here, 3, step, dims)
            group.append(send(k, sum_second.at[at[3]], from_third.at[step - 1], at))
        third.append(group)
    table_add(3, 3, table_copies, table_out)
    for k in range(count):
        sum_second, from_third = bufs[k][5:7]
        for copy in third[k]:
            copy.wait_recv()
        total = sum_second[z].astype(jnp.float32)
        for step in range(1, depth):
            total = total + from_third[step - 1].astype(jnp.float32)
        outs[k][...] = total
    for copy in started:
        copy.wait_send()


def sizes_here():
    rows, depth = lax.axis_size("rows"), lax.axis_size("cols")
    height, width = grid_of(rows)
    return height, width, CORES, depth


def blocked(rows, columns):
    if rows % 16 == 0:
        return rows, columns
    return rows * columns // 128, 128


def gather_all(shards):
    dims = sizes_here()
    height, width, cores, depth = dims
    count = len(shards)
    blocks = [blocked(*shard.shape) for shard in shards]
    slots = (depth - 1) + max(height, width) * 2 * height * width
    outs = pl.pallas_call(
        functools.partial(gather_kernel, dims, count),
        name="gather_all",
        out_shape=[
            jax.ShapeDtypeStruct(dims + block, shard.dtype)
            for block, shard in zip(blocks, shards)
        ],
        in_specs=[pl.BlockSpec(memory_space=pltpu.VMEM)] * count,
        out_specs=[pl.BlockSpec(memory_space=pl.ANY)] * count,
        scratch_shapes=[
            pltpu.SemaphoreType.DMA((count,)),
            pltpu.SemaphoreType.DMA((count, slots)),
            pltpu.SemaphoreType.DMA((count, slots)),
        ],
        compiler_params=pltpu.CompilerParams(collective_id=0, has_side_effects=True),
    )(*[shard.reshape(block) for block, shard in zip(blocks, shards)])
    total = height * width * cores * depth
    return [
        out.reshape(total * shard.shape[0], shard.shape[1]) for out, shard in zip(outs, shards)
    ]


def reduce_all(wholes, table):
    dims = sizes_here()
    height, width, cores, depth = dims
    total = height * width * cores * depth
    count = len(wholes)
    shares = [(whole.shape[0] // total, whole.shape[1]) for whole in wholes]
    blocks = [blocked(*share) for share in shares]
    scratch = []
    for k, (block, whole) in enumerate(zip(blocks, wholes)):
        along, cross = dims[k % 2], dims[1 - k % 2]
        for lead in (
            (height, width, depth),
            (height, width, depth),
            (max(along - 1, 1), cross, depth),
            (cross, depth),
            (max(cross - 1, 1), depth),
            (depth,),
            (max(depth - 1, 1),),
        ):
            scratch.append(pltpu.VMEM(lead + block, whole.dtype))
    for size in (cores, height, width, depth):
        scratch.append(pltpu.VMEM((size,) + table.shape, table.dtype))
    scratch += [pltpu.VMEM(table.shape, table.dtype)] * 3
    slots = 2 * height * width + height + width + depth
    scratch += [pltpu.SemaphoreType.DMA((count + 1, slots))] * 2
    outs = pl.pallas_call(
        functools.partial(reduce_kernel, dims, count),
        name="reduce_all",
        out_shape=[jax.ShapeDtypeStruct(block, jnp.float32) for block in blocks]
        + [jax.ShapeDtypeStruct(table.shape, table.dtype)],
        in_specs=[pl.BlockSpec(memory_space=pltpu.VMEM)] * (count + 1),
        out_specs=[pl.BlockSpec(memory_space=pltpu.VMEM)] * (count + 1),
        scratch_shapes=scratch,
        compiler_params=pltpu.CompilerParams(collective_id=1, has_side_effects=True),
    )(*[whole.reshape(dims + block) for block, whole in zip(blocks, wholes)], table)
    return [out.reshape(share) for out, share in zip(outs, shares)], outs[-1]


def padded(values, multiple):
    size = values.shape[-1]
    extra = -size % multiple
    return jnp.pad(values, [(0, 0)] * (values.ndim - 1) + [(0, extra)])


def plain_block(
    images,
    cotangent,
    rel_index,
    rel_table,
    qkv_weight,
    proj_weight,
    up_weight,
    down_weight,
    norm1_gain,
    norm1_bias,
    query_bias,
    value_bias,
    proj_bias,
    norm2_gain,
    norm2_bias,
    up_bias,
    down_bias,
):
    shards = (
        norm1_gain,
        norm1_bias,
        query_bias,
        value_bias,
        proj_bias,
        norm2_gain,
        norm2_bias,
        up_bias,
        down_bias,
    )
    vector_shard = padded(jnp.concatenate(shards)[None], 2048).reshape(-1, 128)
    qkv_full, down_full, up_full, proj_full, vector_full = gather_all(
        [qkv_weight, down_weight, up_weight, proj_weight, vector_shard]
    )
    device_count = lax.axis_size("rows") * lax.axis_size("cols")
    vector_full = vector_full.reshape(device_count, -1)
    vectors, offset = [], 0
    for shard in shards:
        size = shard.shape[0]
        vectors.append(vector_full[:, offset : offset + size].reshape(device_count * size))
        offset += size
    (
        gain_one_full,
        bias_one_full,
        query_add,
        value_add,
        proj_add,
        gain_two_full,
        bias_two_full,
        up_add,
        down_add,
    ) = vectors
    tokens_tile, grad_tile = roll_in(images, cotangent)
    image_count, tile_side, features = (
        tokens_tile.shape[0],
        tokens_tile.shape[1],
        tokens_tile.shape[3],
    )
    window = tile_side * tile_side
    row_total = image_count * window
    tokens = tokens_tile.reshape(row_total, features)
    grad_rows = grad_tile.reshape(row_total, features)
    local_pos = jnp.arange(tile_side, dtype=jnp.int32)
    band_rows = band_of(
        lax.axis_index("rows") * tile_side + local_pos, lax.axis_size("rows") * tile_side
    )
    band_cols = band_of(
        lax.axis_index("cols") * tile_side + local_pos, lax.axis_size("cols") * tile_side
    )
    region = (3 * band_rows[:, None] + band_cols[None, :]).reshape(window)
    allowed = (region[:, None] == region[None, :])[None, None]
    head_count = rel_table.shape[1]
    table_size = rel_table.shape[0]
    head_width = features // head_count
    score_scale = head_width ** (-0.5)
    onehot = (
        rel_index.reshape(window * window)[:, None]
        == jnp.arange(table_size, dtype=jnp.int32)[None, :]
    ).astype(jnp.float32)
    bias_flat = jnp.dot(
        onehot, rel_table, precision=lax.Precision.HIGHEST, preferred_element_type=jnp.float32
    )
    bias_heads = bias_flat.T.reshape(head_count, window, window)

    def split_heads(values):
        return values.reshape(image_count, window, head_count, head_width)

    def scores_of(query_b, key_b):
        raw_scores = jnp.einsum(
            "wqhd,wkhd->whqk",
            split_heads(query_b),
            split_heads(key_b),
            preferred_element_type=jnp.float32,
        )
        return jnp.where(allowed, raw_scores + bias_heads[None], big_negative)

    gain_one = gain_one_full.astype(jnp.float32)
    gain_two = gain_two_full.astype(jnp.float32)
    out_one, normed_one, inv_one = layer_norm(tokens, gain_one, bias_one_full.astype(jnp.float32))
    h_one = out_one.astype(jnp.bfloat16)
    projected = dot_plain(h_one, qkv_full)
    query_b = ((projected[:, :features] + query_add.astype(jnp.float32)) * score_scale).astype(
        jnp.bfloat16
    )
    key_b = projected[:, features : 2 * features].astype(jnp.bfloat16)
    value_b = (projected[:, 2 * features :] + value_add.astype(jnp.float32)).astype(jnp.bfloat16)
    scores = scores_of(query_b, key_b)
    row_top = jnp.max(scores, axis=-1, keepdims=True)
    log_total = row_top + jnp.log(jnp.sum(jnp.exp(scores - row_top), axis=-1, keepdims=True))
    attend_b = jnp.exp(scores - log_total).astype(jnp.bfloat16)
    attn_b = (
        jnp.einsum(
            "whqk,wkhd->wqhd", attend_b, split_heads(value_b), preferred_element_type=jnp.float32
        )
        .reshape(row_total, features)
        .astype(jnp.bfloat16)
    )
    residual = tokens + dot_plain(attn_b, proj_full) + proj_add.astype(jnp.float32)
    out_two, normed_two, inv_two = layer_norm(residual, gain_two, bias_two_full.astype(jnp.float32))
    h_two = out_two.astype(jnp.bfloat16)
    hidden_pre = dot_plain(h_two, up_full) + up_add.astype(jnp.float32)
    gauss_cdf = 0.5 * (1.0 + lax.erf(hidden_pre * root_half))
    act_b = (hidden_pre * gauss_cdf).astype(jnp.bfloat16)
    result = residual + dot_plain(act_b, down_full) + down_add.astype(jnp.float32)
    grad_b = grad_rows.astype(jnp.bfloat16)
    grad_down = dot_lead(act_b, grad_b)
    grad_down_add = jnp.sum(grad_rows, axis=0)
    grad_act = dot_tail(grad_b, down_full)
    density = jnp.exp(-0.5 * hidden_pre * hidden_pre) * tau_factor
    grad_pre = grad_act * (gauss_cdf + hidden_pre * density)
    grad_pre_b = grad_pre.astype(jnp.bfloat16)
    grad_up = dot_lead(h_two, grad_pre_b)
    grad_up_add = jnp.sum(grad_pre, axis=0)
    grad_h_two = dot_tail(grad_pre_b, up_full)
    grad_resid, grad_gain_two, grad_bias_two = norm_back(
        grad_h_two, normed_two, inv_two, gain_two
    )
    grad_resid = grad_resid + grad_rows
    grad_resid_b = grad_resid.astype(jnp.bfloat16)
    grad_proj = dot_lead(attn_b, grad_resid_b)
    grad_proj_add = jnp.sum(grad_resid, axis=0)
    grad_attn_b = dot_tail(grad_resid_b, proj_full).astype(jnp.bfloat16)
    grad_heads = split_heads(grad_attn_b)
    grad_attend = jnp.einsum(
        "wqhd,wkhd->whqk", grad_heads, split_heads(value_b), preferred_element_type=jnp.float32
    )
    attend = jnp.exp(scores_of(query_b, key_b) - log_total)
    grad_value = jnp.einsum(
        "whqk,wqhd->wkhd",
        attend.astype(jnp.bfloat16),
        grad_heads,
        preferred_element_type=jnp.float32,
    ).reshape(row_total, features)
    row_inner = jnp.sum(attend * grad_attend, axis=-1, keepdims=True)
    grad_scores = attend * (grad_attend - row_inner)
    grad_bias_heads = jnp.sum(grad_scores, axis=0).reshape(head_count, window * window)
    table_local = lax.dot_general(
        onehot,
        grad_bias_heads,
        (((0,), (1,)), ((), ())),
        precision=lax.Precision.HIGHEST,
        preferred_element_type=jnp.float32,
    )
    grad_scores_b = grad_scores.astype(jnp.bfloat16)
    grad_query = (
        jnp.einsum(
            "whqk,wkhd->wqhd", grad_scores_b, split_heads(key_b), preferred_element_type=jnp.float32
        )
        * score_scale
    ).reshape(row_total, features)
    grad_key = jnp.einsum(
        "whqk,wqhd->wkhd", grad_scores_b, split_heads(query_b), preferred_element_type=jnp.float32
    ).reshape(row_total, features)
    grad_query_add = jnp.sum(grad_query, axis=0)
    grad_value_add = jnp.sum(grad_value, axis=0)
    grad_mixed_b = jnp.concatenate([grad_query, grad_key, grad_value], axis=1).astype(jnp.bfloat16)
    grad_qkv = dot_lead(h_one, grad_mixed_b)
    grad_h_one = dot_tail(grad_mixed_b, qkv_full)
    grad_in, grad_gain_one, grad_bias_one = norm_back(
        grad_h_one, normed_one, inv_one, gain_one
    )
    grad_tokens = grad_resid + grad_in
    vector_grads = (
        grad_gain_one,
        grad_bias_one,
        grad_query_add,
        grad_value_add,
        grad_proj_add,
        grad_gain_two,
        grad_bias_two,
        grad_up_add,
        grad_down_add,
    )
    vector_rows = padded(
        jnp.concatenate([grad.reshape(device_count, -1) for grad in vector_grads], axis=1), 2048
    ).reshape(-1, 128)
    table_rows = padded(table_local.reshape(1, -1), 1024).reshape(-1, 128)
    (down_sum, up_sum, qkv_sum, proj_sum, vector_sum), table_sum = reduce_all(
        [
            grad_down.astype(jnp.bfloat16),
            grad_up.astype(jnp.bfloat16),
            grad_qkv.astype(jnp.bfloat16),
            grad_proj.astype(jnp.bfloat16),
            vector_rows,
        ],
        table_rows,
    )
    grad_table = table_sum.reshape(-1)[: table_local.size].reshape(table_local.shape)
    vector_sum = vector_sum.reshape(-1)
    vector_sums, offset = [], 0
    for shard in shards:
        size = shard.shape[0]
        vector_sums.append(vector_sum[offset : offset + size])
        offset += size
    shard_grads = (qkv_sum, proj_sum, up_sum, down_sum, *vector_sums)
    block_out, grad_images = roll_out(
        result.reshape(image_count, tile_side, tile_side, features),
        grad_tokens.reshape(image_count, tile_side, tile_side, features),
    )
    return (
        block_out,
        grad_images,
        shard_grads[0],
        shard_grads[1],
        shard_grads[2],
        shard_grads[3],
        shard_grads[4],
        shard_grads[5],
        shard_grads[6],
        shard_grads[7],
        shard_grads[8],
        shard_grads[9],
        shard_grads[10],
        shard_grads[11],
        shard_grads[12],
        grad_table,
    )


LANES = 128
HALF = 64


def dot_nt(former, latter):
    return lax.dot_general(
        former, latter, (((1,), (1,)), ((), ())), preferred_element_type=jnp.float32
    )


def dot_tn(former, latter):
    return lax.dot_general(
        former, latter, (((0,), (0,)), ((), ())), preferred_element_type=jnp.float32
    )


def iota(shape, dim):
    return lax.broadcasted_iota(jnp.int32, shape, dim)


def aligned(value, multiple):
    return pl.multiple_of(value, multiple)


class Plan:
    def __init__(self, dims, images, rel_table, weights, vectors):
        self.dims = dims
        self.depth = dims[3]
        self.side, _, self.images, self.features = images.shape
        self.keep = self.side - SHIFT
        self.pitch = self.side + 1
        self.span = self.side * self.pitch
        self.rows = self.images * self.span
        self.heads, self.table_size = rel_table.shape
        self.head_width = self.features // self.heads
        self.group_heads = LANES // self.head_width
        self.groups = self.features // LANES
        self.lanes = self.group_heads * self.span
        self.table_rows = -(-self.table_size // 16) * 16
        self.shard_rows = [w.shape[0] for w in weights]
        self.widths = [w.shape[1] for w in weights]
        self.devices = dims[0] * dims[1] * dims[2] * dims[3]
        self.hidden = weights[2].shape[1]
        self.stack = 4
        self.cuts = (3, 1, 4, 2)
        third, part = self.widths[0] // 3, self.hidden // 2
        self.reductions = [(3, 0, self.features), (2, 0, part), (2, part, part)]
        self.reductions += [(1, 0, self.features)]
        self.reductions += [(0, n * third, third) for n in range(3)]
        self.vector_sizes = [v.shape[0] for v in vectors]


def fits_fused(dims, images, weights, vectors):
    return (
        dims[0] == 2
        and dims[1] == 2
        and dims[2] == 2
        and dims[3] > 1
        and all(w.shape[0] % 16 == 0 for w in weights)
        and images.shape[1] == WIN
        and images.shape[2] == WIN
    )


def block_kernel(plan, *refs):
    p = plan
    take = iter(refs)

    def pull(count):
        return [next(take) for _ in range(count)]

    held = pull(13)
    shards = pull(4)
    out_y, out_g = pull(2)
    out_w = pull(4)
    (small_out,) = pull(1)
    (
        vec_shard,
        vec_full,
        vec,
        up_vec,
        xs,
        gs,
        normed,
        inv,
        h_b,
        qkv,
        probs,
        attn,
        attn_b,
        x1,
        normed2,
        inv2,
        h2_b,
        gy_b,
        act_b,
        dpre_b,
        ys,
        dh2,
        dx1,
        dx1_b,
        dattn,
        dqkv,
        dqkv_b,
        dh1,
        work,
        square,
        flipped,
        flipped_pad,
        index_t,
        index_q,
        tab,
        tab_b,
        onehot,
        bias_cube,
        bias,
        dbias,
        dcube,
        dtab,
        sums,
        sums_up,
        small,
        small_in,
        small_mid,
        small_z,
    ) = pull(48)
    full = pull(4)
    grads = pull(4)
    core_in = pull(7)
    x_in, y_in, a_in, b_in, z_in = pull(7), pull(7), pull(7), pull(7), pull(7)
    halo_in_src, halo_in_dst, halo_y_src, halo_y_dst, halo_g_src, halo_g_dst = pull(6)
    g_send, g_recv, r_send, r_recv, h_send, h_recv, s_send, s_recv = pull(8)
    local_sem = next(take)
    staged = pull(13)
    images, cotangent, rel_index, rel_table = staged[:4]
    vector_ins = staged[4:]

    dims, depth = p.dims, p.depth
    rows_total = lax.axis_size("rows")
    row, z = lax.axis_index("rows"), lax.axis_index("cols")
    here = whereabouts(dims)
    y, x, core = here[0], here[1], here[2]
    me = row * depth + z
    partner_at = (y * dims[1] + x) * CORES + (1 - core)
    x_at = (y * dims[1] + (1 - x)) * CORES + core
    y_at = ((1 - y) * dims[1] + x) * CORES + core
    chip_own = y * dims[1] + x
    chip_x = y * dims[1] + (1 - x)
    chip_y = (1 - y) * dims[1] + x
    chip_d = (1 - y) * dims[1] + (1 - x)
    row_up, row_down = lax.rem(row + rows_total - 1, rows_total), lax.rem(row + 1, rows_total)
    col_up, col_down = lax.rem(z + depth - 1, depth), lax.rem(z + 1, depth)
    started = []

    def remote(src, dst, send_sem, recv_sem, device):
        return pltpu.make_async_remote_copy(
            src_ref=src,
            dst_ref=dst,
            send_sem=send_sem,
            recv_sem=recv_sem,
            device_id=device,
            device_id_type=MESH,
        )

    def launch(*args):
        copy = remote(*args)
        copy.start()
        started.append(copy)
        return copy

    loads = [
        pltpu.make_async_copy(src, dst, local_sem.at[n])
        for n, (src, dst) in enumerate(zip(held, staged))
    ]
    for k in range(4):
        size = p.shard_rows[k]
        mine = full[k].at[pl.ds(aligned(me * size, 16), size)]
        loads.append(pltpu.make_async_copy(shards[k], mine, local_sem.at[13 + k]))
    for copy in loads:
        copy.start()

    barrier = pltpu.get_barrier_semaphore()
    peers = [(lax.rem(row + s, rows_total), z) for s in range(1, rows_total)]
    peers += [(row, lax.rem(z + s, depth)) for s in range(1, depth)]
    peers += [(row_up, col_up), (row_down, col_down)]
    for peer in peers:
        pl.semaphore_signal(barrier, inc=1, device_id=peer, device_id_type=MESH)

    span, pitch, keep, side = p.span, p.pitch, p.keep, p.side
    slots = keep * SHIFT

    def pack(read, dst, slot_of):
        for piece, (row_list, col_at, cols) in enumerate(slot_of):
            parts = []
            for b in range(p.images):
                parts += [read(b, i, col_at, cols) for i in row_list]
                if len(row_list) * cols < slots:
                    blank = slots - len(row_list) * cols
                    parts.append(jnp.zeros((blank, p.features), jnp.float32))
            dst(piece)[...] = jnp.concatenate(parts, axis=0).astype(jnp.bfloat16)

    for copy in loads:
        copy.wait()
    head, rest = list(range(SHIFT)), list(range(SHIFT, side))
    pieces_in = [(head, SHIFT, keep), (rest, 0, SHIFT), (head, 0, SHIFT)]
    for n, source in enumerate((images, cotangent)):
        pack(
            lambda b, i, c, cols, source=source: source[i, pl.ds(c, cols), b, :],
            lambda piece, n=n: halo_in_src.at[piece, n],
            pieces_in,
        )

    vec_shard[...] = jnp.zeros_like(vec_shard)
    for k, ref in enumerate(vector_ins):
        vec_shard[k : k + 1, : p.vector_sizes[k]] = ref[...].astype(jnp.float32)
    vec_b = vec_full.at[pl.ds(aligned(me * 16, 16), 16)]
    vec_b[...] = vec_shard[...].astype(jnp.bfloat16)

    streams = [(vec_full, 16, 0, LANES)]
    for k, cuts in enumerate(p.cuts):
        width = p.widths[k] // cuts
        streams += [(full[k], p.shard_rows[k], t * width, width) for t in range(cuts)]
    pl.semaphore_wait(barrier, len(peers))

    def halo_send(n):
        targets = ((row_up, z), (row, col_up), (row_up, col_up))
        return [
            launch(
                halo_in_src.at[piece, n],
                halo_in_dst.at[piece, n],
                h_send.at[6 + 3 * n + piece],
                h_recv.at[6 + 3 * n + piece],
                device,
            )
            for piece, device in enumerate(targets)
        ]

    halo_x = halo_send(0)

    along_z = {}
    hops = {}

    def g_copy(k, slot, src, device):
        copy = launch(src, src, g_send.at[k, slot], g_recv.at[k, slot], device)
        hops[k, slot] = copy

    def block_of(k, row_at):
        ref, size, left, width = streams[k]
        rows_at = pl.ds(aligned(row_at * depth * size, 16), depth * size)
        return ref.at[rows_at, pl.ds(left, width)]

    def chip_row(chip):
        return chip * CORES + core

    def half_of(k, row_at, which):
        ref, size, left, width = streams[k]
        rows_at = pl.ds(aligned(row_at * depth * size, 16), depth * size)
        if width == LANES:
            return ref.at[rows_at, pl.ds(left, width)]
        middle = width // 2
        return ref.at[rows_at, pl.ds(left + which * middle, middle)]

    def gather_z(k):
        ref, size, left, width = streams[k]
        mine = ref.at[pl.ds(aligned(me * size, 16), size), pl.ds(left, width)]
        for s in range(1, depth):
            g_copy(k, 12 + s, mine, (row, lax.rem(z + s, depth)))

    def gather_one(k):
        for s in range(1, depth):
            hops[k, 12 + s].wait_recv()
        block = block_of(k, row)
        g_copy(k, 0, block, (x_at, z))
        g_copy(k, 1, block, (y_at, z))
        g_copy(k, 4, block, (partner_at, z))
        for later in following.get(k, ()):
            gather_z(later)

    def gather_two(k):
        single = streams[k][3] == LANES
        row_x, row_y = chip_row(chip_x), chip_row(chip_y)
        hops[k, 0].wait_recv()
        g_copy(k, 2, half_of(k, row_x, 0), (y_at, z))
        g_copy(k, 5, block_of(k, row_x), (partner_at, z))
        hops[k, 1].wait_recv()
        if not single:
            g_copy(k, 3, half_of(k, row_y, 1), (x_at, z))
        g_copy(k, 6, block_of(k, row_y), (partner_at, z))

    def gather_three(k):
        single = streams[k][3] == LANES
        row_d = chip_row(chip_d)
        hops[k, 2].wait_recv()
        g_copy(k, 7, half_of(k, row_d, 0), (partner_at, z))
        if not single:
            hops[k, 3].wait_recv()
            g_copy(k, 8, half_of(k, row_d, 1), (partner_at, z))

    def gather_end(k):
        for slot in (4, 5, 6, 7, 8):
            if (k, slot) in hops:
                hops[k, slot].wait_recv()

    VEC, Q0, Q1, Q2, PROJ, U0, U1, U2, U3, DOWN0, DOWN1 = range(11)
    following = {VEC: (PROJ,), Q0: (DOWN0,), Q1: (DOWN1,), Q2: (U0,), PROJ: (U1,)}
    following.update({DOWN0: (U2,), DOWN1: (U3,)})
    for k in (VEC, Q0, Q1, Q2):
        gather_z(k)

    window = side * side
    square[...] = jnp.full(square.shape, -1.0, jnp.float32)
    raw_index = rel_index[...].astype(jnp.float32)
    for i in range(side):
        square[i * pitch : i * pitch + side, :window] = raw_index[i * side : (i + 1) * side]
    flipped[...] = square[...].T
    index_t[...] = jnp.full(index_t.shape, -1.0, jnp.float32)
    for i in range(side):
        index_t[i * pitch : i * pitch + side, :] = flipped[i * side : (i + 1) * side, :]
    for t in range(p.stack):
        index_q[:, t * HALF : (t + 1) * HALF] = index_t[
            pl.ds(t, span // p.stack, stride=p.stack), :HALF
        ]
    tab[...] = jnp.zeros_like(tab)
    tab[: p.heads, : p.table_size] = rel_table[...]
    tab_high = tab[...].astype(jnp.bfloat16).astype(jnp.float32)
    tab_b[...] = jnp.concatenate([tab_high, tab[...] - tab_high], axis=0).astype(jnp.bfloat16)

    def bias_step(q, carry):
        wanted = index_q[pl.ds(q, 1), :]
        places = iota((p.table_rows, p.stack * HALF), 0).astype(jnp.float32)
        hot = (places == wanted).astype(jnp.float32).astype(jnp.bfloat16)
        onehot[q] = hot
        entry = dot_plain(tab_b[...], hot)
        entry = entry[: p.heads] + entry[p.heads :]
        for t in range(p.stack):
            bias_cube[:, q * p.stack + t, :HALF] = entry[:, t * HALF : (t + 1) * HALF]
        return carry

    def bias_part(first, last):
        lax.fori_loop(first, last, bias_step, 0)

    def band(local, tile, axis):
        length = lax.axis_size(axis) * side
        at = tile * side + local
        return jnp.where(at >= length - WIN, 1, 0) + jnp.where(at >= length - SHIFT, 1, 0)

    def region_of(token):
        return 3 * band(token // pitch, row, "rows") + band(lax.rem(token, pitch), z, "cols")

    key_token = iota((span, p.lanes), 0)
    query_token = lax.rem(iota((span, p.lanes), 1), span)
    allowed = (region_of(key_token) == region_of(query_token)) & (
        lax.rem(key_token, pitch) < side
    )
    def bias_end():
        for g in range(p.groups):
            parts = [bias_cube[g * p.group_heads + h][:, :span] for h in range(p.group_heads)]
            bias[g] = jnp.where(allowed, jnp.concatenate(parts, axis=1), big_negative)

    bias_part(0, span // p.stack)
    bias_end()
    gather_one(VEC)
    gather_one(Q0)
    gather_one(Q1)

    def arrive(copies, n, source, dst):
        for copy in copies:
            copy.wait_recv()

        by_row, by_col, by_both = [
            halo_in_dst[piece, n].astype(jnp.float32) for piece in range(3)
        ]
        blank = jnp.zeros((pitch - side, p.features), jnp.float32)
        for b in range(p.images):
            for i in range(side):
                if i < keep:
                    at = b * slots + SHIFT * i
                    left, right = source[i + SHIFT, SHIFT:side, b, :], by_col[at : at + SHIFT]
                else:
                    at, near = b * slots + keep * (i - keep), b * slots + SHIFT * (i - keep)
                    left, right = by_row[at : at + keep], by_both[near : near + SHIFT]
                at = b * span + i * pitch
                dst[at : at + pitch, :] = jnp.concatenate([left, right, blank], axis=0)

    def spans(body, count=None):
        lax.fori_loop(0, p.images if count is None else count, body, 0)

    def span_at(w):
        return pl.ds(aligned(w * span, 8), span)

    arrive(halo_x, 0, images, xs)

    def center(ref, dst, inv_ref):
        def body(w, carry):
            value = ref[span_at(w), :]
            mean_val = jnp.mean(value, axis=-1, keepdims=True)
            centred = value - mean_val
            inv_std = lax.rsqrt(
                jnp.mean(centred * centred, axis=-1, keepdims=True) + norm_eps
            )
            dst[span_at(w), :] = centred * inv_std
            inv_ref[span_at(w), :] = jnp.broadcast_to(inv_std, (span, LANES))
            return carry

        spans(body)

    center(xs, normed, inv)
    gather_one(Q2)
    gather_two(VEC)
    gather_two(Q0)
    gather_one(PROJ)
    gather_two(Q1)
    gather_three(VEC)
    gather_three(Q0)
    gather_one(DOWN0)
    gather_two(Q2)
    gather_two(PROJ)
    gather_three(Q1)
    gather_three(Q2)
    gather_one(DOWN1)
    halo_g = halo_send(1)
    gather_two(DOWN0)
    gather_end(VEC)

    size = p.vector_sizes[0]
    per = LANES // size
    for t in range(p.features // LANES):
        spread = (lax.rem(iota((LANES, LANES), 1), size) == iota((LANES, LANES), 0)).astype(
            jnp.float32
        ).astype(jnp.bfloat16)
        value = dot_plain(vec_full[t * per * 16 : (t + 1) * per * 16, :], spread)
        mine = iota(value.shape, 0) // 16 == iota(value.shape, 1) // size
        value = jnp.where(mine, value, 0.0)
        total = value[0:16]
        for d in range(1, per):
            total = total + value[d * 16 : (d + 1) * 16]
        vec[:, t * LANES : (t + 1) * LANES] = total
    size_up = p.vector_sizes[7]
    per_up = LANES // size_up
    for t in range(p.hidden // LANES):
        spread = (lax.rem(iota((LANES, LANES), 1), size_up) == iota((LANES, LANES), 0)).astype(
            jnp.float32
        ).astype(jnp.bfloat16)
        value = dot_plain(vec_full[t * per_up * 16 : (t + 1) * per_up * 16, :], spread)
        mine = iota(value.shape, 0) == 16 * (iota(value.shape, 1) // size_up) + 7
        value = jnp.where(mine, value, 0.0)
        up_vec[:, t * LANES : (t + 1) * LANES] = jnp.sum(value, axis=0, keepdims=True)

    def vector(k):
        return vec[k : k + 1, :]

    h_b[...] = (normed[...] * vector(0) + vector(1)).astype(jnp.bfloat16)
    for k in (Q0, Q1, Q2):
        gather_end(k)

    scale = p.head_width ** (-0.5)
    features = p.features
    for n in range(3):
        cols = slice(n * features, (n + 1) * features)
        value = dot_plain(h_b[...], full[0][:, cols])
        if n == 0:
            value = (value + vector(2)) * scale
        if n == 2:
            value = value + vector(3)
        qkv[:, cols] = value
    gather_three(PROJ)
    gather_one(U0)
    gather_two(DOWN1)
    gather_three(DOWN0)

    def expand(value):
        lane = iota(value.shape, 1) // p.head_width
        parts = [jnp.where(lane == h, value, 0.0) for h in range(p.group_heads)]
        return jnp.concatenate(parts, axis=0).astype(jnp.bfloat16)

    def fold(value):
        total = None
        for h in range(p.group_heads):
            part = value[h * span : (h + 1) * span]
            part = jnp.where(iota(part.shape, 1) // p.head_width == h, part, 0.0)
            total = part if total is None else total + part
        return total

    def lanes_at(g, third=0):
        return pl.ds(aligned(third * features + g * LANES, LANES), LANES)

    def attend(w):
        def body(g, carry):
            at = span_at(w)
            query = qkv[at, lanes_at(g, 0)]
            key = qkv[at, lanes_at(g, 1)].astype(jnp.bfloat16)
            value = qkv[at, lanes_at(g, 2)].astype(jnp.bfloat16)
            scores = dot_nt(key, expand(query)) + bias[g]
            top = jnp.max(scores, axis=0, keepdims=True)
            weight = jnp.exp(scores - top)
            prob = weight / jnp.sum(weight, axis=0, keepdims=True)
            probs[w * p.groups + g] = prob
            attn[at, lanes_at(g)] = fold(dot_tn(prob.astype(jnp.bfloat16), value))
            return carry

        lax.fori_loop(0, p.groups, body, 0, unroll=True)

    steps = {
        0: [lambda: gather_one(U1), lambda: gather_two(U0), lambda: gather_three(DOWN1)],
        1: [lambda: gather_end(PROJ), lambda: gather_one(U2), lambda: gather_two(U1)],
        2: [lambda: gather_three(U0), lambda: gather_one(U3), lambda: gather_two(U2)],
        3: [lambda: arrive(halo_g, 1, cotangent, gs), lambda: gather_three(U1)],
    }
    for w in range(p.images):
        attend(w)
        for step in steps.get(w, []):
            step()
    attn_b[...] = attn[...].astype(jnp.bfloat16)
    x1[...] = xs[...] + dot_plain(attn_b[...], full[1][...]) + vector(4)
    center(x1, normed2, inv2)
    h2_b[...] = (normed2[...] * vector(5) + vector(6)).astype(jnp.bfloat16)
    gy_b[...] = gs[...].astype(jnp.bfloat16)
    gather_two(U3)
    gather_three(U2)
    for k in (DOWN0, DOWN1):
        gather_end(k)

    ys[...] = x1[...] + vector(8)
    dh2[...] = jnp.zeros_like(dh2)
    tiles = dims[0] * dims[1]
    tile = p.hidden // tiles
    DN, UPA, UPB, PR, QA, QB, QC = range(7)
    red = [
        (which, p.shard_rows[which], left, width) for which, left, width in p.reductions
    ]
    sums[...] = jnp.zeros_like(sums)

    def core_copy(k, chip):
        which, size, left, width = red[k]
        at = (chip * CORES + (1 - core)) * depth * size
        return remote(
            grads[which].at[pl.ds(aligned(at, 16), depth * size), pl.ds(left, width)],
            core_in[k].at[chip],
            r_send.at[k, chip],
            r_recv.at[k, chip],
            (partner_at, z),
        )

    def feed(j, carry):
        at = pl.ds(aligned(j * tile, LANES), tile)
        pre = dot_plain(h2_b[...], full[2][:, at]) + up_vec[:, at]
        cdf = 0.5 * (1.0 + lax.erf(pre * root_half))
        act = (pre * cdf).astype(jnp.bfloat16)
        slope = cdf + pre * (jnp.exp(-0.5 * pre * pre) * tau_factor)
        down_rows = full[3][at, :]
        ys[...] += dot_plain(act, down_rows)
        dpre = dot_nt(gy_b[...], down_rows) * slope
        sums_up[:, at] = jnp.sum(dpre, axis=0, keepdims=True)
        dpre_low = dpre.astype(jnp.bfloat16)
        dh2[...] += dot_nt(dpre_low, full[2][:, at])
        grads[3][at, :] = dot_tn(act, gy_b[...]).astype(jnp.bfloat16)
        grads[2][:, at] = dot_tn(h2_b[...], dpre_low).astype(jnp.bfloat16)
        core_copy(DN, j).start()
        return carry

    def swap(k):
        for chip in range(tiles):
            core_copy(k, chip).start()

    first_part = tiles // 2
    ups = (U0, U1, U2, U3)
    for j in range(first_part):
        gather_end(ups[j])
        lax.fori_loop(j, j + 1, feed, 0)
    swap(UPA)

    r_hops = {}

    def r_copy(k, slot, src, dst, device):
        r_hops[k, slot] = launch(src, dst, r_send.at[k, slot], r_recv.at[k, slot], device)

    def add_into(dst, parts, width_at, width):
        count = dst.shape[0]
        step = 16 if count % 32 else 32

        def body(i, carry):
            at = pl.ds(aligned(i * step, 16), step)
            cols = pl.ds(width_at, width)
            total = dst[at, cols].astype(jnp.float32)
            for part in parts:
                total = total + part[at, :].astype(jnp.float32)
            dst[at, cols] = total.astype(jnp.bfloat16)
            return carry

        lax.fori_loop(0, count // step, body, 0)

    def reduce_core(k):
        which, size, left, width = red[k]
        middle = width // 2
        for chip in range(tiles):
            core_copy(k, chip).wait_recv()
        for chip in range(tiles):
            at = (chip * CORES + core) * depth * size
            add_into(
                core_in[k].at[chip],
                [grads[which].at[pl.ds(aligned(at, 16), depth * size), pl.ds(left, width)]],
                0,
                width,
            )
        corner = core_in[k].at[chip_d]
        r_copy(k, 4, corner.at[:, pl.ds(0, middle)], a_in[k], (y_at, z))
        r_copy(k, 5, corner.at[:, pl.ds(middle, middle)], b_in[k], (x_at, z))

    def reduce_cross(k):
        middle = red[k][3] // 2
        to_x, to_y = core_in[k].at[chip_x], core_in[k].at[chip_y]
        r_hops[k, 4].wait_recv()
        add_into(to_x, [a_in[k]], 0, middle)
        r_copy(k, 6, to_x, x_in[k], (x_at, z))
        r_hops[k, 5].wait_recv()
        add_into(to_y, [b_in[k]], middle, middle)
        r_copy(k, 7, to_y, y_in[k], (y_at, z))

    def reduce_chip(k):
        _, size, _, width = red[k]
        own = core_in[k].at[chip_own]
        r_hops[k, 6].wait_recv()
        r_hops[k, 7].wait_recv()
        add_into(own, [x_in[k], y_in[k]], 0, width)
        for s in range(1, depth):
            there = lax.rem(z + s, depth)
            r_copy(
                k,
                7 + s,
                own.at[pl.ds(aligned(there * size, 16), size)],
                z_in[k].at[s - 1],
                (row, there),
            )

    def reduce_end(k):
        which, size, left, width = red[k]
        for s in range(1, depth):
            r_hops[k, 7 + s].wait_recv()
        total = core_in[k][chip_own, pl.ds(aligned(z * size, 16), size), :].astype(jnp.float32)
        for s in range(1, depth):
            total = total + z_in[k][s - 1].astype(jnp.float32)
        out_w[which][:, left : left + width] = total

    def norm_grad(d_ref, n_ref, inv_ref, gain_at, dst, base, keep_sums):
        gain_row, bias_row = keep_sums

        def body(w, carry):
            at = span_at(w)
            d_val, n_val = d_ref[at, :], n_ref[at, :]
            scaled = d_val * vector(gain_at)
            inner = (
                scaled
                - jnp.mean(scaled, axis=-1, keepdims=True)
                - n_val * jnp.mean(scaled * n_val, axis=-1, keepdims=True)
            )
            dst[at, :] = base[at, :] + inv_ref[at, :][:, :1] * inner
            sums[gain_row : gain_row + 1, :] += jnp.sum(d_val * n_val, axis=0, keepdims=True)
            sums[bias_row : bias_row + 1, :] += jnp.sum(d_val, axis=0, keepdims=True)
            return carry

        spans(body)

    def read_span(ref):
        return lambda b, i, c, cols: ref[
            b * span + i * pitch : b * span + (i + 1) * pitch, :
        ][c : c + cols]

    first_rows, last_rows = list(range(keep)), list(range(keep, side))
    pieces_out = [(last_rows, 0, keep), (first_rows, keep, SHIFT), (last_rows, keep, SHIFT)]

    def halo_out(ref, src, dst, base):
        pack(
            read_span(ref),
            lambda piece: src.at[piece],
            pieces_out,
        )
        return [
            launch(
                src.at[piece], dst.at[piece], h_send.at[base + piece], h_recv.at[base + piece],
                device,
            )
            for piece, device in enumerate(((row_down, z), (row, col_down), (row_down, col_down)))
        ]

    def halo_land(copies, ref, dst, out):
        for copy in copies:
            copy.wait_recv()

        by_row, by_col, by_both = [dst[piece].astype(jnp.float32) for piece in range(3)]
        for b in range(p.images):
            for i in range(side):
                if i < SHIFT:
                    near, at = b * slots + SHIFT * i, b * slots + keep * i
                    left, right = by_both[near : near + SHIFT], by_row[at : at + keep]
                else:
                    k = i - SHIFT
                    near, at = b * slots + SHIFT * k, b * span + k * pitch
                    left, right = by_col[near : near + SHIFT], ref[at : at + pitch, :][:keep]
                out[i, :, b, :] = jnp.concatenate([left, right], axis=0)

    gather_three(U3)
    reduce_core(UPA)
    for j in range(first_part, tiles):
        gather_end(ups[j])
        lax.fori_loop(j, j + 1, feed, 0)
    swap(UPB)
    reduce_core(DN)
    reduce_core(UPB)
    norm_grad(dh2, normed2, inv2, 5, dx1, gs, (5, 6))
    dx1_b[...] = dx1[...].astype(jnp.bfloat16)
    dattn[...] = dot_nt(dx1_b[...], full[1][...])

    dbias[...] = jnp.zeros_like(dbias)
    dcube[...] = jnp.zeros_like(dcube)

    def attend_back(w):
        def body(g, carry):
            at = span_at(w)
            query = expand(qkv[at, lanes_at(g, 0)])
            key = qkv[at, lanes_at(g, 1)].astype(jnp.bfloat16)
            value = qkv[at, lanes_at(g, 2)].astype(jnp.bfloat16)
            grad = expand(dattn[at, lanes_at(g)])
            prob = probs[w * p.groups + g]
            dprob = dot_nt(value, grad)
            dscore = prob * (dprob - jnp.sum(prob * dprob, axis=0, keepdims=True))
            dbias[g] += dscore
            dlow = dscore.astype(jnp.bfloat16)
            dqkv[at, lanes_at(g, 2)] = dot_plain(prob.astype(jnp.bfloat16), grad)
            dqkv[at, lanes_at(g, 1)] = dot_plain(dlow, query)
            dqkv[at, lanes_at(g, 0)] = fold(dot_tn(dlow, key)) * scale
            return carry

        lax.fori_loop(0, p.groups, body, 0, unroll=True)

    back_steps = {
        1: [lambda: reduce_cross(UPA), lambda: reduce_cross(DN)],
        2: [lambda: reduce_cross(UPB)],
    }
    for w in range(p.images):
        attend_back(w)
        for step in back_steps.get(w, []):
            step()

    dqkv_b[...] = dqkv[...].astype(jnp.bfloat16)
    for n in range(3):
        cols = slice(n * features, (n + 1) * features)
        grads[0][:, cols] = dot_tn(h_b[...], dqkv_b[:, cols]).astype(jnp.bfloat16)
        swap(QA + n)
    y_copies = halo_out(ys, halo_y_src, halo_y_dst, 0)
    reduce_chip(UPA)
    for k in (QA, QB, QC):
        reduce_core(k)
    grads[1][...] = dot_tn(attn_b[...], dx1_b[...]).astype(jnp.bfloat16)
    swap(PR)
    reduce_chip(DN)
    dh1[...] = dot_nt(dqkv_b[...], full[0][...])
    norm_grad(dh1, normed, inv, 0, work, dx1, (0, 1))
    g_copies = halo_out(work, halo_g_src, halo_g_dst, 3)
    reduce_core(PR)
    for k in (QA, QB, QC):
        reduce_cross(k)
    reduce_chip(UPB)
    sums[2:3, :] = jnp.sum(dqkv[:, :features], axis=0, keepdims=True)
    sums[3:4, :] = jnp.sum(dqkv[:, 2 * features :], axis=0, keepdims=True)
    sums[4:5, :] = jnp.sum(dx1[...], axis=0, keepdims=True)
    sums[7:8, :] = jnp.sum(gs[...], axis=0, keepdims=True)

    for g in range(p.groups):
        for h in range(p.group_heads):
            dcube[g * p.group_heads + h, :, :span] = dbias[g][:, h * span : (h + 1) * span]
    dtab[...] = jnp.zeros_like(dtab)

    def table_step(q, carry):
        parts = [dcube[:, q * p.stack + t, :][:, :HALF] for t in range(p.stack)]
        value = jnp.concatenate(parts, axis=1)
        high = value.astype(jnp.bfloat16).astype(jnp.float32)
        both = jnp.concatenate([high, value - high], axis=0).astype(jnp.bfloat16)
        dtab[...] += dot_nt(both, onehot[q])
        return carry

    lax.fori_loop(0, span // p.stack, table_step, 0)
    reduce_cross(PR)

    small[...] = jnp.zeros_like(small)
    wide = small.shape[1]
    at = 0
    for k in range(8):
        for t in range(features // wide):
            small[at : at + 1, :] = sums[k : k + 1, t * wide : (t + 1) * wide]
            at += 1
    for t in range(p.hidden // wide):
        small[at : at + 1, :] = sums_up[:, t * wide : (t + 1) * wide]
        at += 1
    small[at : at + p.heads, : p.table_rows] = dtab[: p.heads] + dtab[p.heads :]
    share = small.shape[0] // dims[0] // dims[1] // dims[2]
    own_rows = pl.ds(aligned(row * share, 8), share)
    s_copies = []
    for s in range(1, dims[0] * dims[1] * dims[2]):
        there = lax.rem(row + s, rows_total)
        s_copies.append(
            launch(
                small.at[pl.ds(aligned(there * share, 8), share)],
                small_in.at[s - 1],
                s_send.at[0, s],
                s_recv.at[0, s],
                (there, z),
            )
        )
    for copy in s_copies:
        copy.wait_recv()
    total = small[own_rows, :]
    for s in range(1, dims[0] * dims[1] * dims[2]):
        total = total + small_in[s - 1]
    small_mid[...] = total
    small_z[z] = total
    s_copies = [
        launch(
            small_mid,
            small_z.at[z],
            s_send.at[1, s],
            s_recv.at[1, s],
            (row, lax.rem(z + s, depth)),
        )
        for s in range(1, depth)
    ]
    for k in (QA, QB, QC, PR):
        reduce_chip(k)
    reduce_end(UPA)
    reduce_end(DN)
    for copy in s_copies:
        copy.wait_recv()
    total = small_z[0]
    for s in range(1, depth):
        total = total + small_z[s]
    small_out[own_rows, :] = total
    s_copies = [
        launch(
            small_out.at[own_rows],
            small_out.at[own_rows],
            s_send.at[2, s],
            s_recv.at[2, s],
            (lax.rem(row + s, rows_total), z),
        )
        for s in range(1, dims[0] * dims[1] * dims[2])
    ]
    halo_land(y_copies, ys, halo_y_dst, out_y)
    reduce_end(UPB)
    halo_land(g_copies, work, halo_g_dst, out_g)
    reduce_end(PR)
    for k in (QA, QB, QC):
        reduce_end(k)
    for copy in s_copies:
        copy.wait_recv()
    for k in range(7):
        for chip in range(tiles):
            core_copy(k, chip).wait_send()
    for copy in started:
        copy.wait_send()


def fused_block(dims, images, cotangent, rel_index, rel_table, weights, vectors):
    images, cotangent = images.transpose(1, 2, 0, 3), cotangent.transpose(1, 2, 0, 3)
    rel_table = rel_table.T
    p = Plan(dims, images, rel_table, weights, vectors)
    f32, bf16 = jnp.float32, jnp.bfloat16
    rows, feats, hidden, span = p.rows, p.features, p.hidden, p.span
    tiles, depth, plane = dims[0] * dims[1], p.depth, dims[0] * dims[1] * dims[2]
    wide = 2 * LANES
    small_rows = (8 * feats + hidden) // wide + p.heads
    small_rows = -(-small_rows // (8 * plane)) * 8 * plane

    def v(*shape, dtype=f32):
        return pltpu.VMEM(shape, dtype)

    scratch = [
        v(16, LANES),
        v(p.devices * 16, LANES, dtype=bf16),
        v(16, feats),
        v(1, hidden),
        v(rows, feats),
        v(rows, feats),
        v(rows, feats),
        v(rows, LANES),
        v(rows, feats, dtype=bf16),
        v(rows, 3 * feats),
        v(p.images * p.groups, span, p.lanes),
        v(rows, feats),
        v(rows, feats, dtype=bf16),
        v(rows, feats),
        v(rows, feats),
        v(rows, LANES),
        v(rows, feats, dtype=bf16),
        v(rows, feats, dtype=bf16),
        v(8, LANES),
        v(8, LANES),
        v(rows, feats),
        v(rows, feats),
        v(rows, feats),
        v(rows, feats, dtype=bf16),
        v(rows, feats),
        v(rows, 3 * feats),
        v(rows, 3 * feats, dtype=bf16),
        v(rows, feats),
        v(rows, feats),
        v(LANES, LANES),
        v(LANES, LANES),
        v(8, LANES),
        v(span, LANES),
        v(span // p.stack, p.stack * HALF),
        v(p.heads, p.table_rows),
        v(2 * p.heads, p.table_rows, dtype=bf16),
        v(span // p.stack, p.table_rows, p.stack * HALF, dtype=bf16),
        v(p.heads, span, LANES),
        v(p.groups, span, p.lanes),
        v(p.groups, span, p.lanes),
        v(p.heads, span, LANES),
        v(2 * p.heads, p.table_rows),
        v(8, feats),
        v(1, hidden),
        v(small_rows, wide),
        v(plane - 1, small_rows // plane, wide),
        v(small_rows // plane, wide),
        v(depth, small_rows // plane, wide),
    ]
    sizes = [(w.shape[0], w.shape[1]) for w in weights]
    scratch += [v(p.devices * m, n, dtype=bf16) for m, n in sizes]
    scratch += [v(p.devices * m, n, dtype=bf16) for m, n in sizes]
    turned = [(sizes[which][0], width) for which, _, width in p.reductions]
    scratch += [v(tiles, depth * m, n, dtype=bf16) for m, n in turned]
    scratch += [v(depth * m, n, dtype=bf16) for m, n in turned] * 2
    scratch += [v(depth * m, n // 2, dtype=bf16) for m, n in turned] * 2
    scratch += [v(depth - 1, m, n, dtype=bf16) for m, n in turned]
    halo_rows = p.images * SHIFT * p.keep
    scratch += [v(3, 2, halo_rows, feats, dtype=bf16)] * 2
    scratch += [v(3, halo_rows, feats, dtype=bf16)] * 4
    dma = pltpu.SemaphoreType.DMA
    scratch += [dma((11, 12 + depth))] * 2 + [dma((7, 7 + depth))] * 2
    scratch += [dma((12,))] * 2 + [dma((3, plane + depth))] * 2 + [dma((17,))]
    scratch += [v(*images.shape)] * 2 + [v(*rel_index.shape, dtype=rel_index.dtype)]
    scratch += [v(*rel_table.shape)]
    scratch += [v(1, vector.shape[0], dtype=bf16) for vector in vectors]
    out_shape = [
        jax.ShapeDtypeStruct(images.shape, f32),
        jax.ShapeDtypeStruct(images.shape, f32),
    ]
    out_shape += [jax.ShapeDtypeStruct(w.shape, f32) for w in weights]
    out_shape += [jax.ShapeDtypeStruct((small_rows, wide), f32)]
    spec = pl.BlockSpec(memory_space=pltpu.VMEM)
    outs = pl.pallas_call(
        functools.partial(block_kernel, p),
        name="block",
        out_shape=out_shape,
        in_specs=[pl.BlockSpec(memory_space=pltpu.HBM)] * 17,
        out_specs=[spec] * 7,
        scratch_shapes=scratch,
        compiler_params=pltpu.CompilerParams(
            collective_id=2, has_side_effects=True, vmem_limit_bytes=60 * 1024 * 1024
        ),
    )(
        images,
        cotangent,
        rel_index,
        rel_table,
        *[vector.reshape(1, -1) for vector in vectors],
        *weights,
    )
    sizes_small = [vector.shape[0] for vector in vectors]
    held = pl.BlockSpec(memory_space=pl.ANY)
    last_shape = [jax.ShapeDtypeStruct(out.shape, f32) for out in outs[:6]]
    last_shape += [jax.ShapeDtypeStruct((1, size), f32) for size in sizes_small]
    last_shape += [jax.ShapeDtypeStruct((p.heads, p.table_size), f32)]
    last = pl.pallas_call(
        functools.partial(emit_kernel, p, sizes_small),
        name="emit",
        out_shape=last_shape,
        in_specs=[spec] * 7,
        out_specs=[held] * 6 + [spec] * 10,
        scratch_shapes=[dma((6,))],
        compiler_params=pltpu.CompilerParams(vmem_limit_bytes=60 * 1024 * 1024),
    )(*outs)
    tokens = [out.transpose(2, 0, 1, 3) for out in last[:2]]
    vector_outs = [out.reshape(-1) for out in last[6:15]]
    return (*tokens, *last[2:6], *vector_outs, last[15].T)


def emit_kernel(plan, sizes, *refs):
    p = plan
    big, small, big_out = refs[:6], refs[6], refs[7:13]
    vector_outs, table_out, sems = refs[13:22], refs[22], refs[23]
    copies = [pltpu.make_async_copy(big[k], big_out[k], sems.at[k]) for k in range(6)]
    for copy in copies:
        copy.start()
    wide = small.shape[1]
    me = lax.axis_index("rows") * p.depth + lax.axis_index("cols")
    size, size_up = sizes[0], sizes[7]
    per = p.features // wide
    line, turn = me * size // wide, lax.rem(me * size, wide)
    lines = jnp.concatenate([small[pl.ds(k * per + line, 1), :] for k in range(8)], axis=0)
    lines = pltpu.roll(lines, wide - turn, 1)
    for k in range(9):
        if k != 7:
            at = k if k < 7 else 7
            vector_outs[k][...] = lines[at : at + 1, :size]
    line, turn = me * size_up // wide, lax.rem(me * size_up, wide)
    up = small[pl.ds(8 * per + line, 1), :]
    up = pltpu.roll(jnp.broadcast_to(up, (8, wide)), wide - turn, 1)
    vector_outs[7][...] = up[:1, :size_up]
    at = 8 * per + p.hidden // wide
    table_out[...] = small[at : at + p.heads, : p.table_size]
    for copy in copies:
        copy.wait()


def per_device(images, cotangent, rel_index, rel_table, *params):
    dims = sizes_here()
    weights, vectors = params[:4], params[4:]
    if fits_fused(dims, images, weights, vectors):
        return fused_block(dims, images, cotangent, rel_index, rel_table, weights, vectors)
    return plain_block(images, cotangent, rel_index, rel_table, *params)


def solution(mesh):
    in_specs = (
        P(None, "rows", "cols", None),
        P(None, "rows", "cols", None),
        P(),
        P(),
        P(("rows", "cols"), None),
        P(("rows", "cols"), None),
        P(("rows", "cols"), None),
        P(("rows", "cols"), None),
        P(("rows", "cols")),
        P(("rows", "cols")),
        P(("rows", "cols")),
        P(("rows", "cols")),
        P(("rows", "cols")),
        P(("rows", "cols")),
        P(("rows", "cols")),
        P(("rows", "cols")),
        P(("rows", "cols")),
    )
    out_specs = (
        P(None, "rows", "cols", None),
        P(None, "rows", "cols", None),
        P(("rows", "cols"), None),
        P(("rows", "cols"), None),
        P(("rows", "cols"), None),
        P(("rows", "cols"), None),
        P(("rows", "cols")),
        P(("rows", "cols")),
        P(("rows", "cols")),
        P(("rows", "cols")),
        P(("rows", "cols")),
        P(("rows", "cols")),
        P(("rows", "cols")),
        P(("rows", "cols")),
        P(("rows", "cols")),
        P(),
    )
    return jax.shard_map(
        per_device, mesh=mesh, in_specs=in_specs, out_specs=out_specs, check_vma=False
    )
```

```python
import functools

import jax
import jax.numpy as jnp
from jax import lax
from jax.experimental import pallas as pl
from jax.experimental.pallas import tpu as pltpu
from jax.sharding import PartitionSpec as P

WIN = 7
SHIFT = 3


norm_eps = 1e-05
root_half = 0.7071067811865476
tau_factor = 0.3989422804014327
big_negative = -1e30


def shifted(array, axis, by):
    length = lax.axis_size(axis)
    return lax.ppermute(array, axis, [(i, (i + by) % length) for i in range(length)])


def as_sent(array):

    def short(part):
        return part.astype(jnp.bfloat16) if part.dtype == jnp.float32 else part

    return jax.tree.map(short, array)


def layer_norm(values, gain_vec, offset):
    mean_val = jnp.mean(values, axis=-1, keepdims=True)
    centred = values - mean_val
    inv_std = lax.rsqrt(jnp.mean(centred * centred, axis=-1, keepdims=True) + norm_eps)
    normed = centred * inv_std
    return (normed * gain_vec + offset, normed, inv_std)


def norm_back(grad_out, normed, inv_std, gain_vec):
    scaled = grad_out * gain_vec
    row_inner = (
        scaled
        - jnp.mean(scaled, axis=-1, keepdims=True)
        - normed * jnp.mean(scaled * normed, axis=-1, keepdims=True)
    )
    return (inv_std * row_inner, jnp.sum(grad_out * normed, axis=0), jnp.sum(grad_out, axis=0))


def dot_plain(former, latter):
    return jnp.dot(former, latter, preferred_element_type=jnp.float32)


def dot_lead(former, latter):
    return lax.dot_general(
        former, latter, (((0,), (0,)), ((), ())), preferred_element_type=jnp.float32
    )


def dot_tail(former, latter):
    return lax.dot_general(
        former, latter, (((1,), (1,)), ((), ())), preferred_element_type=jnp.float32
    )


def band_of(positions, length):
    return (positions >= length - WIN).astype(jnp.int32) + (positions >= length - SHIFT).astype(
        jnp.int32
    )


def roll_in(images, cotangent):
    from_below = shifted((images[:, :SHIFT], cotangent[:, :SHIFT]), "rows", -1)
    tall_tokens = jnp.concatenate([images[:, SHIFT:], from_below[0]], axis=1)
    tall_grads = jnp.concatenate([cotangent[:, SHIFT:], from_below[1]], axis=1)
    beside = shifted((tall_tokens[:, :, :SHIFT], tall_grads[:, :, :SHIFT]), "cols", -1)
    return (
        jnp.concatenate([tall_tokens[:, :, SHIFT:], beside[0]], axis=2),
        jnp.concatenate([tall_grads[:, :, SHIFT:], beside[1]], axis=2),
    )


def roll_out(result, grad_tokens):
    from_above = (
        shifted(result[:, -SHIFT:].astype(jnp.bfloat16), "rows", 1).astype(jnp.float32),
        shifted(grad_tokens[:, -SHIFT:].astype(jnp.bfloat16), "rows", 1).astype(jnp.float32),
    )
    tall_result = jnp.concatenate([from_above[0], result[:, :-SHIFT]], axis=1)
    tall_grads = jnp.concatenate([from_above[1], grad_tokens[:, :-SHIFT]], axis=1)
    beside = (
        shifted(tall_result[:, :, -SHIFT:].astype(jnp.bfloat16), "cols", 1).astype(jnp.float32),
        shifted(as_sent(tall_grads[:, :, -SHIFT:]), "cols", 1),
    )
    return (
        jnp.concatenate([beside[0], tall_result[:, :, :-SHIFT]], axis=2),
        jnp.concatenate([beside[1], tall_grads[:, :, :-SHIFT]], axis=2),
    )


MESH = pl.DeviceIdType.MESH
CORES = 2


def grid_of(rows):
    chips = rows // CORES
    across = 1
    for size in range(1, chips + 1):
        if chips % size == 0 and size * size <= chips:
            across = size
    return chips // across, across


def whereabouts(dims):
    height, width = dims[0], dims[1]
    row, depth_at = lax.axis_index("rows"), lax.axis_index("cols")
    core = lax.rem(row, CORES)
    chip = row // CORES
    return chip // width, lax.rem(chip, width), core, depth_at


def device_at(dims, y, x, core, z):
    return ((y * dims[1] + x) * CORES + core, z)


def greet(dims, here):
    barrier = pltpu.get_barrier_semaphore()
    total = 0
    for axis in range(4):
        for step in range(1, dims[axis]):
            there = list(here)
            there[axis] = lax.rem(here[axis] + step, dims[axis])
            pl.semaphore_signal(
                barrier, inc=1, device_id=device_at(dims, *there), device_id_type=MESH
            )
            total += 1
    pl.semaphore_wait(barrier, total)


def moved(here, axis, step, dims):
    there = list(here)
    there[axis] = lax.rem(here[axis] + step, dims[axis])
    return there


def gather_kernel(dims, count, *refs):
    ins, outs = refs[:count], refs[count : 2 * count]
    local_sem, send_sem, recv_sem = refs[2 * count :]
    height, width, _, depth = dims
    here = whereabouts(dims)
    y, x, core, z = here
    greet(dims, here)
    used = [0] * count

    def send(stream, src, dst, there):
        slot = used[stream]
        used[stream] += 1
        copy = pltpu.make_async_remote_copy(
            src_ref=src,
            dst_ref=dst,
            send_sem=send_sem.at[stream, slot],
            recv_sem=recv_sem.at[stream, slot],
            device_id=device_at(dims, *there),
            device_id_type=MESH,
        )
        copy.start()
        return copy

    started = []
    along_z, locals_ = [], []
    for k in range(count):
        mine = pltpu.make_async_copy(ins[k], outs[k].at[y, x, core, z], local_sem.at[k])
        mine.start()
        locals_.append(mine)
        along_z.append(
            [
                send(k, ins[k], outs[k].at[y, x, core, z], moved(here, 3, step, dims))
                for step in range(1, depth)
            ]
        )
        started += along_z[k]
    first, second, partner = [], [], []
    other = moved(here, 2, 1, dims)
    for k in range(count):
        locals_[k].wait()
        for copy in along_z[k]:
            copy.wait_recv()
        axis = k % 2
        block = outs[k].at[y, x, core]
        first.append(
            [send(k, block, block, moved(here, axis, s, dims)) for s in range(1, dims[axis])]
        )
        partner.append([send(k, block, block, other)])
        started += first[k] + partner[k]
    for k in range(count):
        axis = k % 2
        cross = 1 - axis
        for copy in first[k]:
            copy.wait_recv()
        copies = []
        for lag in range(dims[axis]):
            at = moved(here, axis, lag, dims)
            block = outs[k].at[at[0], at[1], core]
            copies += [
                send(k, block, block, moved(here, cross, s, dims)) for s in range(1, dims[cross])
            ]
            if lag:
                partner[k].append(send(k, block, block, other))
                started.append(partner[k][-1])
        second.append(copies)
        started += copies
    for k in range(count):
        axis = k % 2
        cross = 1 - axis
        copies = iter(second[k])
        for lag in range(dims[axis]):
            for s in range(1, dims[cross]):
                next(copies).wait_recv()
                at = moved(here, axis, lag, dims)
                at[cross] = lax.rem(here[cross] + dims[cross] - s, dims[cross])
                block = outs[k].at[at[0], at[1], core]
                partner[k].append(send(k, block, block, other))
                started.append(partner[k][-1])
    for k in range(count):
        for copy in partner[k]:
            copy.wait_recv()
    for copy in started:
        copy.wait_send()


def reduce_kernel(dims, count, *refs):
    ins, table = refs[:count], refs[count]
    outs, table_out = refs[count + 1 : 2 * count + 1], refs[2 * count + 1]
    rest = refs[2 * count + 2 :]
    bufs = [rest[7 * k : 7 * k + 7] for k in range(count)]
    table_in = rest[7 * count : 7 * count + 4]
    table_sum = rest[7 * count + 4 : 7 * count + 7]
    send_sem, recv_sem = rest[7 * count + 7 :]
    height, width, _, depth = dims
    here = whereabouts(dims)
    y, x, core, z = here
    greet(dims, here)
    used = [0] * (count + 1)
    started = []

    def send(stream, src, dst, there):
        slot = used[stream]
        used[stream] += 1
        copy = pltpu.make_async_remote_copy(
            src_ref=src,
            dst_ref=dst,
            send_sem=send_sem.at[stream, slot],
            recv_sem=recv_sem.at[stream, slot],
            device_id=device_at(dims, *there),
            device_id_type=MESH,
        )
        copy.start()
        started.append(copy)
        return copy

    def add(dst, parts):
        def body(i, carry):
            total = parts[0][i].astype(jnp.float32)
            for part in parts[1:]:
                total = total + part[i].astype(jnp.float32)
            dst[i] = total.astype(dst.dtype)
            return carry

        lax.fori_loop(0, depth, body, 0)

    def table_step(stage, axis, src):
        table_in[stage][here[axis]] = src[...]
        return [
            send(count, src, table_in[stage].at[here[axis]], moved(here, axis, s, dims))
            for s in range(1, dims[axis])
        ]

    def table_add(stage, axis, copies, dst):
        for copy in copies:
            copy.wait_recv()
        total = table_in[stage][0]
        for j in range(1, dims[axis]):
            total = total + table_in[stage][j]
        dst[...] = total

    other = moved(here, 2, 1, dims)
    table_copies = table_step(0, 2, table)
    core_copies = []
    for k in range(count):
        axis = k % 2
        cross = 1 - axis
        group = {}
        for lag in list(range(1, dims[axis])) + [0]:
            for j in range(dims[cross]):
                at = moved(here, axis, lag, dims)
                at[cross] = j
                group[lag, j] = send(
                    k, ins[k].at[at[0], at[1], other[2]], bufs[k][0].at[at[0], at[1]], other
                )
        core_copies.append(group)
    table_add(0, 2, table_copies, table_sum[0])
    table_copies = table_step(1, 0, table_sum[0])
    first = []
    for k in range(count):
        axis = k % 2
        cross = 1 - axis
        from_core, sum_core, from_first = bufs[k][0], bufs[k][1], bufs[k][2]
        group = []
        for lag in list(range(1, dims[axis])) + [0]:
            for j in range(dims[cross]):
                at = moved(here, axis, lag, dims)
                at[cross] = j
                core_copies[k][lag, j].wait_recv()
                block = sum_core.at[at[0], at[1]]
                add(block, [ins[k].at[at[0], at[1], core], from_core.at[at[0], at[1]]])
                if lag:
                    group.append(
                        send(k, block, from_first.at[lag - 1, j], moved(here, axis, lag, dims))
                    )
        first.append(group)
    table_add(1, 0, table_copies, table_sum[1])
    table_copies = table_step(2, 1, table_sum[1])
    second = []
    for k in range(count):
        axis = k % 2
        cross = 1 - axis
        sum_core, from_first, sum_first, from_second = bufs[k][1:5]
        for copy in first[k]:
            copy.wait_recv()
        group = []
        for lag in list(range(1, dims[cross])) + [0]:
            at = moved(here, cross, lag, dims)
            j = at[cross]
            block = sum_first.at[j]
            add(
                block,
                [sum_core.at[at[0], at[1]]]
                + [from_first.at[s - 1, j] for s in range(1, dims[axis])],
            )
            if lag:
                group.append(send(k, block, from_second.at[lag - 1], at))
        second.append(group)
    table_add(2, 1, table_copies, table_sum[2])
    table_copies = table_step(3, 3, table_sum[2])
    third = []
    for k in range(count):
        axis = k % 2
        cross = 1 - axis
        sum_first, from_second, sum_second, from_third = bufs[k][3:7]
        for copy in second[k]:
            copy.wait_recv()
        add(
            sum_second,
            [sum_first.at[here[cross]]] + [from_second.at[s - 1] for s in range(1, dims[cross])],
        )
        group = []
        for step in range(1, depth):
            at = moved(here, 3, step, dims)
            group.append(send(k, sum_second.at[at[3]], from_third.at[step - 1], at))
        third.append(group)
    table_add(3, 3, table_copies, table_out)
    for k in range(count):
        sum_second, from_third = bufs[k][5:7]
        for copy in third[k]:
            copy.wait_recv()
        total = sum_second[z].astype(jnp.float32)
        for step in range(1, depth):
            total = total + from_third[step - 1].astype(jnp.float32)
        outs[k][...] = total
    for copy in started:
        copy.wait_send()


def sizes_here():
    rows, depth = lax.axis_size("rows"), lax.axis_size("cols")
    height, width = grid_of(rows)
    return height, width, CORES, depth


def blocked(rows, columns):
    if rows % 16 == 0:
        return rows, columns
    return rows * columns // 128, 128


def gather_all(shards):
    dims = sizes_here()
    height, width, cores, depth = dims
    count = len(shards)
    blocks = [blocked(*shard.shape) for shard in shards]
    slots = (depth - 1) + max(height, width) * 2 * height * width
    outs = pl.pallas_call(
        functools.partial(gather_kernel, dims, count),
        name="gather_all",
        out_shape=[
            jax.ShapeDtypeStruct(dims + block, shard.dtype)
            for block, shard in zip(blocks, shards)
        ],
        in_specs=[pl.BlockSpec(memory_space=pltpu.VMEM)] * count,
        out_specs=[pl.BlockSpec(memory_space=pl.ANY)] * count,
        scratch_shapes=[
            pltpu.SemaphoreType.DMA((count,)),
            pltpu.SemaphoreType.DMA((count, slots)),
            pltpu.SemaphoreType.DMA((count, slots)),
        ],
        compiler_params=pltpu.CompilerParams(collective_id=0, has_side_effects=True),
    )(*[shard.reshape(block) for block, shard in zip(blocks, shards)])
    total = height * width * cores * depth
    return [
        out.reshape(total * shard.shape[0], shard.shape[1]) for out, shard in zip(outs, shards)
    ]


def reduce_all(wholes, table):
    dims = sizes_here()
    height, width, cores, depth = dims
    total = height * width * cores * depth
    count = len(wholes)
    shares = [(whole.shape[0] // total, whole.shape[1]) for whole in wholes]
    blocks = [blocked(*share) for share in shares]
    scratch = []
    for k, (block, whole) in enumerate(zip(blocks, wholes)):
        along, cross = dims[k % 2], dims[1 - k % 2]
        for lead in (
            (height, width, depth),
            (height, width, depth),
            (max(along - 1, 1), cross, depth),
            (cross, depth),
            (max(cross - 1, 1), depth),
            (depth,),
            (max(depth - 1, 1),),
        ):
            scratch.append(pltpu.VMEM(lead + block, whole.dtype))
    for size in (cores, height, width, depth):
        scratch.append(pltpu.VMEM((size,) + table.shape, table.dtype))
    scratch += [pltpu.VMEM(table.shape, table.dtype)] * 3
    slots = 2 * height * width + height + width + depth
    scratch += [pltpu.SemaphoreType.DMA((count + 1, slots))] * 2
    outs = pl.pallas_call(
        functools.partial(reduce_kernel, dims, count),
        name="reduce_all",
        out_shape=[jax.ShapeDtypeStruct(block, jnp.float32) for block in blocks]
        + [jax.ShapeDtypeStruct(table.shape, table.dtype)],
        in_specs=[pl.BlockSpec(memory_space=pltpu.VMEM)] * (count + 1),
        out_specs=[pl.BlockSpec(memory_space=pltpu.VMEM)] * (count + 1),
        scratch_shapes=scratch,
        compiler_params=pltpu.CompilerParams(collective_id=1, has_side_effects=True),
    )(*[whole.reshape(dims + block) for block, whole in zip(blocks, wholes)], table)
    return [out.reshape(share) for out, share in zip(outs, shares)], outs[-1]


def padded(values, multiple):
    size = values.shape[-1]
    extra = -size % multiple
    return jnp.pad(values, [(0, 0)] * (values.ndim - 1) + [(0, extra)])


def plain_block(
    images,
    cotangent,
    rel_index,
    rel_table,
    qkv_weight,
    proj_weight,
    up_weight,
    down_weight,
    norm1_gain,
    norm1_bias,
    query_bias,
    value_bias,
    proj_bias,
    norm2_gain,
    norm2_bias,
    up_bias,
    down_bias,
):
    shards = (
        norm1_gain,
        norm1_bias,
        query_bias,
        value_bias,
        proj_bias,
        norm2_gain,
        norm2_bias,
        up_bias,
        down_bias,
    )
    vector_shard = padded(jnp.concatenate(shards)[None], 2048).reshape(-1, 128)
    qkv_full, down_full, up_full, proj_full, vector_full = gather_all(
        [qkv_weight, down_weight, up_weight, proj_weight, vector_shard]
    )
    device_count = lax.axis_size("rows") * lax.axis_size("cols")
    vector_full = vector_full.reshape(device_count, -1)
    vectors, offset = [], 0
    for shard in shards:
        size = shard.shape[0]
        vectors.append(vector_full[:, offset : offset + size].reshape(device_count * size))
        offset += size
    (
        gain_one_full,
        bias_one_full,
        query_add,
        value_add,
        proj_add,
        gain_two_full,
        bias_two_full,
        up_add,
        down_add,
    ) = vectors
    tokens_tile, grad_tile = roll_in(images, cotangent)
    image_count, tile_side, features = (
        tokens_tile.shape[0],
        tokens_tile.shape[1],
        tokens_tile.shape[3],
    )
    window = tile_side * tile_side
    row_total = image_count * window
    tokens = tokens_tile.reshape(row_total, features)
    grad_rows = grad_tile.reshape(row_total, features)
    local_pos = jnp.arange(tile_side, dtype=jnp.int32)
    band_rows = band_of(
        lax.axis_index("rows") * tile_side + local_pos, lax.axis_size("rows") * tile_side
    )
    band_cols = band_of(
        lax.axis_index("cols") * tile_side + local_pos, lax.axis_size("cols") * tile_side
    )
    region = (3 * band_rows[:, None] + band_cols[None, :]).reshape(window)
    allowed = (region[:, None] == region[None, :])[None, None]
    head_count = rel_table.shape[1]
    table_size = rel_table.shape[0]
    head_width = features // head_count
    score_scale = head_width ** (-0.5)
    onehot = (
        rel_index.reshape(window * window)[:, None]
        == jnp.arange(table_size, dtype=jnp.int32)[None, :]
    ).astype(jnp.float32)
    bias_flat = jnp.dot(
        onehot, rel_table, precision=lax.Precision.HIGHEST, preferred_element_type=jnp.float32
    )
    bias_heads = bias_flat.T.reshape(head_count, window, window)

    def split_heads(values):
        return values.reshape(image_count, window, head_count, head_width)

    def scores_of(query_b, key_b):
        raw_scores = jnp.einsum(
            "wqhd,wkhd->whqk",
            split_heads(query_b),
            split_heads(key_b),
            preferred_element_type=jnp.float32,
        )
        return jnp.where(allowed, raw_scores + bias_heads[None], big_negative)

    gain_one = gain_one_full.astype(jnp.float32)
    gain_two = gain_two_full.astype(jnp.float32)
    out_one, normed_one, inv_one = layer_norm(tokens, gain_one, bias_one_full.astype(jnp.float32))
    h_one = out_one.astype(jnp.bfloat16)
    projected = dot_plain(h_one, qkv_full)
    query_b = ((projected[:, :features] + query_add.astype(jnp.float32)) * score_scale).astype(
        jnp.bfloat16
    )
    key_b = projected[:, features : 2 * features].astype(jnp.bfloat16)
    value_b = (projected[:, 2 * features :] + value_add.astype(jnp.float32)).astype(jnp.bfloat16)
    scores = scores_of(query_b, key_b)
    row_top = jnp.max(scores, axis=-1, keepdims=True)
    log_total = row_top + jnp.log(jnp.sum(jnp.exp(scores - row_top), axis=-1, keepdims=True))
    attend_b = jnp.exp(scores - log_total).astype(jnp.bfloat16)
    attn_b = (
        jnp.einsum(
            "whqk,wkhd->wqhd", attend_b, split_heads(value_b), preferred_element_type=jnp.float32
        )
        .reshape(row_total, features)
        .astype(jnp.bfloat16)
    )
    residual = tokens + dot_plain(attn_b, proj_full) + proj_add.astype(jnp.float32)
    out_two, normed_two, inv_two = layer_norm(residual, gain_two, bias_two_full.astype(jnp.float32))
    h_two = out_two.astype(jnp.bfloat16)
    hidden_pre = dot_plain(h_two, up_full) + up_add.astype(jnp.float32)
    gauss_cdf = 0.5 * (1.0 + lax.erf(hidden_pre * root_half))
    act_b = (hidden_pre * gauss_cdf).astype(jnp.bfloat16)
    result = residual + dot_plain(act_b, down_full) + down_add.astype(jnp.float32)
    grad_b = grad_rows.astype(jnp.bfloat16)
    grad_down = dot_lead(act_b, grad_b)
    grad_down_add = jnp.sum(grad_rows, axis=0)
    grad_act = dot_tail(grad_b, down_full)
    density = jnp.exp(-0.5 * hidden_pre * hidden_pre) * tau_factor
    grad_pre = grad_act * (gauss_cdf + hidden_pre * density)
    grad_pre_b = grad_pre.astype(jnp.bfloat16)
    grad_up = dot_lead(h_two, grad_pre_b)
    grad_up_add = jnp.sum(grad_pre, axis=0)
    grad_h_two = dot_tail(grad_pre_b, up_full)
    grad_resid, grad_gain_two, grad_bias_two = norm_back(
        grad_h_two, normed_two, inv_two, gain_two
    )
    grad_resid = grad_resid + grad_rows
    grad_resid_b = grad_resid.astype(jnp.bfloat16)
    grad_proj = dot_lead(attn_b, grad_resid_b)
    grad_proj_add = jnp.sum(grad_resid, axis=0)
    grad_attn_b = dot_tail(grad_resid_b, proj_full).astype(jnp.bfloat16)
    grad_heads = split_heads(grad_attn_b)
    grad_attend = jnp.einsum(
        "wqhd,wkhd->whqk", grad_heads, split_heads(value_b), preferred_element_type=jnp.float32
    )
    attend = jnp.exp(scores_of(query_b, key_b) - log_total)
    grad_value = jnp.einsum(
        "whqk,wqhd->wkhd",
        attend.astype(jnp.bfloat16),
        grad_heads,
        preferred_element_type=jnp.float32,
    ).reshape(row_total, features)
    row_inner = jnp.sum(attend * grad_attend, axis=-1, keepdims=True)
    grad_scores = attend * (grad_attend - row_inner)
    grad_bias_heads = jnp.sum(grad_scores, axis=0).reshape(head_count, window * window)
    table_local = lax.dot_general(
        onehot,
        grad_bias_heads,
        (((0,), (1,)), ((), ())),
        precision=lax.Precision.HIGHEST,
        preferred_element_type=jnp.float32,
    )
    grad_scores_b = grad_scores.astype(jnp.bfloat16)
    grad_query = (
        jnp.einsum(
            "whqk,wkhd->wqhd", grad_scores_b, split_heads(key_b), preferred_element_type=jnp.float32
        )
        * score_scale
    ).reshape(row_total, features)
    grad_key = jnp.einsum(
        "whqk,wqhd->wkhd", grad_scores_b, split_heads(query_b), preferred_element_type=jnp.float32
    ).reshape(row_total, features)
    grad_query_add = jnp.sum(grad_query, axis=0)
    grad_value_add = jnp.sum(grad_value, axis=0)
    grad_mixed_b = jnp.concatenate([grad_query, grad_key, grad_value], axis=1).astype(jnp.bfloat16)
    grad_qkv = dot_lead(h_one, grad_mixed_b)
    grad_h_one = dot_tail(grad_mixed_b, qkv_full)
    grad_in, grad_gain_one, grad_bias_one = norm_back(
        grad_h_one, normed_one, inv_one, gain_one
    )
    grad_tokens = grad_resid + grad_in
    vector_grads = (
        grad_gain_one,
        grad_bias_one,
        grad_query_add,
        grad_value_add,
        grad_proj_add,
        grad_gain_two,
        grad_bias_two,
        grad_up_add,
        grad_down_add,
    )
    vector_rows = padded(
        jnp.concatenate([grad.reshape(device_count, -1) for grad in vector_grads], axis=1), 2048
    ).reshape(-1, 128)
    table_rows = padded(table_local.reshape(1, -1), 1024).reshape(-1, 128)
    (down_sum, up_sum, qkv_sum, proj_sum, vector_sum), table_sum = reduce_all(
        [
            grad_down.astype(jnp.bfloat16),
            grad_up.astype(jnp.bfloat16),
            grad_qkv.astype(jnp.bfloat16),
            grad_proj.astype(jnp.bfloat16),
            vector_rows,
        ],
        table_rows,
    )
    grad_table = table_sum.reshape(-1)[: table_local.size].reshape(table_local.shape)
    vector_sum = vector_sum.reshape(-1)
    vector_sums, offset = [], 0
    for shard in shards:
        size = shard.shape[0]
        vector_sums.append(vector_sum[offset : offset + size])
        offset += size
    shard_grads = (qkv_sum, proj_sum, up_sum, down_sum, *vector_sums)
    block_out, grad_images = roll_out(
        result.reshape(image_count, tile_side, tile_side, features),
        grad_tokens.reshape(image_count, tile_side, tile_side, features),
    )
    return (
        block_out,
        grad_images,
        shard_grads[0],
        shard_grads[1],
        shard_grads[2],
        shard_grads[3],
        shard_grads[4],
        shard_grads[5],
        shard_grads[6],
        shard_grads[7],
        shard_grads[8],
        shard_grads[9],
        shard_grads[10],
        shard_grads[11],
        shard_grads[12],
        grad_table,
    )


LANES = 128
HALF = 64


def dot_nt(former, latter):
    return lax.dot_general(
        former, latter, (((1,), (1,)), ((), ())), preferred_element_type=jnp.float32
    )


def dot_tn(former, latter):
    return lax.dot_general(
        former, latter, (((0,), (0,)), ((), ())), preferred_element_type=jnp.float32
    )


def iota(shape, dim):
    return lax.broadcasted_iota(jnp.int32, shape, dim)


def aligned(value, multiple):
    return pl.multiple_of(value, multiple)


class Plan:
    def __init__(self, dims, images, rel_table, weights, vectors):
        self.dims = dims
        self.depth = dims[3]
        self.side, _, self.images, self.features = images.shape
        self.keep = self.side - SHIFT
        self.pitch = self.side + 1
        self.span = self.side * self.pitch
        self.rows = self.images * self.span
        self.heads, self.table_size = rel_table.shape
        self.head_width = self.features // self.heads
        self.group_heads = LANES // self.head_width
        self.groups = self.features // LANES
        self.lanes = self.group_heads * self.span
        self.table_rows = -(-self.table_size // 16) * 16
        self.shard_rows = [w.shape[0] for w in weights]
        self.widths = [w.shape[1] for w in weights]
        self.devices = dims[0] * dims[1] * dims[2] * dims[3]
        self.hidden = weights[2].shape[1]
        self.stack = 4
        self.cuts = (3, 1, 4, 2)
        third, part = self.widths[0] // 3, self.hidden // 2
        self.reductions = [(3, 0, self.features), (2, 0, part), (2, part, part)]
        self.reductions += [(1, 0, self.features)]
        self.reductions += [(0, n * third, third) for n in range(3)]
        self.vector_sizes = [v.shape[0] for v in vectors]


def fits_fused(dims, images, weights, vectors):
    return (
        dims[0] == 2
        and dims[1] == 2
        and dims[2] == 2
        and dims[3] > 1
        and all(w.shape[0] % 16 == 0 for w in weights)
        and images.shape[1] == WIN
        and images.shape[2] == WIN
    )


def block_kernel(plan, *refs):
    p = plan
    take = iter(refs)

    def pull(count):
        return [next(take) for _ in range(count)]

    held = pull(13)
    shards = pull(4)
    results = pull(6)
    (small_out,) = pull(1)
    (
        vec_shard,
        vec_full,
        vec,
        up_vec,
        xs,
        gs,
        normed,
        inv,
        h_b,
        qkv,
        probs,
        attn,
        attn_b,
        x1,
        normed2,
        inv2,
        h2_b,
        gy_b,
        act_b,
        dpre_b,
        ys,
        dh2,
        dx1,
        dx1_b,
        dattn,
        dqkv,
        dqkv_b,
        dh1,
        work,
        square,
        flipped,
        flipped_pad,
        index_t,
        index_q,
        tab,
        tab_b,
        onehot,
        bias_cube,
        bias,
        dbias,
        dcube,
        dtab,
        sums,
        sums_up,
        small,
        small_in,
        small_mid,
        small_z,
    ) = pull(48)
    full = pull(4)
    grads = pull(4)
    core_in = pull(7)
    x_in, y_in, a_in, b_in, z_in = pull(7), pull(7), pull(7), pull(7), pull(7)
    halo_in_src, halo_in_dst, halo_y_src, halo_y_dst, halo_g_src, halo_g_dst = pull(6)
    g_send, g_recv, r_send, r_recv, h_send, h_recv, s_send, s_recv = pull(8)
    local_sem = next(take)
    staged = pull(13)
    images, cotangent, rel_index, rel_table = staged[:4]
    vector_ins = staged[4:]
    result_sem = next(take)
    kept = pull(6)
    out_y, out_g = kept[:2]
    out_w = kept[2:]
    writes = []

    def write(n):
        copy = pltpu.make_async_copy(kept[n], results[n], result_sem.at[n])
        copy.start()
        writes.append(copy)


    dims, depth = p.dims, p.depth
    rows_total = lax.axis_size("rows")
    row, z = lax.axis_index("rows"), lax.axis_index("cols")
    here = whereabouts(dims)
    y, x, core = here[0], here[1], here[2]
    me = row * depth + z
    partner_at = (y * dims[1] + x) * CORES + (1 - core)
    x_at = (y * dims[1] + (1 - x)) * CORES + core
    y_at = ((1 - y) * dims[1] + x) * CORES + core
    chip_own = y * dims[1] + x
    chip_x = y * dims[1] + (1 - x)
    chip_y = (1 - y) * dims[1] + x
    chip_d = (1 - y) * dims[1] + (1 - x)
    row_up, row_down = lax.rem(row + rows_total - 1, rows_total), lax.rem(row + 1, rows_total)
    col_up, col_down = lax.rem(z + depth - 1, depth), lax.rem(z + 1, depth)
    started = []

    def remote(src, dst, send_sem, recv_sem, device):
        return pltpu.make_async_remote_copy(
            src_ref=src,
            dst_ref=dst,
            send_sem=send_sem,
            recv_sem=recv_sem,
            device_id=device,
            device_id_type=MESH,
        )

    def launch(*args):
        copy = remote(*args)
        copy.start()
        started.append(copy)
        return copy

    loads = [
        pltpu.make_async_copy(src, dst, local_sem.at[n])
        for n, (src, dst) in enumerate(zip(held, staged))
    ]
    for k in range(4):
        size = p.shard_rows[k]
        mine = full[k].at[pl.ds(aligned(me * size, 16), size)]
        loads.append(pltpu.make_async_copy(shards[k], mine, local_sem.at[13 + k]))
    for copy in loads:
        copy.start()

    barrier = pltpu.get_barrier_semaphore()
    peers = [(lax.rem(row + s, rows_total), z) for s in range(1, rows_total)]
    peers += [(row, lax.rem(z + s, depth)) for s in range(1, depth)]
    peers += [(row_up, col_up), (row_down, col_down)]
    for peer in peers:
        pl.semaphore_signal(barrier, inc=1, device_id=peer, device_id_type=MESH)

    span, pitch, keep, side = p.span, p.pitch, p.keep, p.side
    slots = keep * SHIFT

    def pack(read, dst, slot_of):
        for piece, (row_list, col_at, cols) in enumerate(slot_of):
            parts = []
            for b in range(p.images):
                parts += [read(b, i, col_at, cols) for i in row_list]
                if len(row_list) * cols < slots:
                    blank = slots - len(row_list) * cols
                    parts.append(jnp.zeros((blank, p.features), jnp.float32))
            dst(piece)[...] = jnp.concatenate(parts, axis=0).astype(jnp.bfloat16)

    for copy in loads:
        copy.wait()
    head, rest = list(range(SHIFT)), list(range(SHIFT, side))
    pieces_in = [(head, SHIFT, keep), (rest, 0, SHIFT), (head, 0, SHIFT)]
    for n, source in enumerate((images, cotangent)):
        pack(
            lambda b, i, c, cols, source=source: source[i, pl.ds(c, cols), b, :],
            lambda piece, n=n: halo_in_src.at[piece, n],
            pieces_in,
        )

    vec_shard[...] = jnp.zeros_like(vec_shard)
    for k, ref in enumerate(vector_ins):
        vec_shard[k : k + 1, : p.vector_sizes[k]] = ref[...].astype(jnp.float32)
    vec_b = vec_full.at[pl.ds(aligned(me * 16, 16), 16)]
    vec_b[...] = vec_shard[...].astype(jnp.bfloat16)

    streams = [(vec_full, 16, 0, LANES)]
    for k, cuts in enumerate(p.cuts):
        width = p.widths[k] // cuts
        streams += [(full[k], p.shard_rows[k], t * width, width) for t in range(cuts)]
    pl.semaphore_wait(barrier, len(peers))

    def halo_send(n):
        targets = ((row_up, z), (row, col_up), (row_up, col_up))
        return [
            launch(
                halo_in_src.at[piece, n],
                halo_in_dst.at[piece, n],
                h_send.at[6 + 3 * n + piece],
                h_recv.at[6 + 3 * n + piece],
                device,
            )
            for piece, device in enumerate(targets)
        ]

    halo_x = halo_send(0)

    along_z = {}
    hops = {}

    def g_copy(k, slot, src, device):
        copy = launch(src, src, g_send.at[k, slot], g_recv.at[k, slot], device)
        hops[k, slot] = copy

    def block_of(k, row_at):
        ref, size, left, width = streams[k]
        rows_at = pl.ds(aligned(row_at * depth * size, 16), depth * size)
        return ref.at[rows_at, pl.ds(left, width)]

    def chip_row(chip):
        return chip * CORES + core

    def half_of(k, row_at, which):
        ref, size, left, width = streams[k]
        rows_at = pl.ds(aligned(row_at * depth * size, 16), depth * size)
        if width == LANES:
            return ref.at[rows_at, pl.ds(left, width)]
        middle = width // 2
        return ref.at[rows_at, pl.ds(left + which * middle, middle)]

    def gather_z(k):
        ref, size, left, width = streams[k]
        mine = ref.at[pl.ds(aligned(me * size, 16), size), pl.ds(left, width)]
        for s in range(1, depth):
            g_copy(k, 12 + s, mine, (row, lax.rem(z + s, depth)))

    def gather_one(k):
        for s in range(1, depth):
            hops[k, 12 + s].wait_recv()
        block = block_of(k, row)
        g_copy(k, 0, block, (x_at, z))
        g_copy(k, 1, block, (y_at, z))
        g_copy(k, 4, block, (partner_at, z))
        for later in following.get(k, ()):
            gather_z(later)

    def gather_two(k):
        single = streams[k][3] == LANES
        row_x, row_y = chip_row(chip_x), chip_row(chip_y)
        hops[k, 0].wait_recv()
        g_copy(k, 2, half_of(k, row_x, 0), (y_at, z))
        g_copy(k, 5, block_of(k, row_x), (partner_at, z))
        hops[k, 1].wait_recv()
        if not single:
            g_copy(k, 3, half_of(k, row_y, 1), (x_at, z))
        g_copy(k, 6, block_of(k, row_y), (partner_at, z))

    def gather_three(k):
        single = streams[k][3] == LANES
        row_d = chip_row(chip_d)
        hops[k, 2].wait_recv()
        g_copy(k, 7, half_of(k, row_d, 0), (partner_at, z))
        if not single:
            hops[k, 3].wait_recv()
            g_copy(k, 8, half_of(k, row_d, 1), (partner_at, z))

    def gather_end(k):
        for slot in (4, 5, 6, 7, 8):
            if (k, slot) in hops:
                hops[k, slot].wait_recv()

    VEC, Q0, Q1, Q2, PROJ, U0, U1, U2, U3, DOWN0, DOWN1 = range(11)
    following = {VEC: (PROJ,), Q0: (DOWN0,), Q1: (DOWN1,), Q2: (U0,), PROJ: (U1,)}
    following.update({DOWN0: (U2,), DOWN1: (U3,)})
    for k in (VEC, Q0, Q1, Q2):
        gather_z(k)

    window = side * side
    square[...] = jnp.full(square.shape, -1.0, jnp.float32)
    raw_index = rel_index[...].astype(jnp.float32)
    for i in range(side):
        square[i * pitch : i * pitch + side, :window] = raw_index[i * side : (i + 1) * side]
    flipped[...] = square[...].T
    index_t[...] = jnp.full(index_t.shape, -1.0, jnp.float32)
    for i in range(side):
        index_t[i * pitch : i * pitch + side, :] = flipped[i * side : (i + 1) * side, :]
    for t in range(p.stack):
        index_q[:, t * HALF : (t + 1) * HALF] = index_t[
            pl.ds(t, span // p.stack, stride=p.stack), :HALF
        ]
    tab[...] = jnp.zeros_like(tab)
    tab[: p.heads, : p.table_size] = rel_table[...]
    tab_high = tab[...].astype(jnp.bfloat16).astype(jnp.float32)
    tab_b[...] = jnp.concatenate([tab_high, tab[...] - tab_high], axis=0).astype(jnp.bfloat16)

    def bias_step(q, carry):
        wanted = index_q[pl.ds(q, 1), :]
        places = iota((p.table_rows, p.stack * HALF), 0).astype(jnp.float32)
        hot = (places == wanted).astype(jnp.float32).astype(jnp.bfloat16)
        onehot[q] = hot
        entry = dot_plain(tab_b[...], hot)
        entry = entry[: p.heads] + entry[p.heads :]
        for t in range(p.stack):
            bias_cube[:, q * p.stack + t, :HALF] = entry[:, t * HALF : (t + 1) * HALF]
        return carry

    def bias_part(first, last):
        lax.fori_loop(first, last, bias_step, 0)

    def band(local, tile, axis):
        length = lax.axis_size(axis) * side
        at = tile * side + local
        return jnp.where(at >= length - WIN, 1, 0) + jnp.where(at >= length - SHIFT, 1, 0)

    def region_of(token):
        return 3 * band(token // pitch, row, "rows") + band(lax.rem(token, pitch), z, "cols")

    key_token = iota((span, p.lanes), 0)
    query_token = lax.rem(iota((span, p.lanes), 1), span)
    allowed = (region_of(key_token) == region_of(query_token)) & (
        lax.rem(key_token, pitch) < side
    )
    def bias_end():
        for g in range(p.groups):
            parts = [bias_cube[g * p.group_heads + h][:, :span] for h in range(p.group_heads)]
            bias[g] = jnp.where(allowed, jnp.concatenate(parts, axis=1), big_negative)

    bias_part(0, span // p.stack)
    bias_end()
    gather_one(VEC)
    gather_one(Q0)
    gather_one(Q1)

    def arrive(copies, n, source, dst):
        for copy in copies:
            copy.wait_recv()

        by_row, by_col, by_both = [
            halo_in_dst[piece, n].astype(jnp.float32) for piece in range(3)
        ]
        blank = jnp.zeros((pitch - side, p.features), jnp.float32)
        for b in range(p.images):
            for i in range(side):
                if i < keep:
                    at = b * slots + SHIFT * i
                    left, right = source[i + SHIFT, SHIFT:side, b, :], by_col[at : at + SHIFT]
                else:
                    at, near = b * slots + keep * (i - keep), b * slots + SHIFT * (i - keep)
                    left, right = by_row[at : at + keep], by_both[near : near + SHIFT]
                at = b * span + i * pitch
                dst[at : at + pitch, :] = jnp.concatenate([left, right, blank], axis=0)

    def spans(body, count=None):
        lax.fori_loop(0, p.images if count is None else count, body, 0)

    def span_at(w):
        return pl.ds(aligned(w * span, 8), span)


    def center(ref, dst, inv_ref):
        def body(w, carry):
            value = ref[span_at(w), :]
            mean_val = jnp.mean(value, axis=-1, keepdims=True)
            centred = value - mean_val
            inv_std = lax.rsqrt(
                jnp.mean(centred * centred, axis=-1, keepdims=True) + norm_eps
            )
            dst[span_at(w), :] = centred * inv_std
            inv_ref[span_at(w), :] = jnp.broadcast_to(inv_std, (span, LANES))
            return carry

        spans(body)

    gather_one(Q2)
    gather_two(VEC)
    gather_two(Q0)
    arrive(halo_x, 0, images, xs)
    center(xs, normed, inv)
    gather_one(PROJ)
    gather_two(Q1)
    gather_three(VEC)
    gather_three(Q0)
    gather_one(DOWN0)
    gather_two(Q2)
    gather_two(PROJ)
    gather_three(Q1)
    gather_three(Q2)
    gather_one(DOWN1)
    halo_g = halo_send(1)
    gather_two(DOWN0)
    gather_end(VEC)

    size = p.vector_sizes[0]
    per = LANES // size
    for t in range(p.features // LANES):
        spread = (lax.rem(iota((LANES, LANES), 1), size) == iota((LANES, LANES), 0)).astype(
            jnp.float32
        ).astype(jnp.bfloat16)
        value = dot_plain(vec_full[t * per * 16 : (t + 1) * per * 16, :], spread)
        mine = iota(value.shape, 0) // 16 == iota(value.shape, 1) // size
        value = jnp.where(mine, value, 0.0)
        total = value[0:16]
        for d in range(1, per):
            total = total + value[d * 16 : (d + 1) * 16]
        vec[:, t * LANES : (t + 1) * LANES] = total
    size_up = p.vector_sizes[7]
    per_up = LANES // size_up
    for t in range(p.hidden // LANES):
        spread = (lax.rem(iota((LANES, LANES), 1), size_up) == iota((LANES, LANES), 0)).astype(
            jnp.float32
        ).astype(jnp.bfloat16)
        value = dot_plain(vec_full[t * per_up * 16 : (t + 1) * per_up * 16, :], spread)
        mine = iota(value.shape, 0) == 16 * (iota(value.shape, 1) // size_up) + 7
        value = jnp.where(mine, value, 0.0)
        up_vec[:, t * LANES : (t + 1) * LANES] = jnp.sum(value, axis=0, keepdims=True)

    def vector(k):
        return vec[k : k + 1, :]

    h_b[...] = (normed[...] * vector(0) + vector(1)).astype(jnp.bfloat16)
    for k in (Q0, Q1, Q2):
        gather_end(k)

    scale = p.head_width ** (-0.5)
    features = p.features
    for n in range(3):
        cols = slice(n * features, (n + 1) * features)
        value = dot_plain(h_b[...], full[0][:, cols])
        if n == 0:
            value = (value + vector(2)) * scale
        if n == 2:
            value = value + vector(3)
        qkv[:, cols] = value
    gather_three(PROJ)
    gather_one(U0)
    gather_two(DOWN1)
    gather_three(DOWN0)

    def expand(value):
        lane = iota(value.shape, 1) // p.head_width
        parts = [jnp.where(lane == h, value, 0.0) for h in range(p.group_heads)]
        return jnp.concatenate(parts, axis=0).astype(jnp.bfloat16)

    def fold(value):
        total = None
        for h in range(p.group_heads):
            part = value[h * span : (h + 1) * span]
            part = jnp.where(iota(part.shape, 1) // p.head_width == h, part, 0.0)
            total = part if total is None else total + part
        return total

    def lanes_at(g, third=0):
        return pl.ds(aligned(third * features + g * LANES, LANES), LANES)

    def attend(w):
        def body(g, carry):
            at = span_at(w)
            query = qkv[at, lanes_at(g, 0)]
            key = qkv[at, lanes_at(g, 1)].astype(jnp.bfloat16)
            value = qkv[at, lanes_at(g, 2)].astype(jnp.bfloat16)
            scores = dot_nt(key, expand(query)) + bias[g]
            top = jnp.max(scores, axis=0, keepdims=True)
            weight = jnp.exp(scores - top)
            prob = weight / jnp.sum(weight, axis=0, keepdims=True)
            probs[w * p.groups + g] = prob
            attn[at, lanes_at(g)] = fold(dot_tn(prob.astype(jnp.bfloat16), value))
            return carry

        lax.fori_loop(0, p.groups, body, 0, unroll=True)

    steps = {
        0: [lambda: gather_one(U1), lambda: gather_two(U0), lambda: gather_three(DOWN1)],
        1: [lambda: gather_end(PROJ), lambda: gather_one(U2), lambda: gather_two(U1)],
        2: [lambda: gather_three(U0), lambda: gather_one(U3), lambda: gather_two(U2)],
        3: [lambda: arrive(halo_g, 1, cotangent, gs), lambda: gather_three(U1)],
    }
    for w in range(p.images):
        attend(w)
        for step in steps.get(w, []):
            step()
    attn_b[...] = attn[...].astype(jnp.bfloat16)
    x1[...] = xs[...] + dot_plain(attn_b[...], full[1][...]) + vector(4)
    center(x1, normed2, inv2)
    h2_b[...] = (normed2[...] * vector(5) + vector(6)).astype(jnp.bfloat16)
    gy_b[...] = gs[...].astype(jnp.bfloat16)
    gather_two(U3)
    gather_three(U2)
    for k in (DOWN0, DOWN1):
        gather_end(k)

    ys[...] = x1[...] + vector(8)
    dh2[...] = jnp.zeros_like(dh2)
    tiles = dims[0] * dims[1]
    tile = p.hidden // tiles
    DN, UPA, UPB, PR, QA, QB, QC = range(7)
    red = [
        (which, p.shard_rows[which], left, width) for which, left, width in p.reductions
    ]
    sums[...] = jnp.zeros_like(sums)

    def core_copy(k, chip):
        which, size, left, width = red[k]
        at = (chip * CORES + (1 - core)) * depth * size
        return remote(
            grads[which].at[pl.ds(aligned(at, 16), depth * size), pl.ds(left, width)],
            core_in[k].at[chip],
            r_send.at[k, chip],
            r_recv.at[k, chip],
            (partner_at, z),
        )

    def feed(j, carry):
        at = pl.ds(aligned(j * tile, LANES), tile)
        pre = dot_plain(h2_b[...], full[2][:, at]) + up_vec[:, at]
        cdf = 0.5 * (1.0 + lax.erf(pre * root_half))
        act = (pre * cdf).astype(jnp.bfloat16)
        slope = cdf + pre * (jnp.exp(-0.5 * pre * pre) * tau_factor)
        down_rows = full[3][at, :]
        ys[...] += dot_plain(act, down_rows)
        dpre = dot_nt(gy_b[...], down_rows) * slope
        sums_up[:, at] = jnp.sum(dpre, axis=0, keepdims=True)
        dpre_low = dpre.astype(jnp.bfloat16)
        dh2[...] += dot_nt(dpre_low, full[2][:, at])
        grads[3][at, :] = dot_tn(act, gy_b[...]).astype(jnp.bfloat16)
        grads[2][:, at] = dot_tn(h2_b[...], dpre_low).astype(jnp.bfloat16)
        core_copy(DN, j).start()
        return carry

    def swap(k):
        for chip in range(tiles):
            core_copy(k, chip).start()

    first_part = tiles // 2
    ups = (U0, U1, U2, U3)
    for j in range(first_part):
        gather_end(ups[j])
        lax.fori_loop(j, j + 1, feed, 0)
    swap(UPA)

    r_hops = {}

    def r_copy(k, slot, src, dst, device):
        r_hops[k, slot] = launch(src, dst, r_send.at[k, slot], r_recv.at[k, slot], device)

    def add_into(dst, parts, width_at, width):
        count = dst.shape[0]
        step = 16 if count % 32 else 32

        def body(i, carry):
            at = pl.ds(aligned(i * step, 16), step)
            cols = pl.ds(width_at, width)
            total = dst[at, cols].astype(jnp.float32)
            for part in parts:
                total = total + part[at, :].astype(jnp.float32)
            dst[at, cols] = total.astype(jnp.bfloat16)
            return carry

        lax.fori_loop(0, count // step, body, 0)

    def reduce_core(k):
        which, size, left, width = red[k]
        middle = width // 2
        for chip in range(tiles):
            core_copy(k, chip).wait_recv()
        for chip in range(tiles):
            at = (chip * CORES + core) * depth * size
            add_into(
                core_in[k].at[chip],
                [grads[which].at[pl.ds(aligned(at, 16), depth * size), pl.ds(left, width)]],
                0,
                width,
            )
        corner = core_in[k].at[chip_d]
        r_copy(k, 4, corner.at[:, pl.ds(0, middle)], a_in[k], (y_at, z))
        r_copy(k, 5, corner.at[:, pl.ds(middle, middle)], b_in[k], (x_at, z))

    def reduce_cross(k):
        middle = red[k][3] // 2
        to_x, to_y = core_in[k].at[chip_x], core_in[k].at[chip_y]
        r_hops[k, 4].wait_recv()
        add_into(to_x, [a_in[k]], 0, middle)
        r_copy(k, 6, to_x, x_in[k], (x_at, z))
        r_hops[k, 5].wait_recv()
        add_into(to_y, [b_in[k]], middle, middle)
        r_copy(k, 7, to_y, y_in[k], (y_at, z))

    def reduce_chip(k):
        _, size, _, width = red[k]
        own = core_in[k].at[chip_own]
        r_hops[k, 6].wait_recv()
        r_hops[k, 7].wait_recv()
        add_into(own, [x_in[k], y_in[k]], 0, width)
        for s in range(1, depth):
            there = lax.rem(z + s, depth)
            r_copy(
                k,
                7 + s,
                own.at[pl.ds(aligned(there * size, 16), size)],
                z_in[k].at[s - 1],
                (row, there),
            )

    def reduce_end(k):
        which, size, left, width = red[k]
        for s in range(1, depth):
            r_hops[k, 7 + s].wait_recv()
        total = core_in[k][chip_own, pl.ds(aligned(z * size, 16), size), :].astype(jnp.float32)
        for s in range(1, depth):
            total = total + z_in[k][s - 1].astype(jnp.float32)
        out_w[which][:, left : left + width] = total

    def norm_grad(d_ref, n_ref, inv_ref, gain_at, dst, base, keep_sums):
        gain_row, bias_row = keep_sums

        def body(w, carry):
            at = span_at(w)
            d_val, n_val = d_ref[at, :], n_ref[at, :]
            scaled = d_val * vector(gain_at)
            inner = (
                scaled
                - jnp.mean(scaled, axis=-1, keepdims=True)
                - n_val * jnp.mean(scaled * n_val, axis=-1, keepdims=True)
            )
            dst[at, :] = base[at, :] + inv_ref[at, :][:, :1] * inner
            sums[gain_row : gain_row + 1, :] += jnp.sum(d_val * n_val, axis=0, keepdims=True)
            sums[bias_row : bias_row + 1, :] += jnp.sum(d_val, axis=0, keepdims=True)
            return carry

        spans(body)

    def read_span(ref):
        return lambda b, i, c, cols: ref[
            b * span + i * pitch : b * span + (i + 1) * pitch, :
        ][c : c + cols]

    first_rows, last_rows = list(range(keep)), list(range(keep, side))
    pieces_out = [(last_rows, 0, keep), (first_rows, keep, SHIFT), (last_rows, keep, SHIFT)]

    def halo_out(ref, src, dst, base):
        pack(
            read_span(ref),
            lambda piece: src.at[piece],
            pieces_out,
        )
        return [
            launch(
                src.at[piece], dst.at[piece], h_send.at[base + piece], h_recv.at[base + piece],
                device,
            )
            for piece, device in enumerate(((row_down, z), (row, col_down), (row_down, col_down)))
        ]

    def halo_land(copies, ref, dst, out):
        for copy in copies:
            copy.wait_recv()

        by_row, by_col, by_both = [dst[piece].astype(jnp.float32) for piece in range(3)]
        for b in range(p.images):
            for i in range(side):
                if i < SHIFT:
                    near, at = b * slots + SHIFT * i, b * slots + keep * i
                    left, right = by_both[near : near + SHIFT], by_row[at : at + keep]
                else:
                    k = i - SHIFT
                    near, at = b * slots + SHIFT * k, b * span + k * pitch
                    left, right = by_col[near : near + SHIFT], ref[at : at + pitch, :][:keep]
                out[i, :, b, :] = jnp.concatenate([left, right], axis=0)

    gather_three(U3)
    reduce_core(UPA)
    for j in range(first_part, tiles):
        gather_end(ups[j])
        lax.fori_loop(j, j + 1, feed, 0)
    swap(UPB)
    reduce_core(DN)
    reduce_core(UPB)
    norm_grad(dh2, normed2, inv2, 5, dx1, gs, (5, 6))
    dx1_b[...] = dx1[...].astype(jnp.bfloat16)
    dattn[...] = dot_nt(dx1_b[...], full[1][...])

    dbias[...] = jnp.zeros_like(dbias)
    dcube[...] = jnp.zeros_like(dcube)

    def attend_back(w):
        def body(g, carry):
            at = span_at(w)
            query = expand(qkv[at, lanes_at(g, 0)])
            key = qkv[at, lanes_at(g, 1)].astype(jnp.bfloat16)
            value = qkv[at, lanes_at(g, 2)].astype(jnp.bfloat16)
            grad = expand(dattn[at, lanes_at(g)])
            prob = probs[w * p.groups + g]
            dprob = dot_nt(value, grad)
            dscore = prob * (dprob - jnp.sum(prob * dprob, axis=0, keepdims=True))
            dbias[g] += dscore
            dlow = dscore.astype(jnp.bfloat16)
            dqkv[at, lanes_at(g, 2)] = dot_plain(prob.astype(jnp.bfloat16), grad)
            dqkv[at, lanes_at(g, 1)] = dot_plain(dlow, query)
            dqkv[at, lanes_at(g, 0)] = fold(dot_tn(dlow, key)) * scale
            return carry

        lax.fori_loop(0, p.groups, body, 0, unroll=True)

    back_steps = {
        1: [lambda: reduce_cross(UPA), lambda: reduce_cross(DN)],
        2: [lambda: reduce_cross(UPB)],
    }
    for w in range(p.images):
        attend_back(w)
        for step in back_steps.get(w, []):
            step()

    dqkv_b[...] = dqkv[...].astype(jnp.bfloat16)
    for n in range(3):
        cols = slice(n * features, (n + 1) * features)
        grads[0][:, cols] = dot_tn(h_b[...], dqkv_b[:, cols]).astype(jnp.bfloat16)
        swap(QA + n)
    y_copies = halo_out(ys, halo_y_src, halo_y_dst, 0)
    reduce_chip(UPA)
    for k in (QA, QB, QC):
        reduce_core(k)
    grads[1][...] = dot_tn(attn_b[...], dx1_b[...]).astype(jnp.bfloat16)
    swap(PR)
    reduce_chip(DN)
    dh1[...] = dot_nt(dqkv_b[...], full[0][...])
    norm_grad(dh1, normed, inv, 0, work, dx1, (0, 1))
    g_copies = halo_out(work, halo_g_src, halo_g_dst, 3)
    reduce_core(PR)
    for k in (QA, QB, QC):
        reduce_cross(k)
    reduce_chip(UPB)
    sums[2:3, :] = jnp.sum(dqkv[:, :features], axis=0, keepdims=True)
    sums[3:4, :] = jnp.sum(dqkv[:, 2 * features :], axis=0, keepdims=True)
    sums[4:5, :] = jnp.sum(dx1[...], axis=0, keepdims=True)
    sums[7:8, :] = jnp.sum(gs[...], axis=0, keepdims=True)

    for g in range(p.groups):
        for h in range(p.group_heads):
            dcube[g * p.group_heads + h, :, :span] = dbias[g][:, h * span : (h + 1) * span]
    dtab[...] = jnp.zeros_like(dtab)

    def table_step(q, carry):
        parts = [dcube[:, q * p.stack + t, :][:, :HALF] for t in range(p.stack)]
        value = jnp.concatenate(parts, axis=1)
        high = value.astype(jnp.bfloat16).astype(jnp.float32)
        both = jnp.concatenate([high, value - high], axis=0).astype(jnp.bfloat16)
        dtab[...] += dot_nt(both, onehot[q])
        return carry

    lax.fori_loop(0, span // p.stack, table_step, 0)
    reduce_cross(PR)

    small[...] = jnp.zeros_like(small)
    wide = small.shape[1]
    at = 0
    for k in range(8):
        for t in range(features // wide):
            small[at : at + 1, :] = sums[k : k + 1, t * wide : (t + 1) * wide]
            at += 1
    for t in range(p.hidden // wide):
        small[at : at + 1, :] = sums_up[:, t * wide : (t + 1) * wide]
        at += 1
    small[at : at + p.heads, : p.table_rows] = dtab[: p.heads] + dtab[p.heads :]
    share = small.shape[0] // dims[0] // dims[1] // dims[2]
    own_rows = pl.ds(aligned(row * share, 8), share)
    s_copies = []
    for s in range(1, dims[0] * dims[1] * dims[2]):
        there = lax.rem(row + s, rows_total)
        s_copies.append(
            launch(
                small.at[pl.ds(aligned(there * share, 8), share)],
                small_in.at[s - 1],
                s_send.at[0, s],
                s_recv.at[0, s],
                (there, z),
            )
        )
    for k in (QA, QB, QC):
        reduce_chip(k)
    for copy in s_copies:
        copy.wait_recv()
    total = small[own_rows, :]
    for s in range(1, dims[0] * dims[1] * dims[2]):
        total = total + small_in[s - 1]
    small_mid[...] = total
    small_z[z] = total
    s_copies = [
        launch(
            small_mid,
            small_z.at[z],
            s_send.at[1, s],
            s_recv.at[1, s],
            (row, lax.rem(z + s, depth)),
        )
        for s in range(1, depth)
    ]
    reduce_chip(PR)
    reduce_end(UPA)
    reduce_end(DN)
    for copy in s_copies:
        copy.wait_recv()
    total = small_z[0]
    for s in range(1, depth):
        total = total + small_z[s]
    small_out[own_rows, :] = total
    s_copies = [
        launch(
            small_out.at[own_rows],
            small_out.at[own_rows],
            s_send.at[2, s],
            s_recv.at[2, s],
            (lax.rem(row + s, rows_total), z),
        )
        for s in range(1, dims[0] * dims[1] * dims[2])
    ]
    halo_land(y_copies, ys, halo_y_dst, out_y)
    write(0)
    write(5)
    reduce_end(UPB)
    write(4)
    halo_land(g_copies, work, halo_g_dst, out_g)
    write(1)
    reduce_end(PR)
    write(3)
    for k in (QA, QB, QC):
        reduce_end(k)
    write(2)
    for copy in s_copies:
        copy.wait_recv()
    for k in range(7):
        for chip in range(tiles):
            core_copy(k, chip).wait_send()
    for copy in started:
        copy.wait_send()
    for copy in writes:
        copy.wait()


def fused_block(dims, images, cotangent, rel_index, rel_table, weights, vectors):
    images, cotangent = images.transpose(1, 2, 0, 3), cotangent.transpose(1, 2, 0, 3)
    rel_table = rel_table.T
    p = Plan(dims, images, rel_table, weights, vectors)
    f32, bf16 = jnp.float32, jnp.bfloat16
    rows, feats, hidden, span = p.rows, p.features, p.hidden, p.span
    tiles, depth, plane = dims[0] * dims[1], p.depth, dims[0] * dims[1] * dims[2]
    wide = 2 * LANES
    small_rows = (8 * feats + hidden) // wide + p.heads
    small_rows = -(-small_rows // (8 * plane)) * 8 * plane

    def v(*shape, dtype=f32):
        return pltpu.VMEM(shape, dtype)

    scratch = [
        v(16, LANES),
        v(p.devices * 16, LANES, dtype=bf16),
        v(16, feats),
        v(1, hidden),
        v(rows, feats),
        v(rows, feats),
        v(rows, feats),
        v(rows, LANES),
        v(rows, feats, dtype=bf16),
        v(rows, 3 * feats),
        v(p.images * p.groups, span, p.lanes),
        v(rows, feats),
        v(rows, feats, dtype=bf16),
        v(rows, feats),
        v(rows, feats),
        v(rows, LANES),
        v(rows, feats, dtype=bf16),
        v(rows, feats, dtype=bf16),
        v(8, LANES),
        v(8, LANES),
        v(rows, feats),
        v(rows, feats),
        v(rows, feats),
        v(rows, feats, dtype=bf16),
        v(rows, feats),
        v(rows, 3 * feats),
        v(rows, 3 * feats, dtype=bf16),
        v(rows, feats),
        v(rows, feats),
        v(LANES, LANES),
        v(LANES, LANES),
        v(8, LANES),
        v(span, LANES),
        v(span // p.stack, p.stack * HALF),
        v(p.heads, p.table_rows),
        v(2 * p.heads, p.table_rows, dtype=bf16),
        v(span // p.stack, p.table_rows, p.stack * HALF, dtype=bf16),
        v(p.heads, span, LANES),
        v(p.groups, span, p.lanes),
        v(p.groups, span, p.lanes),
        v(p.heads, span, LANES),
        v(2 * p.heads, p.table_rows),
        v(8, feats),
        v(1, hidden),
        v(small_rows, wide),
        v(plane - 1, small_rows // plane, wide),
        v(small_rows // plane, wide),
        v(depth, small_rows // plane, wide),
    ]
    sizes = [(w.shape[0], w.shape[1]) for w in weights]
    scratch += [v(p.devices * m, n, dtype=bf16) for m, n in sizes]
    scratch += [v(p.devices * m, n, dtype=bf16) for m, n in sizes]
    turned = [(sizes[which][0], width) for which, _, width in p.reductions]
    scratch += [v(tiles, depth * m, n, dtype=bf16) for m, n in turned]
    scratch += [v(depth * m, n, dtype=bf16) for m, n in turned] * 2
    scratch += [v(depth * m, n // 2, dtype=bf16) for m, n in turned] * 2
    scratch += [v(depth - 1, m, n, dtype=bf16) for m, n in turned]
    halo_rows = p.images * SHIFT * p.keep
    scratch += [v(3, 2, halo_rows, feats, dtype=bf16)] * 2
    scratch += [v(3, halo_rows, feats, dtype=bf16)] * 4
    dma = pltpu.SemaphoreType.DMA
    scratch += [dma((11, 12 + depth))] * 2 + [dma((7, 7 + depth))] * 2
    scratch += [dma((12,))] * 2 + [dma((3, plane + depth))] * 2 + [dma((17,))]
    scratch += [v(*images.shape)] * 2 + [v(*rel_index.shape, dtype=rel_index.dtype)]
    scratch += [v(*rel_table.shape)]
    scratch += [v(1, vector.shape[0], dtype=bf16) for vector in vectors]
    scratch += [dma((6,)), v(*images.shape), v(*images.shape)]
    scratch += [v(*w.shape) for w in weights]
    out_shape = [
        jax.ShapeDtypeStruct(images.shape, f32),
        jax.ShapeDtypeStruct(images.shape, f32),
    ]
    out_shape += [jax.ShapeDtypeStruct(w.shape, f32) for w in weights]
    out_shape += [jax.ShapeDtypeStruct((small_rows, wide), f32)]
    spec = pl.BlockSpec(memory_space=pltpu.VMEM)
    outs = pl.pallas_call(
        functools.partial(block_kernel, p),
        name="block",
        out_shape=out_shape,
        in_specs=[pl.BlockSpec(memory_space=pltpu.HBM)] * 17,
        out_specs=[pl.BlockSpec(memory_space=pltpu.HBM)] * 6 + [spec],
        scratch_shapes=scratch,
        compiler_params=pltpu.CompilerParams(
            collective_id=2, has_side_effects=True, vmem_limit_bytes=60 * 1024 * 1024
        ),
    )(
        images,
        cotangent,
        rel_index,
        rel_table,
        *[vector.reshape(1, -1) for vector in vectors],
        *weights,
    )
    sizes_small = [vector.shape[0] for vector in vectors]
    held = pl.BlockSpec(memory_space=pl.ANY)
    last_shape = [jax.ShapeDtypeStruct(out.shape, f32) for out in outs[:6]]
    last_shape += [jax.ShapeDtypeStruct((1, size), f32) for size in sizes_small]
    last_shape += [jax.ShapeDtypeStruct((p.heads, p.table_size), f32)]
    last = pl.pallas_call(
        functools.partial(emit_kernel, p, sizes_small),
        name="emit",
        out_shape=last_shape,
        in_specs=[spec] * 7,
        out_specs=[held] * 6 + [spec] * 10,
        scratch_shapes=[dma((6,))],
        compiler_params=pltpu.CompilerParams(vmem_limit_bytes=60 * 1024 * 1024),
    )(*outs)
    tokens = [out.transpose(2, 0, 1, 3) for out in last[:2]]
    vector_outs = [out.reshape(-1) for out in last[6:15]]
    return (*tokens, *last[2:6], *vector_outs, last[15].T)


def emit_kernel(plan, sizes, *refs):
    p = plan
    big, small, big_out = refs[:6], refs[6], refs[7:13]
    vector_outs, table_out, sems = refs[13:22], refs[22], refs[23]
    copies = [pltpu.make_async_copy(big[k], big_out[k], sems.at[k]) for k in range(6)]
    for copy in copies:
        copy.start()
    wide = small.shape[1]
    me = lax.axis_index("rows") * p.depth + lax.axis_index("cols")
    size, size_up = sizes[0], sizes[7]
    per = p.features // wide
    line, turn = me * size // wide, lax.rem(me * size, wide)
    lines = jnp.concatenate([small[pl.ds(k * per + line, 1), :] for k in range(8)], axis=0)
    lines = pltpu.roll(lines, wide - turn, 1)
    for k in range(9):
        if k != 7:
            at = k if k < 7 else 7
            vector_outs[k][...] = lines[at : at + 1, :size]
    line, turn = me * size_up // wide, lax.rem(me * size_up, wide)
    up = small[pl.ds(8 * per + line, 1), :]
    up = pltpu.roll(jnp.broadcast_to(up, (8, wide)), wide - turn, 1)
    vector_outs[7][...] = up[:1, :size_up]
    at = 8 * per + p.hidden // wide
    table_out[...] = small[at : at + p.heads, : p.table_size]
    for copy in copies:
        copy.wait()


def per_device(images, cotangent, rel_index, rel_table, *params):
    dims = sizes_here()
    weights, vectors = params[:4], params[4:]
    if fits_fused(dims, images, weights, vectors):
        return fused_block(dims, images, cotangent, rel_index, rel_table, weights, vectors)
    return plain_block(images, cotangent, rel_index, rel_table, *params)


def solution(mesh):
    in_specs = (
        P(None, "rows", "cols", None),
        P(None, "rows", "cols", None),
        P(),
        P(),
        P(("rows", "cols"), None),
        P(("rows", "cols"), None),
        P(("rows", "cols"), None),
        P(("rows", "cols"), None),
        P(("rows", "cols")),
        P(("rows", "cols")),
        P(("rows", "cols")),
        P(("rows", "cols")),
        P(("rows", "cols")),
        P(("rows", "cols")),
        P(("rows", "cols")),
        P(("rows", "cols")),
        P(("rows", "cols")),
    )
    out_specs = (
        P(None, "rows", "cols", None),
        P(None, "rows", "cols", None),
        P(("rows", "cols"), None),
        P(("rows", "cols"), None),
        P(("rows", "cols"), None),
        P(("rows", "cols"), None),
        P(("rows", "cols")),
        P(("rows", "cols")),
        P(("rows", "cols")),
        P(("rows", "cols")),
        P(("rows", "cols")),
        P(("rows", "cols")),
        P(("rows", "cols")),
        P(("rows", "cols")),
        P(("rows", "cols")),
        P(),
    )
    return jax.shard_map(
        per_device, mesh=mesh, in_specs=in_specs, out_specs=out_specs, check_vma=False
    )
```

```python
import functools

import jax
import jax.numpy as jnp
from jax import lax
from jax.experimental import pallas as pl
from jax.experimental.pallas import tpu as pltpu
from jax.sharding import PartitionSpec as P

WIN = 7
SHIFT = 3


norm_eps = 1e-05
root_half = 0.7071067811865476
tau_factor = 0.3989422804014327
big_negative = -1e30


def shifted(array, axis, by):
    length = lax.axis_size(axis)
    return lax.ppermute(array, axis, [(i, (i + by) % length) for i in range(length)])


def as_sent(array):

    def short(part):
        return part.astype(jnp.bfloat16) if part.dtype == jnp.float32 else part

    return jax.tree.map(short, array)


def layer_norm(values, gain_vec, offset):
    mean_val = jnp.mean(values, axis=-1, keepdims=True)
    centred = values - mean_val
    inv_std = lax.rsqrt(jnp.mean(centred * centred, axis=-1, keepdims=True) + norm_eps)
    normed = centred * inv_std
    return (normed * gain_vec + offset, normed, inv_std)


def norm_back(grad_out, normed, inv_std, gain_vec):
    scaled = grad_out * gain_vec
    row_inner = (
        scaled
        - jnp.mean(scaled, axis=-1, keepdims=True)
        - normed * jnp.mean(scaled * normed, axis=-1, keepdims=True)
    )
    return (inv_std * row_inner, jnp.sum(grad_out * normed, axis=0), jnp.sum(grad_out, axis=0))


def dot_plain(former, latter):
    return jnp.dot(former, latter, preferred_element_type=jnp.float32)


def dot_lead(former, latter):
    return lax.dot_general(
        former, latter, (((0,), (0,)), ((), ())), preferred_element_type=jnp.float32
    )


def dot_tail(former, latter):
    return lax.dot_general(
        former, latter, (((1,), (1,)), ((), ())), preferred_element_type=jnp.float32
    )


def band_of(positions, length):
    return (positions >= length - WIN).astype(jnp.int32) + (positions >= length - SHIFT).astype(
        jnp.int32
    )


def roll_in(images, cotangent):
    from_below = shifted((images[:, :SHIFT], cotangent[:, :SHIFT]), "rows", -1)
    tall_tokens = jnp.concatenate([images[:, SHIFT:], from_below[0]], axis=1)
    tall_grads = jnp.concatenate([cotangent[:, SHIFT:], from_below[1]], axis=1)
    beside = shifted((tall_tokens[:, :, :SHIFT], tall_grads[:, :, :SHIFT]), "cols", -1)
    return (
        jnp.concatenate([tall_tokens[:, :, SHIFT:], beside[0]], axis=2),
        jnp.concatenate([tall_grads[:, :, SHIFT:], beside[1]], axis=2),
    )


def roll_out(result, grad_tokens):
    from_above = (
        shifted(result[:, -SHIFT:].astype(jnp.bfloat16), "rows", 1).astype(jnp.float32),
        shifted(grad_tokens[:, -SHIFT:].astype(jnp.bfloat16), "rows", 1).astype(jnp.float32),
    )
    tall_result = jnp.concatenate([from_above[0], result[:, :-SHIFT]], axis=1)
    tall_grads = jnp.concatenate([from_above[1], grad_tokens[:, :-SHIFT]], axis=1)
    beside = (
        shifted(tall_result[:, :, -SHIFT:].astype(jnp.bfloat16), "cols", 1).astype(jnp.float32),
        shifted(as_sent(tall_grads[:, :, -SHIFT:]), "cols", 1),
    )
    return (
        jnp.concatenate([beside[0], tall_result[:, :, :-SHIFT]], axis=2),
        jnp.concatenate([beside[1], tall_grads[:, :, :-SHIFT]], axis=2),
    )


MESH = pl.DeviceIdType.MESH
CORES = 2


def grid_of(rows):
    chips = rows // CORES
    across = 1
    for size in range(1, chips + 1):
        if chips % size == 0 and size * size <= chips:
            across = size
    return chips // across, across


def whereabouts(dims):
    height, width = dims[0], dims[1]
    row, depth_at = lax.axis_index("rows"), lax.axis_index("cols")
    core = lax.rem(row, CORES)
    chip = row // CORES
    return chip // width, lax.rem(chip, width), core, depth_at


def device_at(dims, y, x, core, z):
    return ((y * dims[1] + x) * CORES + core, z)


def greet(dims, here):
    barrier = pltpu.get_barrier_semaphore()
    total = 0
    for axis in range(4):
        for step in range(1, dims[axis]):
            there = list(here)
            there[axis] = lax.rem(here[axis] + step, dims[axis])
            pl.semaphore_signal(
                barrier, inc=1, device_id=device_at(dims, *there), device_id_type=MESH
            )
            total += 1
    pl.semaphore_wait(barrier, total)


def moved(here, axis, step, dims):
    there = list(here)
    there[axis] = lax.rem(here[axis] + step, dims[axis])
    return there


def gather_kernel(dims, count, *refs):
    ins, outs = refs[:count], refs[count : 2 * count]
    local_sem, send_sem, recv_sem = refs[2 * count :]
    height, width, _, depth = dims
    here = whereabouts(dims)
    y, x, core, z = here
    greet(dims, here)
    used = [0] * count

    def send(stream, src, dst, there):
        slot = used[stream]
        used[stream] += 1
        copy = pltpu.make_async_remote_copy(
            src_ref=src,
            dst_ref=dst,
            send_sem=send_sem.at[stream, slot],
            recv_sem=recv_sem.at[stream, slot],
            device_id=device_at(dims, *there),
            device_id_type=MESH,
        )
        copy.start()
        return copy

    started = []
    along_z, locals_ = [], []
    for k in range(count):
        mine = pltpu.make_async_copy(ins[k], outs[k].at[y, x, core, z], local_sem.at[k])
        mine.start()
        locals_.append(mine)
        along_z.append(
            [
                send(k, ins[k], outs[k].at[y, x, core, z], moved(here, 3, step, dims))
                for step in range(1, depth)
            ]
        )
        started += along_z[k]
    first, second, partner = [], [], []
    other = moved(here, 2, 1, dims)
    for k in range(count):
        locals_[k].wait()
        for copy in along_z[k]:
            copy.wait_recv()
        axis = k % 2
        block = outs[k].at[y, x, core]
        first.append(
            [send(k, block, block, moved(here, axis, s, dims)) for s in range(1, dims[axis])]
        )
        partner.append([send(k, block, block, other)])
        started += first[k] + partner[k]
    for k in range(count):
        axis = k % 2
        cross = 1 - axis
        for copy in first[k]:
            copy.wait_recv()
        copies = []
        for lag in range(dims[axis]):
            at = moved(here, axis, lag, dims)
            block = outs[k].at[at[0], at[1], core]
            copies += [
                send(k, block, block, moved(here, cross, s, dims)) for s in range(1, dims[cross])
            ]
            if lag:
                partner[k].append(send(k, block, block, other))
                started.append(partner[k][-1])
        second.append(copies)
        started += copies
    for k in range(count):
        axis = k % 2
        cross = 1 - axis
        copies = iter(second[k])
        for lag in range(dims[axis]):
            for s in range(1, dims[cross]):
                next(copies).wait_recv()
                at = moved(here, axis, lag, dims)
                at[cross] = lax.rem(here[cross] + dims[cross] - s, dims[cross])
                block = outs[k].at[at[0], at[1], core]
                partner[k].append(send(k, block, block, other))
                started.append(partner[k][-1])
    for k in range(count):
        for copy in partner[k]:
            copy.wait_recv()
    for copy in started:
        copy.wait_send()


def reduce_kernel(dims, count, *refs):
    ins, table = refs[:count], refs[count]
    outs, table_out = refs[count + 1 : 2 * count + 1], refs[2 * count + 1]
    rest = refs[2 * count + 2 :]
    bufs = [rest[7 * k : 7 * k + 7] for k in range(count)]
    table_in = rest[7 * count : 7 * count + 4]
    table_sum = rest[7 * count + 4 : 7 * count + 7]
    send_sem, recv_sem = rest[7 * count + 7 :]
    height, width, _, depth = dims
    here = whereabouts(dims)
    y, x, core, z = here
    greet(dims, here)
    used = [0] * (count + 1)
    started = []

    def send(stream, src, dst, there):
        slot = used[stream]
        used[stream] += 1
        copy = pltpu.make_async_remote_copy(
            src_ref=src,
            dst_ref=dst,
            send_sem=send_sem.at[stream, slot],
            recv_sem=recv_sem.at[stream, slot],
            device_id=device_at(dims, *there),
            device_id_type=MESH,
        )
        copy.start()
        started.append(copy)
        return copy

    def add(dst, parts):
        def body(i, carry):
            total = parts[0][i].astype(jnp.float32)
            for part in parts[1:]:
                total = total + part[i].astype(jnp.float32)
            dst[i] = total.astype(dst.dtype)
            return carry

        lax.fori_loop(0, depth, body, 0)

    def table_step(stage, axis, src):
        table_in[stage][here[axis]] = src[...]
        return [
            send(count, src, table_in[stage].at[here[axis]], moved(here, axis, s, dims))
            for s in range(1, dims[axis])
        ]

    def table_add(stage, axis, copies, dst):
        for copy in copies:
            copy.wait_recv()
        total = table_in[stage][0]
        for j in range(1, dims[axis]):
            total = total + table_in[stage][j]
        dst[...] = total

    other = moved(here, 2, 1, dims)
    table_copies = table_step(0, 2, table)
    core_copies = []
    for k in range(count):
        axis = k % 2
        cross = 1 - axis
        group = {}
        for lag in list(range(1, dims[axis])) + [0]:
            for j in range(dims[cross]):
                at = moved(here, axis, lag, dims)
                at[cross] = j
                group[lag, j] = send(
                    k, ins[k].at[at[0], at[1], other[2]], bufs[k][0].at[at[0], at[1]], other
                )
        core_copies.append(group)
    table_add(0, 2, table_copies, table_sum[0])
    table_copies = table_step(1, 0, table_sum[0])
    first = []
    for k in range(count):
        axis = k % 2
        cross = 1 - axis
        from_core, sum_core, from_first = bufs[k][0], bufs[k][1], bufs[k][2]
        group = []
        for lag in list(range(1, dims[axis])) + [0]:
            for j in range(dims[cross]):
                at = moved(here, axis, lag, dims)
                at[cross] = j
                core_copies[k][lag, j].wait_recv()
                block = sum_core.at[at[0], at[1]]
                add(block, [ins[k].at[at[0], at[1], core], from_core.at[at[0], at[1]]])
                if lag:
                    group.append(
                        send(k, block, from_first.at[lag - 1, j], moved(here, axis, lag, dims))
                    )
        first.append(group)
    table_add(1, 0, table_copies, table_sum[1])
    table_copies = table_step(2, 1, table_sum[1])
    second = []
    for k in range(count):
        axis = k % 2
        cross = 1 - axis
        sum_core, from_first, sum_first, from_second = bufs[k][1:5]
        for copy in first[k]:
            copy.wait_recv()
        group = []
        for lag in list(range(1, dims[cross])) + [0]:
            at = moved(here, cross, lag, dims)
            j = at[cross]
            block = sum_first.at[j]
            add(
                block,
                [sum_core.at[at[0], at[1]]]
                + [from_first.at[s - 1, j] for s in range(1, dims[axis])],
            )
            if lag:
                group.append(send(k, block, from_second.at[lag - 1], at))
        second.append(group)
    table_add(2, 1, table_copies, table_sum[2])
    table_copies = table_step(3, 3, table_sum[2])
    third = []
    for k in range(count):
        axis = k % 2
        cross = 1 - axis
        sum_first, from_second, sum_second, from_third = bufs[k][3:7]
        for copy in second[k]:
            copy.wait_recv()
        add(
            sum_second,
            [sum_first.at[here[cross]]] + [from_second.at[s - 1] for s in range(1, dims[cross])],
        )
        group = []
        for step in range(1, depth):
            at = moved(here, 3, step, dims)
            group.append(send(k, sum_second.at[at[3]], from_third.at[step - 1], at))
        third.append(group)
    table_add(3, 3, table_copies, table_out)
    for k in range(count):
        sum_second, from_third = bufs[k][5:7]
        for copy in third[k]:
            copy.wait_recv()
        total = sum_second[z].astype(jnp.float32)
        for step in range(1, depth):
            total = total + from_third[step - 1].astype(jnp.float32)
        outs[k][...] = total
    for copy in started:
        copy.wait_send()


def sizes_here():
    rows, depth = lax.axis_size("rows"), lax.axis_size("cols")
    height, width = grid_of(rows)
    return height, width, CORES, depth


def blocked(rows, columns):
    if rows % 16 == 0:
        return rows, columns
    return rows * columns // 128, 128


def gather_all(shards):
    dims = sizes_here()
    height, width, cores, depth = dims
    count = len(shards)
    blocks = [blocked(*shard.shape) for shard in shards]
    slots = (depth - 1) + max(height, width) * 2 * height * width
    outs = pl.pallas_call(
        functools.partial(gather_kernel, dims, count),
        name="gather_all",
        out_shape=[
            jax.ShapeDtypeStruct(dims + block, shard.dtype)
            for block, shard in zip(blocks, shards)
        ],
        in_specs=[pl.BlockSpec(memory_space=pltpu.VMEM)] * count,
        out_specs=[pl.BlockSpec(memory_space=pl.ANY)] * count,
        scratch_shapes=[
            pltpu.SemaphoreType.DMA((count,)),
            pltpu.SemaphoreType.DMA((count, slots)),
            pltpu.SemaphoreType.DMA((count, slots)),
        ],
        compiler_params=pltpu.CompilerParams(collective_id=0, has_side_effects=True),
    )(*[shard.reshape(block) for block, shard in zip(blocks, shards)])
    total = height * width * cores * depth
    return [
        out.reshape(total * shard.shape[0], shard.shape[1]) for out, shard in zip(outs, shards)
    ]


def reduce_all(wholes, table):
    dims = sizes_here()
    height, width, cores, depth = dims
    total = height * width * cores * depth
    count = len(wholes)
    shares = [(whole.shape[0] // total, whole.shape[1]) for whole in wholes]
    blocks = [blocked(*share) for share in shares]
    scratch = []
    for k, (block, whole) in enumerate(zip(blocks, wholes)):
        along, cross = dims[k % 2], dims[1 - k % 2]
        for lead in (
            (height, width, depth),
            (height, width, depth),
            (max(along - 1, 1), cross, depth),
            (cross, depth),
            (max(cross - 1, 1), depth),
            (depth,),
            (max(depth - 1, 1),),
        ):
            scratch.append(pltpu.VMEM(lead + block, whole.dtype))
    for size in (cores, height, width, depth):
        scratch.append(pltpu.VMEM((size,) + table.shape, table.dtype))
    scratch += [pltpu.VMEM(table.shape, table.dtype)] * 3
    slots = 2 * height * width + height + width + depth
    scratch += [pltpu.SemaphoreType.DMA((count + 1, slots))] * 2
    outs = pl.pallas_call(
        functools.partial(reduce_kernel, dims, count),
        name="reduce_all",
        out_shape=[jax.ShapeDtypeStruct(block, jnp.float32) for block in blocks]
        + [jax.ShapeDtypeStruct(table.shape, table.dtype)],
        in_specs=[pl.BlockSpec(memory_space=pltpu.VMEM)] * (count + 1),
        out_specs=[pl.BlockSpec(memory_space=pltpu.VMEM)] * (count + 1),
        scratch_shapes=scratch,
        compiler_params=pltpu.CompilerParams(collective_id=1, has_side_effects=True),
    )(*[whole.reshape(dims + block) for block, whole in zip(blocks, wholes)], table)
    return [out.reshape(share) for out, share in zip(outs, shares)], outs[-1]


def padded(values, multiple):
    size = values.shape[-1]
    extra = -size % multiple
    return jnp.pad(values, [(0, 0)] * (values.ndim - 1) + [(0, extra)])


def plain_block(
    images,
    cotangent,
    rel_index,
    rel_table,
    qkv_weight,
    proj_weight,
    up_weight,
    down_weight,
    norm1_gain,
    norm1_bias,
    query_bias,
    value_bias,
    proj_bias,
    norm2_gain,
    norm2_bias,
    up_bias,
    down_bias,
):
    shards = (
        norm1_gain,
        norm1_bias,
        query_bias,
        value_bias,
        proj_bias,
        norm2_gain,
        norm2_bias,
        up_bias,
        down_bias,
    )
    vector_shard = padded(jnp.concatenate(shards)[None], 2048).reshape(-1, 128)
    qkv_full, down_full, up_full, proj_full, vector_full = gather_all(
        [qkv_weight, down_weight, up_weight, proj_weight, vector_shard]
    )
    device_count = lax.axis_size("rows") * lax.axis_size("cols")
    vector_full = vector_full.reshape(device_count, -1)
    vectors, offset = [], 0
    for shard in shards:
        size = shard.shape[0]
        vectors.append(vector_full[:, offset : offset + size].reshape(device_count * size))
        offset += size
    (
        gain_one_full,
        bias_one_full,
        query_add,
        value_add,
        proj_add,
        gain_two_full,
        bias_two_full,
        up_add,
        down_add,
    ) = vectors
    tokens_tile, grad_tile = roll_in(images, cotangent)
    image_count, tile_side, features = (
        tokens_tile.shape[0],
        tokens_tile.shape[1],
        tokens_tile.shape[3],
    )
    window = tile_side * tile_side
    row_total = image_count * window
    tokens = tokens_tile.reshape(row_total, features)
    grad_rows = grad_tile.reshape(row_total, features)
    local_pos = jnp.arange(tile_side, dtype=jnp.int32)
    band_rows = band_of(
        lax.axis_index("rows") * tile_side + local_pos, lax.axis_size("rows") * tile_side
    )
    band_cols = band_of(
        lax.axis_index("cols") * tile_side + local_pos, lax.axis_size("cols") * tile_side
    )
    region = (3 * band_rows[:, None] + band_cols[None, :]).reshape(window)
    allowed = (region[:, None] == region[None, :])[None, None]
    head_count = rel_table.shape[1]
    table_size = rel_table.shape[0]
    head_width = features // head_count
    score_scale = head_width ** (-0.5)
    onehot = (
        rel_index.reshape(window * window)[:, None]
        == jnp.arange(table_size, dtype=jnp.int32)[None, :]
    ).astype(jnp.float32)
    bias_flat = jnp.dot(
        onehot, rel_table, precision=lax.Precision.HIGHEST, preferred_element_type=jnp.float32
    )
    bias_heads = bias_flat.T.reshape(head_count, window, window)

    def split_heads(values):
        return values.reshape(image_count, window, head_count, head_width)

    def scores_of(query_b, key_b):
        raw_scores = jnp.einsum(
            "wqhd,wkhd->whqk",
            split_heads(query_b),
            split_heads(key_b),
            preferred_element_type=jnp.float32,
        )
        return jnp.where(allowed, raw_scores + bias_heads[None], big_negative)

    gain_one = gain_one_full.astype(jnp.float32)
    gain_two = gain_two_full.astype(jnp.float32)
    out_one, normed_one, inv_one = layer_norm(tokens, gain_one, bias_one_full.astype(jnp.float32))
    h_one = out_one.astype(jnp.bfloat16)
    projected = dot_plain(h_one, qkv_full)
    query_b = ((projected[:, :features] + query_add.astype(jnp.float32)) * score_scale).astype(
        jnp.bfloat16
    )
    key_b = projected[:, features : 2 * features].astype(jnp.bfloat16)
    value_b = (projected[:, 2 * features :] + value_add.astype(jnp.float32)).astype(jnp.bfloat16)
    scores = scores_of(query_b, key_b)
    row_top = jnp.max(scores, axis=-1, keepdims=True)
    log_total = row_top + jnp.log(jnp.sum(jnp.exp(scores - row_top), axis=-1, keepdims=True))
    attend_b = jnp.exp(scores - log_total).astype(jnp.bfloat16)
    attn_b = (
        jnp.einsum(
            "whqk,wkhd->wqhd", attend_b, split_heads(value_b), preferred_element_type=jnp.float32
        )
        .reshape(row_total, features)
        .astype(jnp.bfloat16)
    )
    residual = tokens + dot_plain(attn_b, proj_full) + proj_add.astype(jnp.float32)
    out_two, normed_two, inv_two = layer_norm(residual, gain_two, bias_two_full.astype(jnp.float32))
    h_two = out_two.astype(jnp.bfloat16)
    hidden_pre = dot_plain(h_two, up_full) + up_add.astype(jnp.float32)
    gauss_cdf = 0.5 * (1.0 + lax.erf(hidden_pre * root_half))
    act_b = (hidden_pre * gauss_cdf).astype(jnp.bfloat16)
    result = residual + dot_plain(act_b, down_full) + down_add.astype(jnp.float32)
    grad_b = grad_rows.astype(jnp.bfloat16)
    grad_down = dot_lead(act_b, grad_b)
    grad_down_add = jnp.sum(grad_rows, axis=0)
    grad_act = dot_tail(grad_b, down_full)
    density = jnp.exp(-0.5 * hidden_pre * hidden_pre) * tau_factor
    grad_pre = grad_act * (gauss_cdf + hidden_pre * density)
    grad_pre_b = grad_pre.astype(jnp.bfloat16)
    grad_up = dot_lead(h_two, grad_pre_b)
    grad_up_add = jnp.sum(grad_pre, axis=0)
    grad_h_two = dot_tail(grad_pre_b, up_full)
    grad_resid, grad_gain_two, grad_bias_two = norm_back(
        grad_h_two, normed_two, inv_two, gain_two
    )
    grad_resid = grad_resid + grad_rows
    grad_resid_b = grad_resid.astype(jnp.bfloat16)
    grad_proj = dot_lead(attn_b, grad_resid_b)
    grad_proj_add = jnp.sum(grad_resid, axis=0)
    grad_attn_b = dot_tail(grad_resid_b, proj_full).astype(jnp.bfloat16)
    grad_heads = split_heads(grad_attn_b)
    grad_attend = jnp.einsum(
        "wqhd,wkhd->whqk", grad_heads, split_heads(value_b), preferred_element_type=jnp.float32
    )
    attend = jnp.exp(scores_of(query_b, key_b) - log_total)
    grad_value = jnp.einsum(
        "whqk,wqhd->wkhd",
        attend.astype(jnp.bfloat16),
        grad_heads,
        preferred_element_type=jnp.float32,
    ).reshape(row_total, features)
    row_inner = jnp.sum(attend * grad_attend, axis=-1, keepdims=True)
    grad_scores = attend * (grad_attend - row_inner)
    grad_bias_heads = jnp.sum(grad_scores, axis=0).reshape(head_count, window * window)
    table_local = lax.dot_general(
        onehot,
        grad_bias_heads,
        (((0,), (1,)), ((), ())),
        precision=lax.Precision.HIGHEST,
        preferred_element_type=jnp.float32,
    )
    grad_scores_b = grad_scores.astype(jnp.bfloat16)
    grad_query = (
        jnp.einsum(
            "whqk,wkhd->wqhd", grad_scores_b, split_heads(key_b), preferred_element_type=jnp.float32
        )
        * score_scale
    ).reshape(row_total, features)
    grad_key = jnp.einsum(
        "whqk,wqhd->wkhd", grad_scores_b, split_heads(query_b), preferred_element_type=jnp.float32
    ).reshape(row_total, features)
    grad_query_add = jnp.sum(grad_query, axis=0)
    grad_value_add = jnp.sum(grad_value, axis=0)
    grad_mixed_b = jnp.concatenate([grad_query, grad_key, grad_value], axis=1).astype(jnp.bfloat16)
    grad_qkv = dot_lead(h_one, grad_mixed_b)
    grad_h_one = dot_tail(grad_mixed_b, qkv_full)
    grad_in, grad_gain_one, grad_bias_one = norm_back(
        grad_h_one, normed_one, inv_one, gain_one
    )
    grad_tokens = grad_resid + grad_in
    vector_grads = (
        grad_gain_one,
        grad_bias_one,
        grad_query_add,
        grad_value_add,
        grad_proj_add,
        grad_gain_two,
        grad_bias_two,
        grad_up_add,
        grad_down_add,
    )
    vector_rows = padded(
        jnp.concatenate([grad.reshape(device_count, -1) for grad in vector_grads], axis=1), 2048
    ).reshape(-1, 128)
    table_rows = padded(table_local.reshape(1, -1), 1024).reshape(-1, 128)
    (down_sum, up_sum, qkv_sum, proj_sum, vector_sum), table_sum = reduce_all(
        [
            grad_down.astype(jnp.bfloat16),
            grad_up.astype(jnp.bfloat16),
            grad_qkv.astype(jnp.bfloat16),
            grad_proj.astype(jnp.bfloat16),
            vector_rows,
        ],
        table_rows,
    )
    grad_table = table_sum.reshape(-1)[: table_local.size].reshape(table_local.shape)
    vector_sum = vector_sum.reshape(-1)
    vector_sums, offset = [], 0
    for shard in shards:
        size = shard.shape[0]
        vector_sums.append(vector_sum[offset : offset + size])
        offset += size
    shard_grads = (qkv_sum, proj_sum, up_sum, down_sum, *vector_sums)
    block_out, grad_images = roll_out(
        result.reshape(image_count, tile_side, tile_side, features),
        grad_tokens.reshape(image_count, tile_side, tile_side, features),
    )
    return (
        block_out,
        grad_images,
        shard_grads[0],
        shard_grads[1],
        shard_grads[2],
        shard_grads[3],
        shard_grads[4],
        shard_grads[5],
        shard_grads[6],
        shard_grads[7],
        shard_grads[8],
        shard_grads[9],
        shard_grads[10],
        shard_grads[11],
        shard_grads[12],
        grad_table,
    )


LANES = 128
HALF = 64


def dot_nt(former, latter):
    return lax.dot_general(
        former, latter, (((1,), (1,)), ((), ())), preferred_element_type=jnp.float32
    )


def dot_tn(former, latter):
    return lax.dot_general(
        former, latter, (((0,), (0,)), ((), ())), preferred_element_type=jnp.float32
    )


def iota(shape, dim):
    return lax.broadcasted_iota(jnp.int32, shape, dim)


def aligned(value, multiple):
    return pl.multiple_of(value, multiple)


class Plan:
    def __init__(self, dims, images, rel_table, weights, vectors):
        self.dims = dims
        self.depth = dims[3]
        self.side, _, self.images, self.features = images.shape
        self.keep = self.side - SHIFT
        self.pitch = self.side + 1
        self.span = self.side * self.pitch
        self.rows = self.images * self.span
        self.heads, self.table_size = rel_table.shape
        self.head_width = self.features // self.heads
        self.group_heads = LANES // self.head_width
        self.groups = self.features // LANES
        self.lanes = self.group_heads * self.span
        self.table_rows = -(-self.table_size // 16) * 16
        self.shard_rows = [w.shape[0] for w in weights]
        self.widths = [w.shape[1] for w in weights]
        self.devices = dims[0] * dims[1] * dims[2] * dims[3]
        self.hidden = weights[2].shape[1]
        self.stack = 4
        self.cuts = (3, 1, 4, 2)
        third, part = self.widths[0] // 3, self.hidden // 2
        self.reductions = [(3, 0, self.features), (2, 0, part), (2, part, part)]
        self.reductions += [(1, 0, self.features)]
        self.reductions += [(0, n * third, third) for n in range(3)]
        self.vector_sizes = [v.shape[0] for v in vectors]


def fits_fused(dims, images, weights, vectors):
    return (
        dims[0] == 2
        and dims[1] == 2
        and dims[2] == 2
        and dims[3] > 1
        and all(w.shape[0] % 16 == 0 for w in weights)
        and images.shape[1] == WIN
        and images.shape[2] == WIN
    )


def block_kernel(plan, *refs):
    p = plan
    take = iter(refs)

    def pull(count):
        return [next(take) for _ in range(count)]

    held = pull(13)
    shards = pull(4)
    results = pull(6)
    (small_out,) = pull(1)
    (
        vec_shard,
        vec_full,
        vec,
        up_vec,
        xs,
        gs,
        normed,
        inv,
        h_b,
        qkv,
        probs,
        attn,
        attn_b,
        x1,
        normed2,
        inv2,
        h2_b,
        gy_b,
        act_b,
        dpre_b,
        ys,
        dh2,
        dx1,
        dx1_b,
        dattn,
        dqkv,
        dqkv_b,
        dh1,
        work,
        square,
        flipped,
        flipped_pad,
        index_t,
        index_q,
        tab,
        tab_b,
        onehot,
        bias_cube,
        bias,
        dbias,
        dcube,
        dtab,
        sums,
        sums_up,
        small,
        small_in,
        small_mid,
        small_z,
    ) = pull(48)
    full = pull(4)
    grads = pull(4)
    core_in = pull(7)
    x_in, y_in, a_in, b_in, z_in = pull(7), pull(7), pull(7), pull(7), pull(7)
    halo_in_src, halo_in_dst, halo_y_src, halo_y_dst, halo_g_src, halo_g_dst = pull(6)
    g_send, g_recv, r_send, r_recv, h_send, h_recv, s_send, s_recv = pull(8)
    local_sem = next(take)
    staged = pull(13)
    images, cotangent, rel_index, rel_table = staged[:4]
    vector_ins = staged[4:]
    result_sem = next(take)
    kept = pull(6)
    out_y, out_g = kept[:2]
    out_w = kept[2:]
    writes = []

    def write(n):
        copy = pltpu.make_async_copy(kept[n], results[n], result_sem.at[n])
        copy.start()
        writes.append(copy)


    dims, depth = p.dims, p.depth
    rows_total = lax.axis_size("rows")
    row, z = lax.axis_index("rows"), lax.axis_index("cols")
    here = whereabouts(dims)
    y, x, core = here[0], here[1], here[2]
    me = row * depth + z
    partner_at = (y * dims[1] + x) * CORES + (1 - core)
    x_at = (y * dims[1] + (1 - x)) * CORES + core
    y_at = ((1 - y) * dims[1] + x) * CORES + core
    chip_own = y * dims[1] + x
    chip_x = y * dims[1] + (1 - x)
    chip_y = (1 - y) * dims[1] + x
    chip_d = (1 - y) * dims[1] + (1 - x)
    row_up, row_down = lax.rem(row + rows_total - 1, rows_total), lax.rem(row + 1, rows_total)
    col_up, col_down = lax.rem(z + depth - 1, depth), lax.rem(z + 1, depth)
    started = []

    def remote(src, dst, send_sem, recv_sem, device):
        return pltpu.make_async_remote_copy(
            src_ref=src,
            dst_ref=dst,
            send_sem=send_sem,
            recv_sem=recv_sem,
            device_id=device,
            device_id_type=MESH,
        )

    def launch(*args):
        copy = remote(*args)
        copy.start()
        started.append(copy)
        return copy

    loads = [
        pltpu.make_async_copy(src, dst, local_sem.at[n])
        for n, (src, dst) in enumerate(zip(held, staged))
    ]
    for k in range(4):
        size = p.shard_rows[k]
        mine = full[k].at[pl.ds(aligned(me * size, 16), size)]
        loads.append(pltpu.make_async_copy(shards[k], mine, local_sem.at[13 + k]))
    for copy in loads:
        copy.start()

    barrier = pltpu.get_barrier_semaphore()
    peers = [(lax.rem(row + s, rows_total), z) for s in range(1, rows_total)]
    peers += [(row, lax.rem(z + s, depth)) for s in range(1, depth)]
    peers += [(row_up, col_up), (row_down, col_down)]
    for peer in peers:
        pl.semaphore_signal(barrier, inc=1, device_id=peer, device_id_type=MESH)

    span, pitch, keep, side = p.span, p.pitch, p.keep, p.side
    slots = keep * SHIFT

    def pack(read, dst, slot_of):
        for piece, (row_list, col_at, cols) in enumerate(slot_of):
            parts = []
            for b in range(p.images):
                parts += [read(b, i, col_at, cols) for i in row_list]
                if len(row_list) * cols < slots:
                    blank = slots - len(row_list) * cols
                    parts.append(jnp.zeros((blank, p.features), jnp.float32))
            dst(piece)[...] = jnp.concatenate(parts, axis=0).astype(jnp.bfloat16)

    for copy in loads:
        copy.wait()
    head, rest = list(range(SHIFT)), list(range(SHIFT, side))
    pieces_in = [(head, SHIFT, keep), (rest, 0, SHIFT), (head, 0, SHIFT)]
    for n, source in enumerate((images, cotangent)):
        pack(
            lambda b, i, c, cols, source=source: source[i, pl.ds(c, cols), b, :],
            lambda piece, n=n: halo_in_src.at[piece, n],
            pieces_in,
        )

    vec_shard[...] = jnp.zeros_like(vec_shard)
    for k, ref in enumerate(vector_ins):
        vec_shard[k : k + 1, : p.vector_sizes[k]] = ref[...].astype(jnp.float32)
    vec_b = vec_full.at[pl.ds(aligned(me * 16, 16), 16)]
    vec_b[...] = vec_shard[...].astype(jnp.bfloat16)

    streams = [(vec_full, 16, 0, LANES)]
    for k, cuts in enumerate(p.cuts):
        width = p.widths[k] // cuts
        streams += [(full[k], p.shard_rows[k], t * width, width) for t in range(cuts)]
    pl.semaphore_wait(barrier, len(peers))

    def halo_send(n):
        targets = ((row_up, z), (row, col_up), (row_up, col_up))
        return [
            launch(
                halo_in_src.at[piece, n],
                halo_in_dst.at[piece, n],
                h_send.at[6 + 3 * n + piece],
                h_recv.at[6 + 3 * n + piece],
                device,
            )
            for piece, device in enumerate(targets)
        ]

    halo_x = halo_send(0)

    along_z = {}
    hops = {}

    def g_copy(k, slot, src, device):
        copy = launch(src, src, g_send.at[k, slot], g_recv.at[k, slot], device)
        hops[k, slot] = copy

    def block_of(k, row_at):
        ref, size, left, width = streams[k]
        rows_at = pl.ds(aligned(row_at * depth * size, 16), depth * size)
        return ref.at[rows_at, pl.ds(left, width)]

    def chip_row(chip):
        return chip * CORES + core

    def half_of(k, row_at, which):
        ref, size, left, width = streams[k]
        rows_at = pl.ds(aligned(row_at * depth * size, 16), depth * size)
        if width == LANES:
            return ref.at[rows_at, pl.ds(left, width)]
        middle = width // 2
        return ref.at[rows_at, pl.ds(left + which * middle, middle)]

    def gather_z(k):
        ref, size, left, width = streams[k]
        mine = ref.at[pl.ds(aligned(me * size, 16), size), pl.ds(left, width)]
        for s in range(1, depth):
            g_copy(k, 12 + s, mine, (row, lax.rem(z + s, depth)))

    def gather_one(k):
        for s in range(1, depth):
            hops[k, 12 + s].wait_recv()
        block = block_of(k, row)
        g_copy(k, 0, block, (x_at, z))
        g_copy(k, 1, block, (y_at, z))
        g_copy(k, 4, block, (partner_at, z))
        for later in following.get(k, ()):
            gather_z(later)

    def gather_two(k):
        single = streams[k][3] == LANES
        row_x, row_y = chip_row(chip_x), chip_row(chip_y)
        hops[k, 0].wait_recv()
        g_copy(k, 2, half_of(k, row_x, 0), (y_at, z))
        g_copy(k, 5, block_of(k, row_x), (partner_at, z))
        hops[k, 1].wait_recv()
        if not single:
            g_copy(k, 3, half_of(k, row_y, 1), (x_at, z))
        g_copy(k, 6, block_of(k, row_y), (partner_at, z))

    def gather_three(k):
        single = streams[k][3] == LANES
        row_d = chip_row(chip_d)
        hops[k, 2].wait_recv()
        g_copy(k, 7, half_of(k, row_d, 0), (partner_at, z))
        if not single:
            hops[k, 3].wait_recv()
            g_copy(k, 8, half_of(k, row_d, 1), (partner_at, z))

    def gather_end(k):
        for slot in (4, 5, 6, 7, 8):
            if (k, slot) in hops:
                hops[k, slot].wait_recv()

    VEC, Q0, Q1, Q2, PROJ, U0, U1, U2, U3, DOWN0, DOWN1 = range(11)
    following = {VEC: (PROJ,), Q0: (DOWN0,), Q1: (DOWN1,), Q2: (U0,), PROJ: (U1,)}
    following.update({DOWN0: (U2,), DOWN1: (U3,)})
    for k in (VEC, Q0, Q1, Q2):
        gather_z(k)

    window = side * side
    square[...] = jnp.full(square.shape, -1.0, jnp.float32)
    raw_index = rel_index[...].astype(jnp.float32)
    for i in range(side):
        square[i * pitch : i * pitch + side, :window] = raw_index[i * side : (i + 1) * side]
    flipped[...] = square[...].T
    index_t[...] = jnp.full(index_t.shape, -1.0, jnp.float32)
    for i in range(side):
        index_t[i * pitch : i * pitch + side, :] = flipped[i * side : (i + 1) * side, :]
    for t in range(p.stack):
        index_q[:, t * HALF : (t + 1) * HALF] = index_t[
            pl.ds(t, span // p.stack, stride=p.stack), :HALF
        ]
    tab[...] = jnp.zeros_like(tab)
    tab[: p.heads, : p.table_size] = rel_table[...]
    tab_high = tab[...].astype(jnp.bfloat16).astype(jnp.float32)
    tab_b[...] = jnp.concatenate([tab_high, tab[...] - tab_high], axis=0).astype(jnp.bfloat16)

    def bias_step(q, carry):
        wanted = index_q[pl.ds(q, 1), :]
        places = iota((p.table_rows, p.stack * HALF), 0).astype(jnp.float32)
        hot = (places == wanted).astype(jnp.float32).astype(jnp.bfloat16)
        onehot[q] = hot
        entry = dot_plain(tab_b[...], hot)
        entry = entry[: p.heads] + entry[p.heads :]
        for t in range(p.stack):
            bias_cube[:, q * p.stack + t, :HALF] = entry[:, t * HALF : (t + 1) * HALF]
        return carry

    def bias_part(first, last):
        lax.fori_loop(first, last, bias_step, 0)

    def band(local, tile, axis):
        length = lax.axis_size(axis) * side
        at = tile * side + local
        return jnp.where(at >= length - WIN, 1, 0) + jnp.where(at >= length - SHIFT, 1, 0)

    def region_of(token):
        return 3 * band(token // pitch, row, "rows") + band(lax.rem(token, pitch), z, "cols")

    key_token = iota((span, p.lanes), 0)
    query_token = lax.rem(iota((span, p.lanes), 1), span)
    allowed = (region_of(key_token) == region_of(query_token)) & (
        lax.rem(key_token, pitch) < side
    )
    def bias_end():
        for g in range(p.groups):
            parts = [bias_cube[g * p.group_heads + h][:, :span] for h in range(p.group_heads)]
            bias[g] = jnp.where(allowed, jnp.concatenate(parts, axis=1), big_negative)

    bias_part(0, span // p.stack)
    bias_end()
    gather_one(VEC)
    gather_one(Q0)
    gather_one(Q1)

    def arrive(copies, n, source, dst):
        for copy in copies:
            copy.wait_recv()

        by_row, by_col, by_both = [
            halo_in_dst[piece, n].astype(jnp.float32) for piece in range(3)
        ]
        blank = jnp.zeros((pitch - side, p.features), jnp.float32)
        for b in range(p.images):
            for i in range(side):
                if i < keep:
                    at = b * slots + SHIFT * i
                    left, right = source[i + SHIFT, SHIFT:side, b, :], by_col[at : at + SHIFT]
                else:
                    at, near = b * slots + keep * (i - keep), b * slots + SHIFT * (i - keep)
                    left, right = by_row[at : at + keep], by_both[near : near + SHIFT]
                at = b * span + i * pitch
                dst[at : at + pitch, :] = jnp.concatenate([left, right, blank], axis=0)

    def spans(body, count=None):
        lax.fori_loop(0, p.images if count is None else count, body, 0)

    def span_at(w):
        return pl.ds(aligned(w * span, 8), span)


    def center(ref, dst, inv_ref):
        def body(w, carry):
            value = ref[span_at(w), :]
            mean_val = jnp.mean(value, axis=-1, keepdims=True)
            centred = value - mean_val
            inv_std = lax.rsqrt(
                jnp.mean(centred * centred, axis=-1, keepdims=True) + norm_eps
            )
            dst[span_at(w), :] = centred * inv_std
            inv_ref[span_at(w), :] = jnp.broadcast_to(inv_std, (span, LANES))
            return carry

        spans(body)

    gather_one(Q2)
    gather_two(VEC)
    gather_two(Q0)
    arrive(halo_x, 0, images, xs)
    center(xs, normed, inv)
    gather_one(PROJ)
    gather_two(Q1)
    gather_three(VEC)
    gather_three(Q0)
    gather_one(DOWN0)
    gather_two(Q2)
    gather_two(PROJ)
    gather_three(Q1)
    gather_three(Q2)
    gather_one(DOWN1)
    halo_g = []
    gather_two(DOWN0)
    gather_end(VEC)

    size = p.vector_sizes[0]
    per = LANES // size
    for t in range(p.features // LANES):
        spread = (lax.rem(iota((LANES, LANES), 1), size) == iota((LANES, LANES), 0)).astype(
            jnp.float32
        ).astype(jnp.bfloat16)
        value = dot_plain(vec_full[t * per * 16 : (t + 1) * per * 16, :], spread)
        mine = iota(value.shape, 0) // 16 == iota(value.shape, 1) // size
        value = jnp.where(mine, value, 0.0)
        total = value[0:16]
        for d in range(1, per):
            total = total + value[d * 16 : (d + 1) * 16]
        vec[:, t * LANES : (t + 1) * LANES] = total
    size_up = p.vector_sizes[7]
    per_up = LANES // size_up
    for t in range(p.hidden // LANES):
        spread = (lax.rem(iota((LANES, LANES), 1), size_up) == iota((LANES, LANES), 0)).astype(
            jnp.float32
        ).astype(jnp.bfloat16)
        value = dot_plain(vec_full[t * per_up * 16 : (t + 1) * per_up * 16, :], spread)
        mine = iota(value.shape, 0) == 16 * (iota(value.shape, 1) // size_up) + 7
        value = jnp.where(mine, value, 0.0)
        up_vec[:, t * LANES : (t + 1) * LANES] = jnp.sum(value, axis=0, keepdims=True)

    def vector(k):
        return vec[k : k + 1, :]

    h_b[...] = (normed[...] * vector(0) + vector(1)).astype(jnp.bfloat16)
    for k in (Q0, Q1, Q2):
        gather_end(k)

    scale = p.head_width ** (-0.5)
    features = p.features
    for n in range(3):
        cols = slice(n * features, (n + 1) * features)
        value = dot_plain(h_b[...], full[0][:, cols])
        if n == 0:
            value = (value + vector(2)) * scale
        if n == 2:
            value = value + vector(3)
        qkv[:, cols] = value
    gather_three(PROJ)
    gather_one(U0)
    gather_two(DOWN1)
    gather_three(DOWN0)

    def expand(value):
        lane = iota(value.shape, 1) // p.head_width
        parts = [jnp.where(lane == h, value, 0.0) for h in range(p.group_heads)]
        return jnp.concatenate(parts, axis=0).astype(jnp.bfloat16)

    def fold(value):
        total = None
        for h in range(p.group_heads):
            part = value[h * span : (h + 1) * span]
            part = jnp.where(iota(part.shape, 1) // p.head_width == h, part, 0.0)
            total = part if total is None else total + part
        return total

    def lanes_at(g, third=0):
        return pl.ds(aligned(third * features + g * LANES, LANES), LANES)

    def attend(w):
        def body(g, carry):
            at = span_at(w)
            query = qkv[at, lanes_at(g, 0)]
            key = qkv[at, lanes_at(g, 1)].astype(jnp.bfloat16)
            value = qkv[at, lanes_at(g, 2)].astype(jnp.bfloat16)
            scores = dot_nt(key, expand(query)) + bias[g]
            top = jnp.max(scores, axis=0, keepdims=True)
            weight = jnp.exp(scores - top)
            prob = weight / jnp.sum(weight, axis=0, keepdims=True)
            probs[w * p.groups + g] = prob
            attn[at, lanes_at(g)] = fold(dot_tn(prob.astype(jnp.bfloat16), value))
            return carry

        lax.fori_loop(0, p.groups, body, 0, unroll=True)

    steps = {
        0: [lambda: gather_one(U1), lambda: gather_two(U0), lambda: gather_three(DOWN1)],
        1: [lambda: gather_end(PROJ), lambda: gather_one(U2), lambda: gather_two(U1)],
        2: [lambda: gather_three(U0), lambda: gather_one(U3), lambda: halo_g.extend(halo_send(1)), lambda: gather_two(U2)],
        3: [lambda: gather_three(U1)],
    }
    for w in range(p.images):
        attend(w)
        for step in steps.get(w, []):
            step()
    attn_b[...] = attn[...].astype(jnp.bfloat16)
    x1[...] = xs[...] + dot_plain(attn_b[...], full[1][...]) + vector(4)
    center(x1, normed2, inv2)
    h2_b[...] = (normed2[...] * vector(5) + vector(6)).astype(jnp.bfloat16)
    arrive(halo_g, 1, cotangent, gs)
    gy_b[...] = gs[...].astype(jnp.bfloat16)
    gather_two(U3)
    gather_three(U2)
    for k in (DOWN0, DOWN1):
        gather_end(k)

    ys[...] = x1[...] + vector(8)
    dh2[...] = jnp.zeros_like(dh2)
    tiles = dims[0] * dims[1]
    tile = p.hidden // tiles
    DN, UPA, UPB, PR, QA, QB, QC = range(7)
    red = [
        (which, p.shard_rows[which], left, width) for which, left, width in p.reductions
    ]
    sums[...] = jnp.zeros_like(sums)

    def core_copy(k, chip):
        which, size, left, width = red[k]
        at = (chip * CORES + (1 - core)) * depth * size
        return remote(
            grads[which].at[pl.ds(aligned(at, 16), depth * size), pl.ds(left, width)],
            core_in[k].at[chip],
            r_send.at[k, chip],
            r_recv.at[k, chip],
            (partner_at, z),
        )

    def feed(j, carry):
        at = pl.ds(aligned(j * tile, LANES), tile)
        pre = dot_plain(h2_b[...], full[2][:, at]) + up_vec[:, at]
        cdf = 0.5 * (1.0 + lax.erf(pre * root_half))
        act = (pre * cdf).astype(jnp.bfloat16)
        slope = cdf + pre * (jnp.exp(-0.5 * pre * pre) * tau_factor)
        down_rows = full[3][at, :]
        ys[...] += dot_plain(act, down_rows)
        dpre = dot_nt(gy_b[...], down_rows) * slope
        sums_up[:, at] = jnp.sum(dpre, axis=0, keepdims=True)
        dpre_low = dpre.astype(jnp.bfloat16)
        dh2[...] += dot_nt(dpre_low, full[2][:, at])
        grads[3][at, :] = dot_tn(act, gy_b[...]).astype(jnp.bfloat16)
        grads[2][:, at] = dot_tn(h2_b[...], dpre_low).astype(jnp.bfloat16)
        core_copy(DN, j).start()
        return carry

    def swap(k):
        for chip in range(tiles):
            core_copy(k, chip).start()

    first_part = tiles // 2
    ups = (U0, U1, U2, U3)
    for j in range(first_part):
        gather_end(ups[j])
        lax.fori_loop(j, j + 1, feed, 0)
    swap(UPA)

    r_hops = {}

    def r_copy(k, slot, src, dst, device):
        r_hops[k, slot] = launch(src, dst, r_send.at[k, slot], r_recv.at[k, slot], device)

    def add_into(dst, parts, width_at, width):
        count = dst.shape[0]
        step = 16 if count % 32 else 32

        def body(i, carry):
            at = pl.ds(aligned(i * step, 16), step)
            cols = pl.ds(width_at, width)
            total = dst[at, cols].astype(jnp.float32)
            for part in parts:
                total = total + part[at, :].astype(jnp.float32)
            dst[at, cols] = total.astype(jnp.bfloat16)
            return carry

        lax.fori_loop(0, count // step, body, 0)

    def reduce_core(k):
        which, size, left, width = red[k]
        middle = width // 2
        for chip in range(tiles):
            core_copy(k, chip).wait_recv()
        for chip in range(tiles):
            at = (chip * CORES + core) * depth * size
            add_into(
                core_in[k].at[chip],
                [grads[which].at[pl.ds(aligned(at, 16), depth * size), pl.ds(left, width)]],
                0,
                width,
            )
        corner = core_in[k].at[chip_d]
        r_copy(k, 4, corner.at[:, pl.ds(0, middle)], a_in[k], (y_at, z))
        r_copy(k, 5, corner.at[:, pl.ds(middle, middle)], b_in[k], (x_at, z))

    def reduce_cross(k):
        middle = red[k][3] // 2
        to_x, to_y = core_in[k].at[chip_x], core_in[k].at[chip_y]
        r_hops[k, 4].wait_recv()
        add_into(to_x, [a_in[k]], 0, middle)
        r_copy(k, 6, to_x, x_in[k], (x_at, z))
        r_hops[k, 5].wait_recv()
        add_into(to_y, [b_in[k]], middle, middle)
        r_copy(k, 7, to_y, y_in[k], (y_at, z))

    def reduce_chip(k):
        _, size, _, width = red[k]
        own = core_in[k].at[chip_own]
        r_hops[k, 6].wait_recv()
        r_hops[k, 7].wait_recv()
        add_into(own, [x_in[k], y_in[k]], 0, width)
        for s in range(1, depth):
            there = lax.rem(z + s, depth)
            r_copy(
                k,
                7 + s,
                own.at[pl.ds(aligned(there * size, 16), size)],
                z_in[k].at[s - 1],
                (row, there),
            )

    def reduce_end(k):
        which, size, left, width = red[k]
        for s in range(1, depth):
            r_hops[k, 7 + s].wait_recv()
        total = core_in[k][chip_own, pl.ds(aligned(z * size, 16), size), :].astype(jnp.float32)
        for s in range(1, depth):
            total = total + z_in[k][s - 1].astype(jnp.float32)
        out_w[which][:, left : left + width] = total

    def norm_grad(d_ref, n_ref, inv_ref, gain_at, dst, base, keep_sums):
        gain_row, bias_row = keep_sums

        def body(w, carry):
            at = span_at(w)
            d_val, n_val = d_ref[at, :], n_ref[at, :]
            scaled = d_val * vector(gain_at)
            inner = (
                scaled
                - jnp.mean(scaled, axis=-1, keepdims=True)
                - n_val * jnp.mean(scaled * n_val, axis=-1, keepdims=True)
            )
            dst[at, :] = base[at, :] + inv_ref[at, :][:, :1] * inner
            sums[gain_row : gain_row + 1, :] += jnp.sum(d_val * n_val, axis=0, keepdims=True)
            sums[bias_row : bias_row + 1, :] += jnp.sum(d_val, axis=0, keepdims=True)
            return carry

        spans(body)

    def read_span(ref):
        return lambda b, i, c, cols: ref[
            b * span + i * pitch : b * span + (i + 1) * pitch, :
        ][c : c + cols]

    first_rows, last_rows = list(range(keep)), list(range(keep, side))
    pieces_out = [(last_rows, 0, keep), (first_rows, keep, SHIFT), (last_rows, keep, SHIFT)]

    def halo_out(ref, src, dst, base):
        pack(
            read_span(ref),
            lambda piece: src.at[piece],
            pieces_out,
        )
        return [
            launch(
                src.at[piece], dst.at[piece], h_send.at[base + piece], h_recv.at[base + piece],
                device,
            )
            for piece, device in enumerate(((row_down, z), (row, col_down), (row_down, col_down)))
        ]

    def halo_land(copies, ref, dst, out):
        for copy in copies:
            copy.wait_recv()

        by_row, by_col, by_both = [dst[piece].astype(jnp.float32) for piece in range(3)]
        for b in range(p.images):
            for i in range(side):
                if i < SHIFT:
                    near, at = b * slots + SHIFT * i, b * slots + keep * i
                    left, right = by_both[near : near + SHIFT], by_row[at : at + keep]
                else:
                    k = i - SHIFT
                    near, at = b * slots + SHIFT * k, b * span + k * pitch
                    left, right = by_col[near : near + SHIFT], ref[at : at + pitch, :][:keep]
                out[i, :, b, :] = jnp.concatenate([left, right], axis=0)

    gather_three(U3)
    reduce_core(UPA)
    for j in range(first_part, tiles):
        gather_end(ups[j])
        lax.fori_loop(j, j + 1, feed, 0)
    swap(UPB)
    reduce_core(DN)
    reduce_core(UPB)
    norm_grad(dh2, normed2, inv2, 5, dx1, gs, (5, 6))
    dx1_b[...] = dx1[...].astype(jnp.bfloat16)
    dattn[...] = dot_nt(dx1_b[...], full[1][...])

    dbias[...] = jnp.zeros_like(dbias)
    dcube[...] = jnp.zeros_like(dcube)

    def attend_back(w):
        def body(g, carry):
            at = span_at(w)
            query = expand(qkv[at, lanes_at(g, 0)])
            key = qkv[at, lanes_at(g, 1)].astype(jnp.bfloat16)
            value = qkv[at, lanes_at(g, 2)].astype(jnp.bfloat16)
            grad = expand(dattn[at, lanes_at(g)])
            prob = probs[w * p.groups + g]
            dprob = dot_nt(value, grad)
            dscore = prob * (dprob - jnp.sum(prob * dprob, axis=0, keepdims=True))
            dbias[g] += dscore
            dlow = dscore.astype(jnp.bfloat16)
            dqkv[at, lanes_at(g, 2)] = dot_plain(prob.astype(jnp.bfloat16), grad)
            dqkv[at, lanes_at(g, 1)] = dot_plain(dlow, query)
            dqkv[at, lanes_at(g, 0)] = fold(dot_tn(dlow, key)) * scale
            return carry

        lax.fori_loop(0, p.groups, body, 0, unroll=True)

    back_steps = {
        1: [lambda: reduce_cross(UPA), lambda: reduce_cross(DN)],
        2: [lambda: reduce_cross(UPB)],
    }
    for w in range(p.images):
        attend_back(w)
        for step in back_steps.get(w, []):
            step()

    dqkv_b[...] = dqkv[...].astype(jnp.bfloat16)
    for n in range(3):
        cols = slice(n * features, (n + 1) * features)
        grads[0][:, cols] = dot_tn(h_b[...], dqkv_b[:, cols]).astype(jnp.bfloat16)
        swap(QA + n)
    y_copies = halo_out(ys, halo_y_src, halo_y_dst, 0)
    reduce_chip(UPA)
    for k in (QA, QB, QC):
        reduce_core(k)
    grads[1][...] = dot_tn(attn_b[...], dx1_b[...]).astype(jnp.bfloat16)
    swap(PR)
    reduce_chip(DN)
    dh1[...] = dot_nt(dqkv_b[...], full[0][...])
    norm_grad(dh1, normed, inv, 0, work, dx1, (0, 1))
    g_copies = halo_out(work, halo_g_src, halo_g_dst, 3)
    reduce_core(PR)
    for k in (QA, QB, QC):
        reduce_cross(k)
    reduce_chip(UPB)
    sums[2:3, :] = jnp.sum(dqkv[:, :features], axis=0, keepdims=True)
    sums[3:4, :] = jnp.sum(dqkv[:, 2 * features :], axis=0, keepdims=True)
    sums[4:5, :] = jnp.sum(dx1[...], axis=0, keepdims=True)
    sums[7:8, :] = jnp.sum(gs[...], axis=0, keepdims=True)

    for g in range(p.groups):
        for h in range(p.group_heads):
            dcube[g * p.group_heads + h, :, :span] = dbias[g][:, h * span : (h + 1) * span]
    dtab[...] = jnp.zeros_like(dtab)

    def table_step(q, carry):
        parts = [dcube[:, q * p.stack + t, :][:, :HALF] for t in range(p.stack)]
        value = jnp.concatenate(parts, axis=1)
        high = value.astype(jnp.bfloat16).astype(jnp.float32)
        both = jnp.concatenate([high, value - high], axis=0).astype(jnp.bfloat16)
        dtab[...] += dot_nt(both, onehot[q])
        return carry

    lax.fori_loop(0, span // p.stack, table_step, 0)
    reduce_cross(PR)

    small[...] = jnp.zeros_like(small)
    wide = small.shape[1]
    at = 0
    for k in range(8):
        for t in range(features // wide):
            small[at : at + 1, :] = sums[k : k + 1, t * wide : (t + 1) * wide]
            at += 1
    for t in range(p.hidden // wide):
        small[at : at + 1, :] = sums_up[:, t * wide : (t + 1) * wide]
        at += 1
    small[at : at + p.heads, : p.table_rows] = dtab[: p.heads] + dtab[p.heads :]
    share = small.shape[0] // dims[0] // dims[1] // dims[2]
    own_rows = pl.ds(aligned(row * share, 8), share)
    s_copies = []
    for s in range(1, dims[0] * dims[1] * dims[2]):
        there = lax.rem(row + s, rows_total)
        s_copies.append(
            launch(
                small.at[pl.ds(aligned(there * share, 8), share)],
                small_in.at[s - 1],
                s_send.at[0, s],
                s_recv.at[0, s],
                (there, z),
            )
        )
    for k in (QA, QB, QC):
        reduce_chip(k)
    for copy in s_copies:
        copy.wait_recv()
    total = small[own_rows, :]
    for s in range(1, dims[0] * dims[1] * dims[2]):
        total = total + small_in[s - 1]
    small_mid[...] = total
    small_z[z] = total
    s_copies = [
        launch(
            small_mid,
            small_z.at[z],
            s_send.at[1, s],
            s_recv.at[1, s],
            (row, lax.rem(z + s, depth)),
        )
        for s in range(1, depth)
    ]
    reduce_chip(PR)
    reduce_end(UPA)
    reduce_end(DN)
    for copy in s_copies:
        copy.wait_recv()
    total = small_z[0]
    for s in range(1, depth):
        total = total + small_z[s]
    small_out[own_rows, :] = total
    s_copies = [
        launch(
            small_out.at[own_rows],
            small_out.at[own_rows],
            s_send.at[2, s],
            s_recv.at[2, s],
            (lax.rem(row + s, rows_total), z),
        )
        for s in range(1, dims[0] * dims[1] * dims[2])
    ]
    halo_land(y_copies, ys, halo_y_dst, out_y)
    write(0)
    write(5)
    reduce_end(UPB)
    write(4)
    halo_land(g_copies, work, halo_g_dst, out_g)
    write(1)
    reduce_end(PR)
    write(3)
    for k in (QA, QB, QC):
        reduce_end(k)
    write(2)
    for copy in s_copies:
        copy.wait_recv()
    for k in range(7):
        for chip in range(tiles):
            core_copy(k, chip).wait_send()
    for copy in started:
        copy.wait_send()
    for copy in writes:
        copy.wait()


def fused_block(dims, images, cotangent, rel_index, rel_table, weights, vectors):
    images, cotangent = images.transpose(1, 2, 0, 3), cotangent.transpose(1, 2, 0, 3)
    rel_table = rel_table.T
    p = Plan(dims, images, rel_table, weights, vectors)
    f32, bf16 = jnp.float32, jnp.bfloat16
    rows, feats, hidden, span = p.rows, p.features, p.hidden, p.span
    tiles, depth, plane = dims[0] * dims[1], p.depth, dims[0] * dims[1] * dims[2]
    wide = 2 * LANES
    small_rows = (8 * feats + hidden) // wide + p.heads
    small_rows = -(-small_rows // (8 * plane)) * 8 * plane

    def v(*shape, dtype=f32):
        return pltpu.VMEM(shape, dtype)

    scratch = [
        v(16, LANES),
        v(p.devices * 16, LANES, dtype=bf16),
        v(16, feats),
        v(1, hidden),
        v(rows, feats),
        v(rows, feats),
        v(rows, feats),
        v(rows, LANES),
        v(rows, feats, dtype=bf16),
        v(rows, 3 * feats),
        v(p.images * p.groups, span, p.lanes),
        v(rows, feats),
        v(rows, feats, dtype=bf16),
        v(rows, feats),
        v(rows, feats),
        v(rows, LANES),
        v(rows, feats, dtype=bf16),
        v(rows, feats, dtype=bf16),
        v(8, LANES),
        v(8, LANES),
        v(rows, feats),
        v(rows, feats),
        v(rows, feats),
        v(rows, feats, dtype=bf16),
        v(rows, feats),
        v(rows, 3 * feats),
        v(rows, 3 * feats, dtype=bf16),
        v(rows, feats),
        v(rows, feats),
        v(LANES, LANES),
        v(LANES, LANES),
        v(8, LANES),
        v(span, LANES),
        v(span // p.stack, p.stack * HALF),
        v(p.heads, p.table_rows),
        v(2 * p.heads, p.table_rows, dtype=bf16),
        v(span // p.stack, p.table_rows, p.stack * HALF, dtype=bf16),
        v(p.heads, span, LANES),
        v(p.groups, span, p.lanes),
        v(p.groups, span, p.lanes),
        v(p.heads, span, LANES),
        v(2 * p.heads, p.table_rows),
        v(8, feats),
        v(1, hidden),
        v(small_rows, wide),
        v(plane - 1, small_rows // plane, wide),
        v(small_rows // plane, wide),
        v(depth, small_rows // plane, wide),
    ]
    sizes = [(w.shape[0], w.shape[1]) for w in weights]
    scratch += [v(p.devices * m, n, dtype=bf16) for m, n in sizes]
    scratch += [v(p.devices * m, n, dtype=bf16) for m, n in sizes]
    turned = [(sizes[which][0], width) for which, _, width in p.reductions]
    scratch += [v(tiles, depth * m, n, dtype=bf16) for m, n in turned]
    scratch += [v(depth * m, n, dtype=bf16) for m, n in turned] * 2
    scratch += [v(depth * m, n // 2, dtype=bf16) for m, n in turned] * 2
    scratch += [v(depth - 1, m, n, dtype=bf16) for m, n in turned]
    halo_rows = p.images * SHIFT * p.keep
    scratch += [v(3, 2, halo_rows, feats, dtype=bf16)] * 2
    scratch += [v(3, halo_rows, feats, dtype=bf16)] * 4
    dma = pltpu.SemaphoreType.DMA
    scratch += [dma((11, 12 + depth))] * 2 + [dma((7, 7 + depth))] * 2
    scratch += [dma((12,))] * 2 + [dma((3, plane + depth))] * 2 + [dma((17,))]
    scratch += [v(*images.shape)] * 2 + [v(*rel_index.shape, dtype=rel_index.dtype)]
    scratch += [v(*rel_table.shape)]
    scratch += [v(1, vector.shape[0], dtype=bf16) for vector in vectors]
    scratch += [dma((6,)), v(*images.shape), v(*images.shape)]
    scratch += [v(*w.shape) for w in weights]
    out_shape = [
        jax.ShapeDtypeStruct(images.shape, f32),
        jax.ShapeDtypeStruct(images.shape, f32),
    ]
    out_shape += [jax.ShapeDtypeStruct(w.shape, f32) for w in weights]
    out_shape += [jax.ShapeDtypeStruct((small_rows, wide), f32)]
    spec = pl.BlockSpec(memory_space=pltpu.VMEM)
    outs = pl.pallas_call(
        functools.partial(block_kernel, p),
        name="block",
        out_shape=out_shape,
        in_specs=[pl.BlockSpec(memory_space=pltpu.HBM)] * 17,
        out_specs=[pl.BlockSpec(memory_space=pltpu.HBM)] * 6 + [spec],
        scratch_shapes=scratch,
        compiler_params=pltpu.CompilerParams(
            collective_id=2, has_side_effects=True, vmem_limit_bytes=60 * 1024 * 1024
        ),
    )(
        images,
        cotangent,
        rel_index,
        rel_table,
        *[vector.reshape(1, -1) for vector in vectors],
        *weights,
    )
    sizes_small = [vector.shape[0] for vector in vectors]
    held = pl.BlockSpec(memory_space=pl.ANY)
    last_shape = [jax.ShapeDtypeStruct(out.shape, f32) for out in outs[:6]]
    last_shape += [jax.ShapeDtypeStruct((1, size), f32) for size in sizes_small]
    last_shape += [jax.ShapeDtypeStruct((p.heads, p.table_size), f32)]
    last = pl.pallas_call(
        functools.partial(emit_kernel, p, sizes_small),
        name="emit",
        out_shape=last_shape,
        in_specs=[spec] * 7,
        out_specs=[held] * 6 + [spec] * 10,
        scratch_shapes=[dma((6,))],
        compiler_params=pltpu.CompilerParams(vmem_limit_bytes=60 * 1024 * 1024),
    )(*outs)
    tokens = [out.transpose(2, 0, 1, 3) for out in last[:2]]
    vector_outs = [out.reshape(-1) for out in last[6:15]]
    return (*tokens, *last[2:6], *vector_outs, last[15].T)


def emit_kernel(plan, sizes, *refs):
    p = plan
    big, small, big_out = refs[:6], refs[6], refs[7:13]
    vector_outs, table_out, sems = refs[13:22], refs[22], refs[23]
    copies = [pltpu.make_async_copy(big[k], big_out[k], sems.at[k]) for k in range(6)]
    for copy in copies:
        copy.start()
    wide = small.shape[1]
    me = lax.axis_index("rows") * p.depth + lax.axis_index("cols")
    size, size_up = sizes[0], sizes[7]
    per = p.features // wide
    line, turn = me * size // wide, lax.rem(me * size, wide)
    lines = jnp.concatenate([small[pl.ds(k * per + line, 1), :] for k in range(8)], axis=0)
    lines = pltpu.roll(lines, wide - turn, 1)
    for k in range(9):
        if k != 7:
            at = k if k < 7 else 7
            vector_outs[k][...] = lines[at : at + 1, :size]
    line, turn = me * size_up // wide, lax.rem(me * size_up, wide)
    up = small[pl.ds(8 * per + line, 1), :]
    up = pltpu.roll(jnp.broadcast_to(up, (8, wide)), wide - turn, 1)
    vector_outs[7][...] = up[:1, :size_up]
    at = 8 * per + p.hidden // wide
    table_out[...] = small[at : at + p.heads, : p.table_size]
    for copy in copies:
        copy.wait()


def per_device(images, cotangent, rel_index, rel_table, *params):
    dims = sizes_here()
    weights, vectors = params[:4], params[4:]
    if fits_fused(dims, images, weights, vectors):
        return fused_block(dims, images, cotangent, rel_index, rel_table, weights, vectors)
    return plain_block(images, cotangent, rel_index, rel_table, *params)


def solution(mesh):
    in_specs = (
        P(None, "rows", "cols", None),
        P(None, "rows", "cols", None),
        P(),
        P(),
        P(("rows", "cols"), None),
        P(("rows", "cols"), None),
        P(("rows", "cols"), None),
        P(("rows", "cols"), None),
        P(("rows", "cols")),
        P(("rows", "cols")),
        P(("rows", "cols")),
        P(("rows", "cols")),
        P(("rows", "cols")),
        P(("rows", "cols")),
        P(("rows", "cols")),
        P(("rows", "cols")),
        P(("rows", "cols")),
    )
    out_specs = (
        P(None, "rows", "cols", None),
        P(None, "rows", "cols", None),
        P(("rows", "cols"), None),
        P(("rows", "cols"), None),
        P(("rows", "cols"), None),
        P(("rows", "cols"), None),
        P(("rows", "cols")),
        P(("rows", "cols")),
        P(("rows", "cols")),
        P(("rows", "cols")),
        P(("rows", "cols")),
        P(("rows", "cols")),
        P(("rows", "cols")),
        P(("rows", "cols")),
        P(("rows", "cols")),
        P(),
    )
    return jax.shard_map(
        per_device, mesh=mesh, in_specs=in_specs, out_specs=out_specs, check_vma=False
    )
```
